128 devices in a mesh: gx: 16 (over x, y), gy: 8 (over z, core).
Axes of the slice: x: 4, y: 4, z: 4, core: 2. Of those that a mesh axis runs over, the one named last changes fastest.
Arguments:
- volts: float32 [32, 4, 128, 1024], P(None, None, 'gx', 'gy'), may hold values from -6 to 6
- cap: float32 [4, 128, 1024], P(None, 'gx', 'gy'), may hold values from 0.05 to 1
- cond_x: float32 [4, 128, 1024], P(None, 'gx', 'gy'), may hold values from 0.5 to 2
- cond_y: float32 [4, 128, 1024], P(None, 'gx', 'gy'), may hold values from 0.5 to 2
- via: float32 [4, 128, 1024], P(None, 'gx', 'gy'), may hold values from 0.2 to 2
- waveforms: float32 [64, 64], replicated, may hold values from -6 to 6
- placement: int32 [1048576, 1], P(('gx', 'gy')), may hold values from 0 to 127; in each aligned block of 8192 rows (0 to 8191, 8192 to 16383, ...) at most 128 rows name the same one
- cells: int32 [1048576], P(('gx', 'gy')), may hold values from 0 to 1023
- wave_ids: int32 [1048576], P(('gx', 'gy')), may hold values from 0 to 63
- amps: float32 [1048576], P(('gx', 'gy')), may hold values from 0.5 to 4
Outputs:
- volts_out: float32 [32, 4, 128, 1024], P(None, None, 'gx', 'gy')
- residual: float32 [32, 4, 128, 1024], P(None, None, 'gx', 'gy')
The draws below stay inside these ranges and needn't reach their ends.
Inputs may be any that keep to these rules, and one draw needn't show every extreme that they name: `placement`: in each device's block of 8192 rows no tile is named more than 128 times, a bound that some block reaches.
All inputs are finite; a program needn't handle non-finite values.
Results may differ from the reference program's by a relative error of at most 0.0029.
Values may be sent and summed in bfloat16 or wider, within the bound.
No kernel may reach another device: no remote copies, remote signals or barrier semaphores. Data moves between devices by JAX's collectives and lax.ppermute only.
A program may use at most 64 MiB of HBM per device.

```python
import math
import jax
import jax.numpy as jnp
import numpy as np
from jax import lax

SCEN = 32
LAYERS = 4
WAVES = 64
CX = 8
CY = 128
INST_DEV = 8192
STEPS = 2
ITERS = 3
CAP = 128
INSTANCES = 1048576
NX = 128
NY = 1024
N_GY = 8
DEVICES = 128


def touch_ends(drawn, key, least, largest):
    place = [jax.random.randint(jax.random.fold_in(key, axis), (), 0, length) for axis, length in enumerate(drawn.shape)]
    widest = drawn.shape.index(max(drawn.shape))
    beside = place[:widest] + [(place[widest] + 1) % drawn.shape[widest]] + place[widest + 1:]
    return drawn.at[tuple(place)].set(least).at[tuple(beside)].set(largest)


def steps_of(rng, dims, shards, smallest, high):
    def one(axis_at, parts):
        draws = jax.random.uniform(jax.random.fold_in(jax.random.fold_in(rng, 6), axis_at), (parts,), jnp.float32, smallest / len(shards), high / len(shards))
        return jnp.repeat(jnp.exp(draws), dims[axis_at] // parts).reshape((-1,) + (1,) * (len(dims) - axis_at - 1))

    factor_of = one(*shards[0])
    for cut in shards[1:]:
        factor_of = factor_of * one(*cut)
    return factor_of


def assign_block(rng, own, number, rows, number_of, top, limit, slope):
    order = jax.random.permutation(rng, number_of)
    heavy_load, usual = shares(number_of, rows * top, limit, slope, True), shares(number_of, rows * top, limit, slope, False)
    places = jnp.arange(number_of)

    def named(tallies, rotation):
        used = int((tallies > 0).sum())
        fixed = max(1, used // 4)
        passed = fixed + (places - fixed + rotation * (used - fixed)) % max(1, number_of - fixed)
        return jnp.zeros((number_of,), jnp.int32).at[order[jnp.where(places < fixed, places, passed)]].set(jnp.asarray(tallies, jnp.int32))

    tallies = jnp.where(number % 4 == 0, named(heavy_load, number // 4), named(usual, number - number // 4 - 1))
    mixed = jax.random.permutation(jax.random.fold_in(own, 3), number_of)
    donor, taker = mixed[0:number_of // 2 * 2:2], mixed[1:number_of // 2 * 2:2]
    slack = jnp.minimum(tallies[donor] - 1, limit - tallies[taker]) // 2
    slack = jnp.where((donor == order[0]) | (taker == order[0]) | (tallies[taker] == 0), 0, jnp.maximum(slack, 0))
    passed = jax.random.randint(jax.random.fold_in(own, 4), (number_of // 2,), 0, 1 << 20) % (slack + 1)
    tallies = tallies.at[donor].add(-passed).at[taker].add(passed)
    labels = jnp.searchsorted(jnp.cumsum(tallies), jnp.arange(rows * top), side="right").astype(jnp.int32)
    grid = labels.reshape(top, rows).T
    grid = grid[jax.random.permutation(jax.random.fold_in(own, 1), rows)]
    rotation = jax.random.randint(jax.random.fold_in(own, 2), (rows, 1), 0, top)
    return jnp.take_along_axis(grid, (jnp.arange(top)[None, :] + rotation) % top, axis=1)


def shares(number_of, total, limit, slope, full):
    loads = [(1 << 20) // math.isqrt(grade ** slope) + 1 for grade in range(1, number_of + 1)]
    largest = limit if full else min(limit, max(-(-total // number_of), total * loads[0] // sum(loads)))
    least = 1 if total - largest >= number_of - 1 else 0
    counts, rest = [largest] + [least] * (number_of - 1), total - largest - least * (number_of - 1)
    while rest > 0:
        free = [i for i in range(1, number_of) if counts[i] < largest] or [i for i in range(1, number_of) if counts[i] < limit]
        mass, left = sum([loads[i] for i in free]), rest
        for i in free:
            more = min(limit - counts[i], max(1, left * loads[i] // mass), rest)
            counts[i] = counts[i] + more
            rest = rest - more
    return np.array(counts)


def normal_values(stream_key, shape, spread, most, split=(), held_as=jnp.bfloat16):
    values = spread * jax.random.normal(stream_key, shape, jnp.float32)
    if split:
        values = values * steps_of(stream_key, shape, split, -0.22, 0.18)
    return jnp.clip(values, -most, most).astype(held_as)


def setup_inputs(seed: int = 0) -> dict:
    arg_keys = jax.random.split(jax.random.key(seed), 11)
    volts = normal_values(arg_keys[0], (SCEN, LAYERS, NX, NY), 1.0, 6.0, ((2, 16), (3, 8)), jnp.float32)
    cap = jnp.clip(jnp.exp(math.log(1.0) - 2.9957323 * jax.random.uniform(arg_keys[1], (LAYERS, NX, NY), jnp.float32) ** steps_of(arg_keys[1], (LAYERS, NX, NY), ((1, 16), (2, 8)), -0.2, 0.2)), 0.05, 1.0)
    cond_x = jnp.clip(jnp.exp(math.log(2.0) - 1.3862944 * jax.random.uniform(arg_keys[2], (LAYERS, NX, NY), jnp.float32) ** steps_of(arg_keys[2], (LAYERS, NX, NY), ((1, 16), (2, 8)), -0.2, 0.2)), 0.5, 2.0)
    cond_y = jnp.clip(jnp.exp(math.log(2.0) - 1.3862944 * jax.random.uniform(arg_keys[3], (LAYERS, NX, NY), jnp.float32) ** steps_of(arg_keys[3], (LAYERS, NX, NY), ((1, 16), (2, 8)), -0.2, 0.2)), 0.5, 2.0)
    via = jnp.clip(jnp.exp(math.log(2.0) - 2.3025851 * jax.random.uniform(arg_keys[4], (LAYERS, NX, NY), jnp.float32) ** steps_of(arg_keys[4], (LAYERS, NX, NY), ((1, 16), (2, 8)), -0.2, 0.2)), 0.2, 2.0)
    waveforms = normal_values(arg_keys[5], (STEPS * SCEN, WAVES), 1.0, 6.0, (), jnp.float32)
    placement_keys = jax.random.split(jax.random.fold_in(arg_keys[6], 1), INSTANCES // INST_DEV)
    placement_turns = jax.random.permutation(jax.random.fold_in(arg_keys[6], 3), INSTANCES // INST_DEV)
    placement = jax.vmap(lambda own, number: assign_block(jax.random.fold_in(arg_keys[6], 2), own, number, INST_DEV, DEVICES, 1, CAP, 2))(placement_keys, placement_turns).reshape((INSTANCES, 1))
    cells = touch_ends(jax.random.randint(arg_keys[7], (INSTANCES,), 0, CX * CY), jax.random.fold_in(arg_keys[7], 1), 0, (CX * CY) - 1).astype(jnp.int32)
    wave_ids = touch_ends(jax.random.randint(arg_keys[8], (INSTANCES,), 0, WAVES), jax.random.fold_in(arg_keys[8], 1), 0, WAVES - 1).astype(jnp.int32)
    amps = jnp.clip(jnp.exp(math.log(4.0) - 2.0794415 * jax.random.uniform(arg_keys[9], (INSTANCES,), jnp.float32) ** steps_of(arg_keys[9], (INSTANCES,), ((0, 128),), -0.2, 0.2)), 0.5, 4.0)
    return dict(volts=volts, cap=cap, cond_x=cond_x, cond_y=cond_y, via=via, waveforms=waveforms, placement=placement, cells=cells, wave_ids=wave_ids, amps=amps)


def operate(field, cap, cond_x, cond_y, via):
    cond_x_low = jnp.pad(cond_x, ((0, 0), (1, 0), (0, 0)))[:, :-1, :]
    cond_y_low = jnp.pad(cond_y, ((0, 0), (0, 0), (1, 0)))[:, :, :-1]
    via_low = jnp.pad(via, ((1, 0), (0, 0), (0, 0)))[:-1]
    padded = jnp.pad(field, ((0, 0), (0, 0), (1, 1), (1, 1)))
    upper = jnp.pad(field, ((0, 0), (0, 1), (0, 0), (0, 0)))[:, 1:]
    lower = jnp.pad(field, ((0, 0), (1, 0), (0, 0), (0, 0)))[:, :-1]
    result = cap * field
    result = result + cond_x * (field - padded[:, :, 2:, 1:-1])
    result = result + cond_x_low * (field - padded[:, :, :-2, 1:-1])
    result = result + cond_y * (field - padded[:, :, 1:-1, 2:])
    result = result + cond_y_low * (field - padded[:, :, 1:-1, :-2])
    result = result + via * (field - upper) + via_low * (field - lower)
    return result

def gram(left, right):
    left_rows = left.reshape(left.shape[0], -1)
    right_rows = right.reshape(right.shape[0], -1)
    return lax.dot_general(left_rows, right_rows, (((1,), (1,)), ((), ())), precision=lax.Precision.HIGHEST)

def combine(coef, field):
    return jnp.einsum('st,slxy->tlxy', coef, field, precision=lax.Precision.HIGHEST)

def spd_solve(matrix, right):
    factor = jnp.linalg.cholesky(matrix)
    return jax.scipy.linalg.cho_solve((factor, True), right)

def reference(volts, cap, cond_x, cond_y, via, waveforms, placement, cells, wave_ids, amps):
    tile = placement[:, 0]
    row_x = tile // N_GY * CX + cells // CY
    col_y = tile % N_GY * CY + cells % CY
    flat = (row_x * NY + col_y).astype(jnp.int32)
    currents = (waveforms[:, wave_ids] * amps[None, :]).astype(jnp.bfloat16)
    injected = jax.ops.segment_sum(currents.astype(jnp.float32).T, flat, num_segments=NX * NY)
    injected = injected.T.reshape(STEPS, SCEN, NX, NY)
    voltage = volts
    residual = volts
    for step in range(STEPS):
        rhs = cap * voltage
        rhs = rhs.at[:, 0].add(-injected[step])
        iterate = voltage
        residual = rhs - operate(iterate, cap, cond_x, cond_y, via)
        direction = residual
        norm_gram = gram(residual, residual)
        for sweep in range(ITERS):
            image = operate(direction, cap, cond_x, cond_y, via)
            curve_gram = gram(direction, image)
            step_coef = spd_solve(curve_gram, norm_gram)
            iterate = iterate + combine(step_coef, direction)
            residual = residual - combine(step_coef, image)
            if sweep + 1 < ITERS:
                new_gram = gram(residual, residual)
                turn_coef = spd_solve(norm_gram, new_gram)
                direction = residual + combine(turn_coef, direction)
                norm_gram = new_gram
        voltage = iterate
    return (voltage, residual)
```

```python
import jax
import jax.numpy as jnp
from jax import lax
from jax.experimental import pallas as pl
from jax.experimental.pallas import tpu as pltpu
from jax.sharding import Mesh
from jax.sharding import PartitionSpec as P

GX = ("gx_0", "gx_1")
GY = ("gy_0", "gy_1")
GX_GY = GX + GY
F32 = jnp.float32
BF16 = jnp.bfloat16
HIGHEST = lax.Precision.HIGHEST
SHIFT = 7.0
SCALE = 7.0
XE = 22
YE = 144


def iota(shape, dim):
    return lax.broadcasted_iota(jnp.int32, shape, dim)


def dot(a, b, dims, precision=None):
    return lax.dot_general(
        a, b, (dims, ((), ())), precision=precision, preferred_element_type=F32
    )


def split3(x):
    hi = x.astype(BF16)
    rest = x - hi.astype(F32)
    mid = rest.astype(BF16)
    return hi, mid, (rest - mid.astype(F32)).astype(BF16)


def call(kernel, outs, args, scratch=(), limit=48):
    return pl.pallas_call(
        kernel,
        out_shape=tuple(jax.ShapeDtypeStruct(s, F32) for s in outs),
        scratch_shapes=list(scratch),
        compiler_params=pltpu.CompilerParams(vmem_limit_bytes=limit << 20),
        name=kernel.__name__,
    )(*args)


def to_lanes(volts, cap, cond_x, cond_y, via, v_out, c_out, low_out, high_out, stack):
    for c, ref in enumerate((cap, cond_x, cond_y, via)):
        stack[c * 32 : (c + 1) * 32, :] = ref[...]
    for x in range(8):
        rows = [volts[pl.ds(l * 8 + x, 32, stride=32), :] for l in range(4)]
        field = jnp.concatenate(rows, axis=0).T
        v_out[x] = field
        coef = stack[pl.ds(x, 16, stride=8), :]
        coef = jnp.concatenate([coef, jnp.zeros((112, 128), F32)], axis=0).T
        c_out[x] = coef
        low_out[x * 8 : x * 8 + 8, :] = field[:8]
        low_out[64 + x * 8 : 72 + x * 8, :] = coef[:8]
        high_out[x * 8 : x * 8 + 8, :] = field[120:]
        high_out[64 + x * 8 : 72 + x * 8, :] = coef[120:]


def widened(low, own, high, x, base=0):
    at = pl.ds(base + x * 8, 8)
    return jnp.concatenate([low[at, :], own[x], high[at, :]], axis=0)


def pack_rows(v, c, low, high, first_out, last_out):
    for x in range(8):
        field = widened(low, v, high, x)
        coef = widened(low, c, high, x, 64)
        packed = coef[:24]
        for g in range(1, 6):
            packed = packed + pltpu.roll(coef[g * 24 : (g + 1) * 24], 16 * g, 1)
        row = jnp.concatenate([field, packed], axis=0)
        if x < 7:
            first_out[x] = row
        if x > 0:
            last_out[x - 1] = row


def place_slots(tile, cell, wave, amp, out, acc):
    acc[...] = jnp.zeros_like(acc)
    lane = iota((128, 256), 1)
    before = ((iota((128, 256), 0) < lane) | (lane >= 128)).astype(F32).astype(BF16)
    tile_line = iota((128, 128), 0)

    def chunk(turn, seen):
        at = pl.ds(pl.multiple_of(turn * 8, 8), 8)
        tiles = tile[at, :]
        code = cell[at, :] * 64 + wave[at, :]
        parts = list(split3(amp[at, :]))
        parts.append((code >> 8).astype(F32).astype(BF16))
        parts.append((code & 255).astype(F32).astype(BF16))
        hits = [
            (tile_line == tiles[j : j + 1, :]).astype(F32) for j in range(8)
        ]
        hits_b = [h.astype(BF16) for h in hits]
        ranks = dot(jnp.concatenate(hits_b, axis=0), before, ((1,), (0,)))
        slots = []
        for j in range(8):
            rank = ranks[j * 128 : (j + 1) * 128]
            slot = jnp.sum(hits[j] * (rank[:, :128] + seen), axis=0, keepdims=True)
            slots.append((tile_line == slot.astype(jnp.int32)).astype(F32).astype(BF16))
            seen = seen + rank[:, 128:]
        hit = jnp.concatenate(hits_b, axis=1)
        slot = jnp.concatenate(slots, axis=1)
        left = []
        for part in parts:
            wide = part.astype(F32)
            wide = jnp.concatenate([wide[j : j + 1, :] for j in range(8)], axis=1)
            left.append(hit * wide.astype(BF16))
        acc[...] += dot(jnp.concatenate(left, axis=0), slot, ((1,), (1,)))
        return seen

    lax.fori_loop(0, 8, chunk, jnp.zeros((128, 128), F32))
    out[:, 0, :] = acc[0:128] + acc[128:256] + acc[256:384]
    out[:, 1, :] = acc[384:512] * 256.0 + acc[512:640]


def add_currents(slots, waves, out, low_out, high_out, acc):
    acc[...] = jnp.zeros_like(acc)
    table = jnp.concatenate([p.astype(F32) for p in split3(waves[...])], axis=0).astype(BF16)
    wave_line = iota((64, 512), 0)
    cell_line = iota((256, 512), 0)

    def chunk(turn, carry):
        rows = [slots[turn * 4 + j] for j in range(4)]
        amp = jnp.concatenate([r[0:1, :] for r in rows], axis=1)
        code = jnp.concatenate([r[1:2, :] for r in rows], axis=1).astype(jnp.int32)
        hit = (wave_line == (code & 63)).astype(F32).astype(BF16)
        picked = dot(table, hit, ((1,), (0,)))
        current = (picked[:64] + picked[64:128]) + picked[128:]
        current = (current * amp).astype(BF16).astype(F32)
        cell = code >> 6
        block = cell >> 8
        right = [jnp.where(block == r, current, 0.0).astype(BF16) for r in range(4)]
        left = (cell_line == (cell & 255)).astype(F32).astype(BF16)
        acc[...] += dot(left, jnp.concatenate(right, axis=0), ((1,), (1,)))
        return carry

    lax.fori_loop(0, 32, chunk, 0)
    low_lanes = iota((256, 128), 1) < 64
    for r in range(4):
        half = acc[:, (r // 2) * 128 : (r // 2 + 1) * 128]
        if r % 2:
            half = pltpu.roll(half, 64, 1)
        half = jnp.where(low_lanes, half, 0.0)
        for b in range(2):
            x = 2 * r + b
            rows = half[b * 128 : (b + 1) * 128]
            out[x] = rows
            low_out[x * 8 : x * 8 + 8, :] = rows[:8]
            high_out[x * 8 : x * 8 + 8, :] = rows[120:]


def pack_injected(own, low, high, first_out, last_out):
    rows = [widened(low, own, high, x) for x in range(8)]
    for j in range(3):
        first_out[j] = rows[j] + pltpu.roll(rows[j + 3], 64, 1)
        last_out[j] = rows[j + 2] + pltpu.roll(rows[j + 5], 64, 1)


def apply_row(src, i, diag, wx, wy, wv):
    v = src[i]
    wyi, wvi = wy[i], wv[i]
    out = diag[i] * v - wx[i] * src[i + 1] - wx[i - 1] * src[i - 1]
    out = out - wyi * pltpu.roll(v, YE - 1, 0) - pltpu.roll(wyi * v, 1, 0)
    return out - wvi * pltpu.roll(v, 96, 1) - pltpu.roll(wvi * v, 32, 1)


def power(src, dst, first, last, weights):
    def row(i, carry):
        dst[i] = apply_row(src, i, *weights)
        return carry

    lax.fori_loop(first, last + 1, row, 0)


def moments(fields, out, first):
    own = [f[first : first + 8, 8:136, :].reshape(1024, 128) for f in fields]
    lane = iota((32, 128), 1)
    blocks = [jnp.zeros((32, 128), F32), jnp.zeros((32, 128), F32)]
    for k in range(3):
        pair = jnp.concatenate([own[k], own[k + 1]], axis=1)
        product = dot(own[k], pair, ((0,), (0,)), HIGHEST)
        for b in range(2):
            n = 2 * k + b
            place = 32 * (n % 4)
            total = jnp.zeros((32, 128), F32)
            for l in range(4):
                piece = product[l * 32 : (l + 1) * 32, b * 128 : (b + 1) * 128]
                turn = (place - 32 * l) % 128
                total = total + (pltpu.roll(piece, turn, 1) if turn else piece)
            inside = (lane >= place) & (lane < place + 32)
            blocks[n // 4] = blocks[n // 4] + jnp.where(inside, total, 0.0)
    out[0:32, :] = blocks[0]
    out[32:64, :] = blocks[1]


def coefficients(gram):
    lane = iota((32, 128), 1)

    def moment(k, place):
        block = gram[(k // 4) * 32 : (k // 4) * 32 + 32, :]
        turn = (place - 32 * (k % 4)) % 128
        block = pltpu.roll(block, turn, 1) if turn else block
        return jnp.where((lane >= place) & (lane < place + 32), block, 0.0)

    tiles = []
    for i in range(3):
        block = moment(i, 96)
        for j in range(3):
            block = block + SCALE * moment(i + j + 1, 32 * j) + SHIFT * moment(i + j, 32 * j)
        tiles += [block[r * 8 : r * 8 + 8] for r in range(4)]
    sub = iota((8, 128), 0)
    for k in range(96):
        mine, at = tiles[k // 8], k % 8
        row = mine[at : at + 1, :]
        row = row * (1.0 / row[:, k : k + 1])
        new = []
        for t, block in enumerate(tiles):
            less = block - block[:, k : k + 1] * row
            new.append(jnp.where(sub == at, row, less) if t == k // 8 else less)
        tiles = new
    lane = iota((32, 128), 1)
    outs = []
    for i in range(3):
        y = jnp.concatenate(tiles[i * 4 : i * 4 + 4], axis=0)
        y = jnp.where(lane >= 96, y, 0.0)
        y = y + pltpu.roll(y, 32, 1) + pltpu.roll(y, 64, 1) + pltpu.roll(y, 96, 1)
        outs.append(
            jnp.concatenate([jnp.where(lane // 32 == l, y, 0.0) for l in range(4)], axis=0)
        )
    return outs


def combination(gram):
    y0, y1, y2 = coefficients(gram)
    step = jnp.concatenate([y0, y1, y2, jnp.zeros_like(y0)], axis=0)
    less = jnp.concatenate(
        [
            -SHIFT * y0,
            -SCALE * y0 - SHIFT * y1,
            -SCALE * y1 - SHIFT * y2,
            -SCALE * y2,
        ],
        axis=0,
    )
    return jnp.concatenate([step, less], axis=1)


def first_basis(
    v, c, low, high, x_low, x_high, inj, i_low, i_high, ix_low, ix_high,
    diag, wx, wy, wv, cap, change, v0, v1, v2, v3, gram, ext,
):
    lane = iota((YE, 128), 1)
    n = iota((128, 512), 1)
    q = iota((128, 512), 0)
    spread = ((q % 16 == (n // 128) * 4 + (n % 128) // 32) & (q < 48)).astype(F32).astype(BF16)

    def expand(i, coef):
        hi, mid, lo = [p.astype(F32) for p in split3(coef)]
        parts = hi + pltpu.roll(mid, 16, 1) + pltpu.roll(lo, 32, 1)
        wide = dot(parts.astype(BF16), spread, ((1,), (0,)))
        cap[i] = wide[:, :128]
        wx[i] = wide[:, 128:256]
        wy[i] = wide[:, 256:384]
        wv[i] = jnp.where(lane < 96, wide[:, 384:], 0.0)
        diag[i] = wide[:, :128] + wide[:, 384:]

    def halo_row(j, ref, base):
        ext[base + j] = ref[j, :YE, :]
        packed = ref[j, YE:, :]
        groups = [packed] + [pltpu.roll(packed, 128 - 16 * g, 1) for g in range(1, 6)]
        coef = jnp.concatenate(groups, axis=0)
        expand(base + j, jnp.where(lane < 16, coef, 0.0))

    def own_row(x, carry):
        at = pl.ds(pl.multiple_of(x * 8, 8), 8)
        at_c = pl.ds(pl.multiple_of(64 + x * 8, 8), 8)
        ext[7 + x] = jnp.concatenate([low[at, :], v[x], high[at, :]], axis=0)
        expand(7 + x, jnp.concatenate([low[at_c, :], c[x], high[at_c, :]], axis=0))
        return carry

    def halo_rows(j, carry):
        halo_row(j, x_low, 0)
        halo_row(j, x_high, 15)
        return carry

    lax.fori_loop(0, 8, own_row, 0)
    lax.fori_loop(0, 7, halo_rows, 0)

    def diagonal(i, carry):
        total = diag[i] + wx[i] + wx[i - 1] + wy[i] + pltpu.roll(wy[i], 1, 0)
        total = total + pltpu.roll(wv[i], 32, 1)
        diag[i] = (total - SHIFT) * (1.0 / SCALE)
        return carry

    lax.fori_loop(1, 21, diagonal, 0)

    def edges(i, carry):
        wx[i] = jnp.where(cap[i + 1] > 0, wx[i] * (1.0 / SCALE), 0.0)
        wy[i] = jnp.where(pltpu.roll(cap[i], YE - 1, 0) > 0, wy[i] * (1.0 / SCALE), 0.0)
        wv[i] = wv[i] * (1.0 / SCALE)
        return carry

    lax.fori_loop(0, 21, edges, 0)
    weights = (diag, wx, wy, wv)

    def start(i, both):
        now = jnp.where(lane < 32, both, 0.0)
        then = jnp.where(lane < 32, pltpu.roll(both, 96, 1), 0.0)
        change[i] = now - then
        e = ext[i]
        v0[i] = (cap[i] - SHIFT) * e - SCALE * apply_row(ext, i, *weights) - now

    def own_start(x, carry):
        at = pl.ds(pl.multiple_of(x * 8, 8), 8)
        start(7 + x, jnp.concatenate([i_low[at, :], inj[x], i_high[at, :]], axis=0))
        return carry

    def halo_start(j, carry):
        for ref, base in ((ix_low, 1), (ix_high, 15)):
            both = ref[j]
            start(base + j, both)
            start(base + 3 + j, pltpu.roll(both, 64, 1))
        return carry

    lax.fori_loop(0, 8, own_start, 0)
    lax.fori_loop(0, 3, halo_start, 0)
    power(v0, v1, 2, 19, weights)
    power(v1, v2, 3, 18, weights)
    power(v2, v3, 4, 17, weights)
    moments((v0, v1, v2, v3), gram, 7)


def second_basis(
    gram, diag, wx, wy, wv, cap, change, v0, v1, v2, v3, v,
    w0, w1, w2, w3, volts, gram_out, b0, b1, b2, b3, step,
):
    weights = (diag, wx, wy, wv)
    mix = combination(gram)

    def row(i, carry):
        fields = jnp.concatenate([v0[i], v1[i], v2[i], v3[i]], axis=1)
        both = dot(fields, mix, ((1,), (0,)), HIGHEST)
        moved = both[:, :128]
        step[i] = moved
        b0[i] = v0[i] + both[:, 128:] + cap[i] * moved + change[i]
        return carry

    lax.fori_loop(4, 18, row, 0)
    power(b0, b1, 5, 16, weights)
    power(b1, b2, 6, 15, weights)
    power(b2, b3, 7, 14, weights)
    moments((b0, b1, b2, b3), gram_out, 7)
    for x in range(8):
        volts[x] = v[x] + step[7 + x, 8:136, :]
        for src, dst in ((b0, w0), (b1, w1), (b2, w2), (b3, w3)):
            dst[x] = src[7 + x, 8:136, :]


def finish(gram, w0, w1, w2, w3, volts, volts_out, residual_out):
    mix = combination(gram)
    for x in range(8):
        fields = jnp.concatenate([w0[x], w1[x], w2[x], w3[x]], axis=1)
        both = dot(fields, mix, ((1,), (0,)), HIGHEST)
        for value, out in (
            (volts[x] + both[:, :128], volts_out),
            (w0[x] + both[:, 128:], residual_out),
        ):
            value = value.T
            for l in range(4):
                out[pl.ds(l * 8 + x, 32, stride=32), :] = value[l * 32 : (l + 1) * 32]


def neighbours(to_low, to_high, axis):
    size = lax.axis_size(axis)
    up = [(i, i + 1) for i in range(size - 1)]
    from_low = lax.ppermute(to_high, axis, up)
    return from_low, lax.ppermute(to_low, axis, [(b, a) for a, b in up])


def everywhere(x):
    x = x + lax.ppermute(x, "gy_1", [(0, 1), (1, 0)])
    for axis in ("gy_0", "gx_1", "gx_0"):
        x = x + lax.ppermute(x, axis, [(0, 1), (1, 0), (2, 3), (3, 2)])
        x = x + lax.ppermute(x, axis, [(0, 3), (3, 0), (1, 2), (2, 1)])
    return x


def body(volts, cap, cond_x, cond_y, via, waveforms, placement, cells, wave_ids, amps):
    vmem = pltpu.VMEM
    coefs = [a.reshape(32, 128) for a in (cap, cond_x, cond_y, via)]
    v, c, y_low, y_high = call(
        to_lanes,
        [(8, 128, 128), (8, 128, 128), (128, 128), (128, 128)],
        [volts.reshape(1024, 128)] + coefs,
        [vmem((128, 128), F32)],
    )
    y_low, y_high = neighbours(y_low, y_high, GY)
    lists = [a.reshape(64, 128) for a in (placement, cells, wave_ids, amps)]
    (slots,) = call(place_slots, [(128, 2, 128)], lists, [vmem((640, 128), F32)])
    x_low, x_high = call(pack_rows, [(7, 168, 128)] * 2, [v, c, y_low, y_high])
    x_low, x_high = neighbours(x_low, x_high, GX)
    slots = lax.all_to_all(slots, GX_GY, split_axis=0, concat_axis=0, tiled=True)
    inj, i_low, i_high = call(
        add_currents,
        [(8, 128, 128), (64, 128), (64, 128)],
        [slots, waveforms],
        [vmem((256, 256), F32)],
    )
    i_low, i_high = neighbours(i_low, i_high, GY)
    ix_low, ix_high = call(pack_injected, [(3, YE, 128)] * 2, [inj, i_low, i_high])
    ix_low, ix_high = neighbours(ix_low, ix_high, GX)
    wide = (XE, YE, 128)
    *kept, gram = call(
        first_basis,
        [wide] * 10 + [(64, 128)],
        [v, c, y_low, y_high, x_low, x_high, inj, i_low, i_high, ix_low, ix_high],
        [vmem(wide, F32)],
    )
    own = (8, 128, 128)
    *basis, gram = call(
        second_basis,
        [own] * 5 + [(64, 128)],
        [everywhere(gram)] + kept + [v],
        [vmem(wide, F32)] * 5,
    )
    outs = call(finish, [(1024, 128)] * 2, [everywhere(gram)] + basis)
    return tuple(o.reshape(volts.shape) for o in outs)


def solution(mesh):
    finer = Mesh(mesh.devices.reshape(4, 4, 4, 2), ("gx_0", "gx_1", "gy_0", "gy_1"))
    in_specs = (
        P(None, None, GX, GY),
        P(None, GX, GY),
        P(None, GX, GY),
        P(None, GX, GY),
        P(None, GX, GY),
        P(),
        P(GX_GY, None),
        P(GX_GY),
        P(GX_GY),
        P(GX_GY),
    )
    out_specs = (P(None, None, GX, GY), P(None, None, GX, GY))
    return jax.shard_map(body, mesh=finer, in_specs=in_specs, out_specs=out_specs, check_vma=False)
```

```python
import jax
import jax.numpy as jnp
from jax import lax
from jax.experimental import pallas as pl
from jax.experimental.pallas import tpu as pltpu
from jax.sharding import Mesh
from jax.sharding import PartitionSpec as P

GX = ("gx_0", "gx_1")
GY = ("gy_0", "gy_1")
GX_GY = GX + GY
F32 = jnp.float32
BF16 = jnp.bfloat16
HIGHEST = lax.Precision.HIGHEST
SHIFT = 7.0
SCALE = 7.0
XE = 22
YE = 144


def iota(shape, dim):
    return lax.broadcasted_iota(jnp.int32, shape, dim)


def dot(a, b, dims, precision=None):
    return lax.dot_general(
        a, b, (dims, ((), ())), precision=precision, preferred_element_type=F32
    )


def split2(x):
    hi = x.astype(BF16)
    return hi, (x - hi.astype(F32)).astype(BF16)


def dot_split(a, b, dims):
    a_hi, a_lo = split2(a)
    b_hi, b_lo = split2(b)
    return dot(a_hi, b_hi, dims) + dot(a_hi, b_lo, dims) + dot(a_lo, b_hi, dims)


def split3(x):
    hi = x.astype(BF16)
    rest = x - hi.astype(F32)
    mid = rest.astype(BF16)
    return hi, mid, (rest - mid.astype(F32)).astype(BF16)


def call(kernel, outs, args, scratch=(), limit=14):
    return pl.pallas_call(
        kernel,
        out_shape=tuple(jax.ShapeDtypeStruct(s, F32) for s in outs),
        scratch_shapes=list(scratch),
        compiler_params=pltpu.CompilerParams(vmem_limit_bytes=limit << 20),
        name=kernel.__name__,
    )(*args)


def to_lanes(volts, cap, cond_x, cond_y, via, v_out, c_out, low_out, high_out, stack):
    for c, ref in enumerate((cap, cond_x, cond_y, via)):
        stack[c * 32 : (c + 1) * 32, :] = ref[...]
    for x in range(8):
        rows = [volts[pl.ds(l * 8 + x, 32, stride=32), :] for l in range(4)]
        field = jnp.concatenate(rows, axis=0).T
        v_out[x] = field
        coef = stack[pl.ds(x, 16, stride=8), :]
        coef = jnp.concatenate([coef, jnp.zeros((112, 128), F32)], axis=0).T
        c_out[x] = coef
        low_out[x * 8 : x * 8 + 8, :] = field[:8]
        low_out[64 + x * 8 : 72 + x * 8, :] = coef[:8]
        high_out[x * 8 : x * 8 + 8, :] = field[120:]
        high_out[64 + x * 8 : 72 + x * 8, :] = coef[120:]


def widened(low, own, high, x, base=0):
    at = pl.ds(base + x * 8, 8)
    return jnp.concatenate([low[at, :], own[x], high[at, :]], axis=0)


def pack_rows(v, c, low, high, first_out, last_out):
    for x in range(8):
        field = widened(low, v, high, x)
        coef = widened(low, c, high, x, 64)
        packed = coef[:24]
        for g in range(1, 6):
            packed = packed + pltpu.roll(coef[g * 24 : (g + 1) * 24], 16 * g, 1)
        row = jnp.concatenate([field, packed], axis=0)
        if x < 7:
            first_out[x] = row
        if x > 0:
            last_out[x - 1] = row


def place_slots(tile, cell, wave, amp, out, acc):
    acc[...] = jnp.zeros_like(acc)
    lane = iota((128, 256), 1)
    before = ((iota((128, 256), 0) < lane) | (lane >= 128)).astype(F32).astype(BF16)
    tile_line = iota((128, 128), 0)

    def chunk(turn, seen):
        at = pl.ds(pl.multiple_of(turn * 8, 8), 8)
        tiles = tile[at, :]
        code = cell[at, :] * 64 + wave[at, :]
        parts = list(split3(amp[at, :]))
        parts.append((code >> 8).astype(F32).astype(BF16))
        parts.append((code & 255).astype(F32).astype(BF16))
        hits = [
            (tile_line == tiles[j : j + 1, :]).astype(F32) for j in range(8)
        ]
        hits_b = [h.astype(BF16) for h in hits]
        ranks = dot(jnp.concatenate(hits_b, axis=0), before, ((1,), (0,)))
        slots = []
        for j in range(8):
            rank = ranks[j * 128 : (j + 1) * 128]
            slot = jnp.sum(hits[j] * (rank[:, :128] + seen), axis=0, keepdims=True)
            slots.append((tile_line == slot.astype(jnp.int32)).astype(F32).astype(BF16))
            seen = seen + rank[:, 128:]
        hit = jnp.concatenate(hits_b, axis=1)
        slot = jnp.concatenate(slots, axis=1)
        left = []
        for part in parts:
            wide = part.astype(F32)
            wide = jnp.concatenate([wide[j : j + 1, :] for j in range(8)], axis=1)
            left.append(hit * wide.astype(BF16))
        acc[...] += dot(jnp.concatenate(left, axis=0), slot, ((1,), (1,)))
        return seen

    lax.fori_loop(0, 8, chunk, jnp.zeros((128, 128), F32))
    out[:, 0, :] = acc[0:128] + acc[128:256] + acc[256:384]
    out[:, 1, :] = acc[384:512] * 256.0 + acc[512:640]


def add_currents(slots, waves, out, low_out, high_out, acc):
    acc[...] = jnp.zeros_like(acc)
    table = jnp.concatenate([p.astype(F32) for p in split3(waves[...])], axis=0).astype(BF16)
    wave_line = iota((64, 512), 0)
    cell_line = iota((256, 512), 0)

    def chunk(turn, carry):
        rows = [slots[turn * 4 + j] for j in range(4)]
        amp = jnp.concatenate([r[0:1, :] for r in rows], axis=1)
        code = jnp.concatenate([r[1:2, :] for r in rows], axis=1).astype(jnp.int32)
        hit = (wave_line == (code & 63)).astype(F32).astype(BF16)
        picked = dot(table, hit, ((1,), (0,)))
        current = (picked[:64] + picked[64:128]) + picked[128:]
        current = (current * amp).astype(BF16).astype(F32)
        cell = code >> 6
        block = cell >> 8
        right = [jnp.where(block == r, current, 0.0).astype(BF16) for r in range(4)]
        left = (cell_line == (cell & 255)).astype(F32).astype(BF16)
        acc[...] += dot(left, jnp.concatenate(right, axis=0), ((1,), (1,)))
        return carry

    lax.fori_loop(0, 32, chunk, 0)
    low_lanes = iota((256, 128), 1) < 64
    for r in range(4):
        half = acc[:, (r // 2) * 128 : (r // 2 + 1) * 128]
        if r % 2:
            half = pltpu.roll(half, 64, 1)
        half = jnp.where(low_lanes, half, 0.0)
        for b in range(2):
            x = 2 * r + b
            rows = half[b * 128 : (b + 1) * 128]
            out[x] = rows
            low_out[x * 8 : x * 8 + 8, :] = rows[:8]
            high_out[x * 8 : x * 8 + 8, :] = rows[120:]


def pack_injected(own, low, high, first_out, last_out):
    rows = [widened(low, own, high, x) for x in range(8)]
    for j in range(3):
        first_out[j] = rows[j] + pltpu.roll(rows[j + 3], 64, 1)
        last_out[j] = rows[j + 2] + pltpu.roll(rows[j + 5], 64, 1)


def apply_row(src, i, diag, wx, wy, wv):
    v = src[i]
    wyi, wvi = wy[i], wv[i]
    out = diag[i] * v - wx[i] * src[i + 1] - wx[i - 1] * src[i - 1]
    out = out - wyi * pltpu.roll(v, YE - 1, 0) - pltpu.roll(wyi * v, 1, 0)
    return out - wvi * pltpu.roll(v, 96, 1) - pltpu.roll(wvi * v, 32, 1)


def power(src, dst, first, last, weights):
    def row(i, carry):
        dst[i] = apply_row(src, i, *weights)
        return carry

    lax.fori_loop(first, last + 1, row, 0)


def moments(fields, out, first):
    own = [f[first : first + 8, 8:136, :].reshape(1024, 128) for f in fields]
    lane = iota((32, 128), 1)
    blocks = [jnp.zeros((32, 128), F32), jnp.zeros((32, 128), F32)]
    for k in range(3):
        pair = jnp.concatenate([own[k], own[k + 1]], axis=1)
        product = dot_split(own[k], pair, ((0,), (0,)))
        for b in range(2):
            n = 2 * k + b
            place = 32 * (n % 4)
            total = jnp.zeros((32, 128), F32)
            for l in range(4):
                piece = product[l * 32 : (l + 1) * 32, b * 128 : (b + 1) * 128]
                turn = (place - 32 * l) % 128
                total = total + (pltpu.roll(piece, turn, 1) if turn else piece)
            inside = (lane >= place) & (lane < place + 32)
            blocks[n // 4] = blocks[n // 4] + jnp.where(inside, total, 0.0)
    out[0:32, :] = blocks[0]
    out[32:64, :] = blocks[1]


def coefficients(gram):
    lane = iota((32, 128), 1)

    def moment(k, place):
        block = gram[(k // 4) * 32 : (k // 4) * 32 + 32, :]
        turn = (place - 32 * (k % 4)) % 128
        block = pltpu.roll(block, turn, 1) if turn else block
        return jnp.where((lane >= place) & (lane < place + 32), block, 0.0)

    tiles = []
    for i in range(3):
        block = moment(i, 96)
        for j in range(3):
            block = block + SCALE * moment(i + j + 1, 32 * j) + SHIFT * moment(i + j, 32 * j)
        tiles += [block[r * 8 : r * 8 + 8] for r in range(4)]
    sub = iota((8, 128), 0)
    for t in range(12):
        rows = tiles[t]
        cols = [jnp.broadcast_to(rows[:, t * 8 + j : t * 8 + j + 1], (8, 128)) for j in range(8)]
        for j in range(8):
            inverse = 1.0 / cols[j][j : j + 1, :]
            pivot = rows[j : j + 1, :] * inverse
            rows = jnp.where(sub == j, pivot, rows - cols[j] * pivot)
            for n in range(j + 1, 8):
                top = cols[n][j : j + 1, :] * inverse
                cols[n] = jnp.where(sub == j, top, cols[n] - cols[j] * top)
        for i in range(12):
            block = tiles[i]
            for j in range(8):
                if i != t:
                    block = block - tiles[i][:, t * 8 + j : t * 8 + j + 1] * rows[j : j + 1, :]
            tiles[i] = block
        tiles[t] = rows
    lane = iota((32, 128), 1)
    outs = []
    for i in range(3):
        y = jnp.concatenate(tiles[i * 4 : i * 4 + 4], axis=0)
        y = jnp.where(lane >= 96, y, 0.0)
        y = y + pltpu.roll(y, 32, 1) + pltpu.roll(y, 64, 1) + pltpu.roll(y, 96, 1)
        outs.append(
            jnp.concatenate([jnp.where(lane // 32 == l, y, 0.0) for l in range(4)], axis=0)
        )
    return outs


def combination(gram):
    y0, y1, y2 = coefficients(gram)
    step = jnp.concatenate([y0, y1, y2, jnp.zeros_like(y0)], axis=0)
    less = jnp.concatenate(
        [
            -SHIFT * y0,
            -SCALE * y0 - SHIFT * y1,
            -SCALE * y1 - SHIFT * y2,
            -SCALE * y2,
        ],
        axis=0,
    )
    return jnp.concatenate([step, less], axis=1)


def grid_weights(
    v, c, low, high, x_low, x_high, diag, wx, wy, wv, cap, free, ext,
):
    lane = iota((YE, 128), 1)
    n = iota((128, 512), 1)
    q = iota((128, 512), 0)
    spread = ((q % 16 == (n // 128) * 4 + (n % 128) // 32) & (q < 48)).astype(F32).astype(BF16)

    def expand(i, coef):
        hi, mid, lo = [p.astype(F32) for p in split3(coef)]
        parts = hi + pltpu.roll(mid, 16, 1) + pltpu.roll(lo, 32, 1)
        wide = dot(parts.astype(BF16), spread, ((1,), (0,)))
        cap[i] = wide[:, :128]
        wx[i] = wide[:, 128:256]
        wy[i] = wide[:, 256:384]
        wv[i] = jnp.where(lane < 96, wide[:, 384:], 0.0)
        diag[i] = wide[:, :128] + wide[:, 384:]

    def halo_row(j, ref, base):
        ext[base + j] = ref[j, :YE, :]
        packed = ref[j, YE:, :]
        groups = [packed] + [pltpu.roll(packed, 128 - 16 * g, 1) for g in range(1, 6)]
        coef = jnp.concatenate(groups, axis=0)
        expand(base + j, jnp.where(lane < 16, coef, 0.0))

    def own_row(x, carry):
        at = pl.ds(pl.multiple_of(x * 8, 8), 8)
        at_c = pl.ds(pl.multiple_of(64 + x * 8, 8), 8)
        ext[7 + x] = jnp.concatenate([low[at, :], v[x], high[at, :]], axis=0)
        expand(7 + x, jnp.concatenate([low[at_c, :], c[x], high[at_c, :]], axis=0))
        return carry

    def halo_rows(j, carry):
        halo_row(j, x_low, 0)
        halo_row(j, x_high, 15)
        return carry

    lax.fori_loop(0, 8, own_row, 0)
    lax.fori_loop(0, 7, halo_rows, 0)

    def diagonal(i, carry):
        total = diag[i] + wx[i] + wx[i - 1] + wy[i] + pltpu.roll(wy[i], 1, 0)
        total = total + pltpu.roll(wv[i], 32, 1)
        diag[i] = (total - SHIFT) * (1.0 / SCALE)
        return carry

    lax.fori_loop(1, 21, diagonal, 0)

    def edges(i, carry):
        wx[i] = jnp.where(cap[i + 1] > 0, wx[i] * (1.0 / SCALE), 0.0)
        wy[i] = jnp.where(pltpu.roll(cap[i], YE - 1, 0) > 0, wy[i] * (1.0 / SCALE), 0.0)
        wv[i] = wv[i] * (1.0 / SCALE)
        return carry

    lax.fori_loop(0, 21, edges, 0)
    weights = (diag, wx, wy, wv)


    def start(i, carry):
        e = ext[i]
        free[i] = (cap[i] - SHIFT) * e - SCALE * apply_row(ext, i, *weights)
        return carry

    lax.fori_loop(1, 21, start, 0)


def first_basis(
    diag, wx, wy, wv, free, inj, i_low, i_high, ix_low, ix_high,
    change, v0, v1, v2, v3, gram,
):
    lane = iota((YE, 128), 1)
    weights = (diag, wx, wy, wv)

    def start(i, both):
        now = jnp.where(lane < 32, both, 0.0)
        then = jnp.where(lane < 32, pltpu.roll(both, 96, 1), 0.0)
        change[i] = now - then
        v0[i] = free[i] - now

    def own_start(x, carry):
        at = pl.ds(pl.multiple_of(x * 8, 8), 8)
        start(7 + x, jnp.concatenate([i_low[at, :], inj[x], i_high[at, :]], axis=0))
        return carry

    def halo_start(j, carry):
        for ref, base in ((ix_low, 1), (ix_high, 15)):
            both = ref[j]
            start(base + j, both)
            start(base + 3 + j, pltpu.roll(both, 64, 1))
        return carry

    lax.fori_loop(0, 8, own_start, 0)
    lax.fori_loop(0, 3, halo_start, 0)
    power(v0, v1, 2, 19, weights)
    power(v1, v2, 3, 18, weights)
    power(v2, v3, 4, 17, weights)
    moments((v0, v1, v2, v3), gram, 7)


def second_basis(
    gram, diag, wx, wy, wv, cap, change, v0, v1, v2, v3, v,
    w0, w1, w2, w3, volts, gram_out, b0, b1, b2, b3, step,
):
    weights = (diag, wx, wy, wv)
    mix = combination(gram)

    def row(i, carry):
        fields = jnp.concatenate([v0[i], v1[i], v2[i], v3[i]], axis=1)
        both = dot_split(fields, mix, ((1,), (0,)))
        moved = both[:, :128]
        step[i] = moved
        b0[i] = v0[i] + both[:, 128:] + cap[i] * moved + change[i]
        return carry

    lax.fori_loop(4, 18, row, 0)
    power(b0, b1, 5, 16, weights)
    power(b1, b2, 6, 15, weights)
    power(b2, b3, 7, 14, weights)
    moments((b0, b1, b2, b3), gram_out, 7)
    for x in range(8):
        volts[x] = v[x] + step[7 + x, 8:136, :]
        for src, dst in ((b0, w0), (b1, w1), (b2, w2), (b3, w3)):
            dst[x] = src[7 + x, 8:136, :]


def finish(gram, w0, w1, w2, w3, volts, volts_out, residual_out):
    mix = combination(gram)
    for x in range(8):
        fields = jnp.concatenate([w0[x], w1[x], w2[x], w3[x]], axis=1)
        both = dot_split(fields, mix, ((1,), (0,)))
        for value, out in (
            (volts[x] + both[:, :128], volts_out),
            (w0[x] + both[:, 128:], residual_out),
        ):
            value = value.T
            for l in range(4):
                out[pl.ds(l * 8 + x, 32, stride=32), :] = value[l * 32 : (l + 1) * 32]


def neighbours(to_low, to_high, axis):
    size = lax.axis_size(axis)
    up = [(i, i + 1) for i in range(size - 1)]
    from_low = lax.ppermute(to_high, axis, up)
    return from_low, lax.ppermute(to_low, axis, [(b, a) for a, b in up])


def everywhere(x):
    x = x + lax.ppermute(x, "gy_1", [(0, 1), (1, 0)])
    for axis in ("gy_0", "gx_1", "gx_0"):
        x = x + lax.ppermute(x, axis, [(0, 1), (1, 0), (2, 3), (3, 2)])
        x = x + lax.ppermute(x, axis, [(0, 3), (3, 0), (1, 2), (2, 1)])
    return x


def exchange(slots):
    return lax.all_to_all(slots, GX_GY, split_axis=0, concat_axis=0, tiled=True)


def body(volts, cap, cond_x, cond_y, via, waveforms, placement, cells, wave_ids, amps):
    vmem = pltpu.VMEM
    coefs = [a.reshape(32, 128) for a in (cap, cond_x, cond_y, via)]
    v, c, y_low, y_high = call(
        to_lanes,
        [(8, 128, 128), (8, 128, 128), (128, 128), (128, 128)],
        [volts.reshape(1024, 128)] + coefs,
        [vmem((128, 128), F32)],
    )
    y_low, y_high = neighbours(y_low, y_high, GY)
    lists = [a.reshape(64, 128) for a in (placement, cells, wave_ids, amps)]
    (slots,) = call(place_slots, [(128, 2, 128)], lists, [vmem((640, 128), F32)])
    y_low, y_high, slots = lax.optimization_barrier((y_low, y_high, slots))
    x_low, x_high = call(pack_rows, [(7, 168, 128)] * 2, [v, c, y_low, y_high])
    x_low, x_high = neighbours(x_low, x_high, GX)
    slots = exchange(slots)
    inj, i_low, i_high = call(
        add_currents,
        [(8, 128, 128), (64, 128), (64, 128)],
        [slots, waveforms],
        [vmem((256, 256), F32)],
    )
    i_low, i_high = neighbours(i_low, i_high, GY)
    ix_low, ix_high = call(pack_injected, [(3, YE, 128)] * 2, [inj, i_low, i_high])
    ix_low, ix_high = neighbours(ix_low, ix_high, GX)
    wide = (XE, YE, 128)
    diag, wx, wy, wv, cap, free = call(
        grid_weights, [wide] * 6, [v, c, y_low, y_high, x_low, x_high], [vmem(wide, F32)]
    )
    *kept, gram = call(
        first_basis,
        [wide] * 5 + [(64, 128)],
        [diag, wx, wy, wv, free, inj, i_low, i_high, ix_low, ix_high],
    )
    own = (8, 128, 128)
    *basis, gram = call(
        second_basis,
        [own] * 5 + [(64, 128)],
        [everywhere(gram), diag, wx, wy, wv, cap] + kept + [v],
        [vmem(wide, F32)] * 5,
    )
    outs = call(finish, [(1024, 128)] * 2, [everywhere(gram)] + basis)
    return tuple(o.reshape(volts.shape) for o in outs)


def solution(mesh):
    finer = Mesh(mesh.devices.reshape(4, 4, 4, 2), ("gx_0", "gx_1", "gy_0", "gy_1"))
    in_specs = (
        P(None, None, GX, GY),
        P(None, GX, GY),
        P(None, GX, GY),
        P(None, GX, GY),
        P(None, GX, GY),
        P(),
        P(GX_GY, None),
        P(GX_GY),
        P(GX_GY),
        P(GX_GY),
    )
    out_specs = (P(None, None, GX, GY), P(None, None, GX, GY))
    return jax.shard_map(body, mesh=finer, in_specs=in_specs, out_specs=out_specs, check_vma=False)
```

```python
import jax
import jax.numpy as jnp
from jax import lax
from jax.experimental import pallas as pl
from jax.experimental.pallas import tpu as pltpu
from jax.sharding import Mesh
from jax.sharding import PartitionSpec as P

GX = ("gx_0", "gx_1")
GY = ("gy_0", "gy_1")
GX_GY = GX + GY
F32 = jnp.float32
BF16 = jnp.bfloat16
HIGHEST = lax.Precision.HIGHEST
SHIFT = 7.0
SCALE = 7.0
XE = 22
YE = 144


def iota(shape, dim):
    return lax.broadcasted_iota(jnp.int32, shape, dim)


def dot(a, b, dims, precision=None):
    return lax.dot_general(
        a, b, (dims, ((), ())), precision=precision, preferred_element_type=F32
    )


def split2(x):
    hi = x.astype(BF16)
    return hi, (x - hi.astype(F32)).astype(BF16)


def dot_split(a, b, dims):
    a_hi, a_lo = split2(a)
    b_hi, b_lo = split2(b)
    return dot(a_hi, b_hi, dims) + dot(a_hi, b_lo, dims) + dot(a_lo, b_hi, dims)


def split3(x):
    hi = x.astype(BF16)
    rest = x - hi.astype(F32)
    mid = rest.astype(BF16)
    return hi, mid, (rest - mid.astype(F32)).astype(BF16)


def call(kernel, outs, args, scratch=(), limit=14, in_specs=None):
    outs = [o if isinstance(o, jax.ShapeDtypeStruct) else jax.ShapeDtypeStruct(o, F32) for o in outs]
    specs = {} if in_specs is None else {"in_specs": in_specs}
    return pl.pallas_call(
        kernel,
        out_shape=tuple(outs),
        scratch_shapes=list(scratch),
        **specs,
        compiler_params=pltpu.CompilerParams(vmem_limit_bytes=limit << 20),
        name=kernel.__name__,
    )(*args)


def to_lanes(
    volts_in, cap, cond_x, cond_y, via, tile_in, cell_in, wave_in, amp_in,
    v_out, c_out, low_out, high_out, tile, cell, wave, amp, volts, stack, sems,
):
    pairs = [(volts_in, volts)]
    for c, ref in enumerate((cap, cond_x, cond_y, via)):
        pairs.append((ref, stack.at[pl.ds(c * 32, 32), :]))
    pairs += [(tile_in, tile), (cell_in, cell), (wave_in, wave), (amp_in, amp)]
    copies = [pltpu.make_async_copy(src, dst, sems.at[n]) for n, (src, dst) in enumerate(pairs)]
    for copy in copies:
        copy.start()
    for copy in copies:
        copy.wait()
    for x in range(8):
        rows = [volts[pl.ds(l * 8 + x, 32, stride=32), :] for l in range(4)]
        field = jnp.concatenate(rows, axis=0).T
        v_out[x] = field
        coef = stack[pl.ds(x, 16, stride=8), :]
        coef = jnp.concatenate([coef, jnp.zeros((112, 128), F32)], axis=0).T
        c_out[x] = coef
        low_out[x * 8 : x * 8 + 8, :] = field[:8]
        low_out[64 + x * 8 : 72 + x * 8, :] = coef[:8]
        high_out[x * 8 : x * 8 + 8, :] = field[120:]
        high_out[64 + x * 8 : 72 + x * 8, :] = coef[120:]


def widened(low, own, high, x, base=0):
    at = pl.ds(base + x * 8, 8)
    return jnp.concatenate([low[at, :], own[x], high[at, :]], axis=0)


def pack_rows(v, c, low, high, first_out, last_out):
    for x in range(8):
        field = widened(low, v, high, x)
        coef = widened(low, c, high, x, 64)
        packed = coef[:24]
        for g in range(1, 6):
            packed = packed + pltpu.roll(coef[g * 24 : (g + 1) * 24], 16 * g, 1)
        row = jnp.concatenate([field, packed], axis=0)
        if x < 7:
            first_out[x] = row
        if x > 0:
            last_out[x - 1] = row


def place_slots(tile, cell, wave, amp, out, acc):
    acc[...] = jnp.zeros_like(acc)
    lane = iota((128, 256), 1)
    before = ((iota((128, 256), 0) < lane) | (lane >= 128)).astype(F32).astype(BF16)
    tile_line = iota((128, 128), 0)

    def chunk(turn, seen):
        at = pl.ds(pl.multiple_of(turn * 8, 8), 8)
        tiles = tile[at, :]
        code = cell[at, :] * 64 + wave[at, :]
        parts = list(split2(amp[at, :]))
        parts.append((code >> 8).astype(F32).astype(BF16))
        parts.append((code & 255).astype(F32).astype(BF16))
        hits = [
            (tile_line == tiles[j : j + 1, :]).astype(F32) for j in range(8)
        ]
        hits_b = [h.astype(BF16) for h in hits]
        ranks = dot(jnp.concatenate(hits_b, axis=0), before, ((1,), (0,)))
        slots = []
        for j in range(8):
            rank = ranks[j * 128 : (j + 1) * 128]
            slot = jnp.sum(hits[j] * (rank[:, :128] + seen), axis=0, keepdims=True)
            slots.append((tile_line == slot.astype(jnp.int32)).astype(F32).astype(BF16))
            seen = seen + rank[:, 128:]
        hit = jnp.concatenate(hits_b, axis=1)
        slot = jnp.concatenate(slots, axis=1)
        left = []
        for part in parts:
            wide = part.astype(F32)
            wide = jnp.concatenate([wide[j : j + 1, :] for j in range(8)], axis=1)
            left.append(hit * wide.astype(BF16))
        acc[...] += dot(jnp.concatenate(left, axis=0), slot, ((1,), (1,)))
        return seen

    lax.fori_loop(0, 8, chunk, jnp.zeros((128, 128), F32), unroll=8)
    out[:, 0, :] = acc[0:128] + acc[128:256]
    out[:, 1, :] = acc[256:384] * 256.0 + acc[384:512]


def add_currents(slots, waves, out, low_out, high_out, acc):
    acc[...] = jnp.zeros_like(acc)
    table = jnp.concatenate([p.astype(F32) for p in split3(waves[...])], axis=0).astype(BF16)
    wave_line = iota((64, 2048), 0).astype(F32).astype(BF16)
    cell_line = iota((256, 2048), 0).astype(F32).astype(BF16)
    one, zero = jnp.ones((), BF16), jnp.zeros((), BF16)

    def chunk(turn, carry):
        rows = [slots[turn * 16 + j] for j in range(16)]
        amp = jnp.concatenate([r[0:1, :] for r in rows], axis=1)
        code = jnp.concatenate([r[1:2, :] for r in rows], axis=1).astype(jnp.int32)
        hit = jnp.where(wave_line == (code & 63).astype(F32).astype(BF16), one, zero)
        picked = dot(table, hit, ((1,), (0,)))
        current = (picked[:64] + picked[64:128]) + picked[128:]
        current = (current * amp).astype(BF16)
        cell = code >> 6
        block = (cell >> 8).astype(F32).astype(BF16)
        right = [jnp.where(block == jnp.array(r, BF16), current, zero) for r in range(4)]
        left = jnp.where(cell_line == (cell & 255).astype(F32).astype(BF16), one, zero)
        acc[...] += dot(left, jnp.concatenate(right, axis=0), ((1,), (1,)))
        return carry

    lax.fori_loop(0, 8, chunk, 0, unroll=2)
    low_lanes = iota((256, 128), 1) < 64
    for r in range(4):
        half = acc[:, (r // 2) * 128 : (r // 2 + 1) * 128]
        if r % 2:
            half = pltpu.roll(half, 64, 1)
        half = jnp.where(low_lanes, half, 0.0)
        for b in range(2):
            x = 2 * r + b
            rows = half[b * 128 : (b + 1) * 128]
            out[x] = rows
            low_out[x * 8 : x * 8 + 8, :] = rows[:8]
            high_out[x * 8 : x * 8 + 8, :] = rows[120:]


def pack_injected(own, low, high, first_out, last_out):
    rows = [widened(low, own, high, x) for x in range(8)]
    for j in range(3):
        first_out[j] = rows[j] + pltpu.roll(rows[j + 3], 64, 1)
        last_out[j] = rows[j + 2] + pltpu.roll(rows[j + 5], 64, 1)


def apply_row(src, i, diag, wx, wy, wv):
    v = src[i]
    wyi, wvi = wy[i], wv[i]
    out = diag[i] * v - wx[i] * src[i + 1] - wx[i - 1] * src[i - 1]
    out = out - wyi * pltpu.roll(v, YE - 1, 0) - pltpu.roll(wyi * v, 1, 0)
    return out - wvi * pltpu.roll(v, 96, 1) - pltpu.roll(wvi * v, 32, 1)


def power(src, dst, first, last, weights):
    def row(i, carry):
        dst[i] = apply_row(src, i, *weights)
        return carry

    lax.fori_loop(first, last + 1, row, 0, unroll=2)


def moments(fields, out, first):
    own = [f[first : first + 8, 8:136, :].reshape(1024, 128) for f in fields]
    lane = iota((32, 128), 1)
    blocks = [jnp.zeros((32, 128), F32), jnp.zeros((32, 128), F32)]
    for k in range(3):
        pair = jnp.concatenate([own[k], own[k + 1]], axis=1)
        product = dot_split(own[k], pair, ((0,), (0,)))
        for b in range(2):
            n = 2 * k + b
            place = 32 * (n % 4)
            total = jnp.zeros((32, 128), F32)
            for l in range(4):
                piece = product[l * 32 : (l + 1) * 32, b * 128 : (b + 1) * 128]
                turn = (place - 32 * l) % 128
                total = total + (pltpu.roll(piece, turn, 1) if turn else piece)
            inside = (lane >= place) & (lane < place + 32)
            blocks[n // 4] = blocks[n // 4] + jnp.where(inside, total, 0.0)
    out[0:32, :] = blocks[0]
    out[32:64, :] = blocks[1]


def coefficients(gram):
    lane = iota((32, 128), 1)

    def moment(k, place):
        block = gram[(k // 4) * 32 : (k // 4) * 32 + 32, :]
        turn = (place - 32 * (k % 4)) % 128
        block = pltpu.roll(block, turn, 1) if turn else block
        return jnp.where((lane >= place) & (lane < place + 32), block, 0.0)

    tiles = []
    for i in range(3):
        block = moment(i, 96)
        for j in range(3):
            block = block + SCALE * moment(i + j + 1, 32 * j) + SHIFT * moment(i + j, 32 * j)
        tiles += [block[r * 8 : r * 8 + 8] for r in range(4)]
    sub = iota((8, 128), 0)
    for t in range(12):
        rows = tiles[t]
        cols = [jnp.broadcast_to(rows[:, t * 8 + j : t * 8 + j + 1], (8, 128)) for j in range(8)]
        for j in range(8):
            inverse = 1.0 / cols[j][j : j + 1, :]
            pivot = rows[j : j + 1, :] * inverse
            rows = jnp.where(sub == j, pivot, rows - cols[j] * pivot)
            for n in range(j + 1, 8):
                top = cols[n][j : j + 1, :] * inverse
                cols[n] = jnp.where(sub == j, top, cols[n] - cols[j] * top)
        for i in range(12):
            block = tiles[i]
            for j in range(8):
                if i != t:
                    block = block - tiles[i][:, t * 8 + j : t * 8 + j + 1] * rows[j : j + 1, :]
            tiles[i] = block
        tiles[t] = rows
    lane = iota((32, 128), 1)
    outs = []
    for i in range(3):
        y = jnp.concatenate(tiles[i * 4 : i * 4 + 4], axis=0)
        y = jnp.where(lane >= 96, y, 0.0)
        y = y + pltpu.roll(y, 32, 1) + pltpu.roll(y, 64, 1) + pltpu.roll(y, 96, 1)
        outs.append(
            jnp.concatenate([jnp.where(lane // 32 == l, y, 0.0) for l in range(4)], axis=0)
        )
    return outs


def combination(gram):
    y0, y1, y2 = coefficients(gram)
    step = jnp.concatenate([y0, y1, y2, jnp.zeros_like(y0)], axis=0)
    less = jnp.concatenate(
        [
            -SHIFT * y0,
            -SCALE * y0 - SHIFT * y1,
            -SCALE * y1 - SHIFT * y2,
            -SCALE * y2,
        ],
        axis=0,
    )
    return jnp.concatenate([step, less], axis=1)


def grid_weights(
    v, c, low, high, x_low, x_high, diag, wx, wy, wv, cap, free, ext,
):
    lane = iota((YE, 128), 1)
    n = iota((128, 512), 1)
    q = iota((128, 512), 0)
    spread = ((q % 16 == (n // 128) * 4 + (n % 128) // 32) & (q < 48)).astype(F32).astype(BF16)

    def expand(i, coef):
        hi, mid, lo = [p.astype(F32) for p in split3(coef)]
        parts = hi + pltpu.roll(mid, 16, 1) + pltpu.roll(lo, 32, 1)
        wide = dot(parts.astype(BF16), spread, ((1,), (0,)))
        cap[i] = wide[:, :128]
        wx[i] = wide[:, 128:256]
        wy[i] = wide[:, 256:384]
        wv[i] = jnp.where(lane < 96, wide[:, 384:], 0.0)
        diag[i] = wide[:, :128] + wide[:, 384:]

    def halo_row(j, ref, base):
        ext[base + j] = ref[j, :YE, :]
        packed = ref[j, YE:, :]
        groups = [packed] + [pltpu.roll(packed, 128 - 16 * g, 1) for g in range(1, 6)]
        coef = jnp.concatenate(groups, axis=0)
        expand(base + j, jnp.where(lane < 16, coef, 0.0))

    def own_row(x, carry):
        at = pl.ds(pl.multiple_of(x * 8, 8), 8)
        at_c = pl.ds(pl.multiple_of(64 + x * 8, 8), 8)
        ext[7 + x] = jnp.concatenate([low[at, :], v[x], high[at, :]], axis=0)
        expand(7 + x, jnp.concatenate([low[at_c, :], c[x], high[at_c, :]], axis=0))
        return carry

    def halo_rows(j, carry):
        halo_row(j, x_low, 0)
        halo_row(j, x_high, 15)
        return carry

    lax.fori_loop(0, 8, own_row, 0, unroll=2)
    lax.fori_loop(0, 7, halo_rows, 0)

    def diagonal(i, carry):
        total = diag[i] + wx[i] + wx[i - 1] + wy[i] + pltpu.roll(wy[i], 1, 0)
        total = total + pltpu.roll(wv[i], 32, 1)
        diag[i] = (total - SHIFT) * (1.0 / SCALE)
        return carry

    lax.fori_loop(1, 21, diagonal, 0, unroll=2)

    def edges(i, carry):
        wx[i] = jnp.where(cap[i + 1] > 0, wx[i] * (1.0 / SCALE), 0.0)
        wy[i] = jnp.where(pltpu.roll(cap[i], YE - 1, 0) > 0, wy[i] * (1.0 / SCALE), 0.0)
        wv[i] = wv[i] * (1.0 / SCALE)
        return carry

    lax.fori_loop(0, 21, edges, 0, unroll=3)
    weights = (diag, wx, wy, wv)


    def start(i, carry):
        e = ext[i]
        free[i] = (cap[i] - SHIFT) * e - SCALE * apply_row(ext, i, *weights)
        return carry

    lax.fori_loop(1, 21, start, 0, unroll=2)


def first_basis(
    diag, wx, wy, wv, free, inj, i_low, i_high, ix_low, ix_high,
    change, v0, v1, v2, v3, gram,
):
    lane = iota((YE, 128), 1)
    weights = (diag, wx, wy, wv)

    def start(i, both):
        now = jnp.where(lane < 32, both, 0.0)
        then = jnp.where(lane < 32, pltpu.roll(both, 96, 1), 0.0)
        change[i] = now - then
        v0[i] = free[i] - now

    def own_start(x, carry):
        at = pl.ds(pl.multiple_of(x * 8, 8), 8)
        start(7 + x, jnp.concatenate([i_low[at, :], inj[x], i_high[at, :]], axis=0))
        return carry

    def halo_start(j, carry):
        for ref, base in ((ix_low, 1), (ix_high, 15)):
            both = ref[j]
            start(base + j, both)
            start(base + 3 + j, pltpu.roll(both, 64, 1))
        return carry

    lax.fori_loop(0, 8, own_start, 0)
    lax.fori_loop(0, 3, halo_start, 0)
    power(v0, v1, 2, 19, weights)
    power(v1, v2, 3, 18, weights)
    power(v2, v3, 4, 17, weights)
    moments((v0, v1, v2, v3), gram, 7)


def second_basis(
    gram, diag, wx, wy, wv, cap, change, v0, v1, v2, v3, v,
    w0, w1, w2, w3, volts, gram_out, b0, b1, b2, b3, step,
):
    weights = (diag, wx, wy, wv)
    mix = combination(gram)

    def row(i, carry):
        fields = jnp.concatenate([v0[i], v1[i], v2[i], v3[i]], axis=1)
        both = dot_split(fields, mix, ((1,), (0,)))
        moved = both[:, :128]
        step[i] = moved
        b0[i] = v0[i] + both[:, 128:] + cap[i] * moved + change[i]
        return carry

    lax.fori_loop(4, 18, row, 0, unroll=2)
    power(b0, b1, 5, 16, weights)
    power(b1, b2, 6, 15, weights)
    power(b2, b3, 7, 14, weights)
    moments((b0, b1, b2, b3), gram_out, 7)
    for x in range(8):
        volts[x] = v[x] + step[7 + x, 8:136, :]
        for src, dst in ((b0, w0), (b1, w1), (b2, w2), (b3, w3)):
            dst[x] = src[7 + x, 8:136, :]


def finish(gram, w0, w1, w2, w3, volts, volts_out, residual_out):
    mix = combination(gram)
    for x in range(8):
        fields = jnp.concatenate([w0[x], w1[x], w2[x], w3[x]], axis=1)
        both = dot_split(fields, mix, ((1,), (0,)))
        for value, out in (
            (volts[x] + both[:, :128], volts_out),
            (w0[x] + both[:, 128:], residual_out),
        ):
            value = value.T
            for l in range(4):
                out[pl.ds(l * 8 + x, 32, stride=32), :] = value[l * 32 : (l + 1) * 32]


def neighbours(to_low, to_high, axis):
    size = lax.axis_size(axis)
    up = [(i, i + 1) for i in range(size - 1)]
    from_low = lax.ppermute(to_high, axis, up)
    return from_low, lax.ppermute(to_low, axis, [(b, a) for a, b in up])


def everywhere(x):
    x = x + lax.ppermute(x, "gy_1", [(0, 1), (1, 0)])
    for axis in ("gy_0", "gx_1", "gx_0"):
        one, two, three = [
            lax.ppermute(x, axis, [(i, i ^ k) for i in range(4)]) for k in (1, 2, 3)
        ]
        x = (x + one) + (two + three)
    return x


def exchange(slots):
    return lax.all_to_all(slots, GX_GY, split_axis=0, concat_axis=0, tiled=True)


def body(volts, cap, cond_x, cond_y, via, waveforms, placement, cells, wave_ids, amps):
    vmem = pltpu.VMEM
    coefs = [a.reshape(32, 128) for a in (cap, cond_x, cond_y, via)]
    lists = [a.reshape(64, 128) for a in (placement, cells, wave_ids, amps)]
    v, c, y_low, y_high, *lists = call(
        to_lanes,
        [(8, 128, 128), (8, 128, 128), (128, 128), (128, 128)]
        + [jax.ShapeDtypeStruct(a.shape, a.dtype) for a in lists],
        [volts.reshape(1024, 128)] + coefs + lists,
        [vmem((1024, 128), F32), vmem((128, 128), F32), pltpu.SemaphoreType.DMA((9,))],
        in_specs=[pl.BlockSpec(memory_space=pl.ANY)] * 9,
    )
    y_low, y_high = neighbours(y_low, y_high, GY)
    (slots,) = call(place_slots, [(128, 2, 128)], lists, [vmem((512, 128), F32)])
    y_low, y_high, slots = lax.optimization_barrier((y_low, y_high, slots))
    x_low, x_high = call(pack_rows, [(7, 168, 128)] * 2, [v, c, y_low, y_high])
    x_low, x_high = neighbours(x_low, x_high, GX)
    slots = exchange(slots)
    inj, i_low, i_high = call(
        add_currents,
        [(8, 128, 128), (64, 128), (64, 128)],
        [slots, waveforms],
        [vmem((256, 256), F32)],
    )
    i_low, i_high = neighbours(i_low, i_high, GY)
    ix_low, ix_high = call(pack_injected, [(3, YE, 128)] * 2, [inj, i_low, i_high])
    ix_low, ix_high = neighbours(ix_low, ix_high, GX)
    wide = (XE, YE, 128)
    diag, wx, wy, wv, cap, free = call(
        grid_weights, [wide] * 6, [v, c, y_low, y_high, x_low, x_high], [vmem(wide, F32)]
    )
    *kept, gram = call(
        first_basis,
        [wide] * 5 + [(64, 128)],
        [diag, wx, wy, wv, free, inj, i_low, i_high, ix_low, ix_high],
    )
    own = (8, 128, 128)
    *basis, gram = call(
        second_basis,
        [own] * 5 + [(64, 128)],
        [everywhere(gram), diag, wx, wy, wv, cap] + kept + [v],
        [vmem(wide, F32)] * 5,
    )
    outs = call(finish, [(1024, 128)] * 2, [everywhere(gram)] + basis)
    return tuple(o.reshape(volts.shape) for o in outs)


def solution(mesh):
    finer = Mesh(mesh.devices.reshape(4, 4, 4, 2), ("gx_0", "gx_1", "gy_0", "gy_1"))
    in_specs = (
        P(None, None, GX, GY),
        P(None, GX, GY),
        P(None, GX, GY),
        P(None, GX, GY),
        P(None, GX, GY),
        P(),
        P(GX_GY, None),
        P(GX_GY),
        P(GX_GY),
        P(GX_GY),
    )
    out_specs = (P(None, None, GX, GY), P(None, None, GX, GY))
    return jax.shard_map(body, mesh=finer, in_specs=in_specs, out_specs=out_specs, check_vma=False)
```

```python
import jax
import jax.numpy as jnp
from jax import lax
from jax.experimental import pallas as pl
from jax.experimental.pallas import tpu as pltpu
from jax.sharding import Mesh
from jax.sharding import PartitionSpec as P

GX = ("gx_0", "gx_1")
GY = ("gy_0", "gy_1")
GX_GY = GX + GY
F32 = jnp.float32
BF16 = jnp.bfloat16
HIGHEST = lax.Precision.HIGHEST
SHIFT = 7.0
SCALE = 7.0
XE = 22
YE = 144


def iota(shape, dim):
    return lax.broadcasted_iota(jnp.int32, shape, dim)


def dot(a, b, dims, precision=None):
    return lax.dot_general(
        a, b, (dims, ((), ())), precision=precision, preferred_element_type=F32
    )


def split2(x):
    hi = x.astype(BF16)
    return hi, (x - hi.astype(F32)).astype(BF16)


def dot_split(a, b, dims):
    a_hi, a_lo = split2(a)
    b_hi, b_lo = split2(b)
    return dot(a_hi, b_hi, dims) + dot(a_hi, b_lo, dims) + dot(a_lo, b_hi, dims)


def split3(x):
    hi = x.astype(BF16)
    rest = x - hi.astype(F32)
    mid = rest.astype(BF16)
    return hi, mid, (rest - mid.astype(F32)).astype(BF16)


def call(kernel, outs, args, scratch=(), limit=14, in_specs=None):
    outs = [o if isinstance(o, jax.ShapeDtypeStruct) else jax.ShapeDtypeStruct(o, F32) for o in outs]
    specs = {} if in_specs is None else {"in_specs": in_specs}
    return pl.pallas_call(
        kernel,
        out_shape=tuple(outs),
        scratch_shapes=list(scratch),
        **specs,
        compiler_params=pltpu.CompilerParams(vmem_limit_bytes=limit << 20),
        name=kernel.__name__,
    )(*args)


def to_lanes(volts, stack, v_out, c_out, low_out, high_out):
    for x in range(8):
        rows = [volts[pl.ds(l * 8 + x, 32, stride=32), :] for l in range(4)]
        field = jnp.concatenate(rows, axis=0).T
        v_out[x] = field
        coef = stack[pl.ds(x, 16, stride=8), :]
        coef = jnp.concatenate([coef, jnp.zeros((112, 128), F32)], axis=0).T
        c_out[x] = coef
        low_out[x * 8 : x * 8 + 8, :] = field[:8]
        low_out[64 + x * 8 : 72 + x * 8, :] = coef[:8]
        high_out[x * 8 : x * 8 + 8, :] = field[120:]
        high_out[64 + x * 8 : 72 + x * 8, :] = coef[120:]


def widened(low, own, high, x, base=0):
    at = pl.ds(base + x * 8, 8)
    return jnp.concatenate([low[at, :], own[x], high[at, :]], axis=0)


def pack_rows(v, c, low, high, first_out, last_out):
    for x in range(8):
        field = widened(low, v, high, x)
        coef = widened(low, c, high, x, 64)
        packed = coef[:24]
        for g in range(1, 6):
            packed = packed + pltpu.roll(coef[g * 24 : (g + 1) * 24], 16 * g, 1)
        row = jnp.concatenate([field, packed], axis=0)
        if x < 7:
            first_out[x] = row
        if x > 0:
            last_out[x - 1] = row


def place_slots(codes, amps, out, acc):
    acc[...] = jnp.zeros_like(acc)
    lane = iota((128, 256), 1)
    before = ((iota((128, 256), 0) < lane) | (lane >= 128)).astype(F32).astype(BF16)
    tile_line = iota((128, 128), 0)

    def chunk(turn, seen):
        at = pl.ds(pl.multiple_of(turn * 8, 8), 8)
        code = codes[at, :]
        tiles = code >> 16
        parts = list(split2(amps[at, :]))
        parts.append(((code >> 8) & 255).astype(F32).astype(BF16))
        parts.append((code & 255).astype(F32).astype(BF16))
        hits = [
            (tile_line == tiles[j : j + 1, :]).astype(F32) for j in range(8)
        ]
        hits_b = [h.astype(BF16) for h in hits]
        ranks = dot(jnp.concatenate(hits_b, axis=0), before, ((1,), (0,)))
        slots = []
        for j in range(8):
            rank = ranks[j * 128 : (j + 1) * 128]
            slot = jnp.sum(hits[j] * (rank[:, :128] + seen), axis=0, keepdims=True)
            slots.append((tile_line == slot.astype(jnp.int32)).astype(F32).astype(BF16))
            seen = seen + rank[:, 128:]
        hit = jnp.concatenate(hits_b, axis=1)
        slot = jnp.concatenate(slots, axis=1)
        left = []
        for part in parts:
            wide = part.astype(F32)
            wide = jnp.concatenate([wide[j : j + 1, :] for j in range(8)], axis=1)
            left.append(hit * wide.astype(BF16))
        acc[...] += dot(jnp.concatenate(left, axis=0), slot, ((1,), (1,)))
        return seen

    lax.fori_loop(0, 8, chunk, jnp.zeros((128, 128), F32), unroll=8)
    out[:, 0, :] = acc[0:128] + acc[128:256]
    out[:, 1, :] = acc[256:384] * 256.0 + acc[384:512]


def add_currents(slots, waves, out, low_out, high_out, acc):
    acc[...] = jnp.zeros_like(acc)
    table = jnp.concatenate([p.astype(F32) for p in split3(waves[...])], axis=0).astype(BF16)
    wave_line = iota((64, 2048), 0).astype(F32).astype(BF16)
    cell_line = iota((256, 2048), 0).astype(F32).astype(BF16)
    one, zero = jnp.ones((), BF16), jnp.zeros((), BF16)

    def chunk(turn, carry):
        rows = [slots[turn * 16 + j] for j in range(16)]
        amp = jnp.concatenate([r[0:1, :] for r in rows], axis=1)
        code = jnp.concatenate([r[1:2, :] for r in rows], axis=1).astype(jnp.int32)
        hit = jnp.where(wave_line == (code & 63).astype(F32).astype(BF16), one, zero)
        picked = dot(table, hit, ((1,), (0,)))
        current = (picked[:64] + picked[64:128]) + picked[128:]
        current = (current * amp).astype(BF16)
        cell = code >> 6
        block = (cell >> 8).astype(F32).astype(BF16)
        right = [jnp.where(block == jnp.array(r, BF16), current, zero) for r in range(4)]
        left = jnp.where(cell_line == (cell & 255).astype(F32).astype(BF16), one, zero)
        acc[...] += dot(left, jnp.concatenate(right, axis=0), ((1,), (1,)))
        return carry

    lax.fori_loop(0, 8, chunk, 0, unroll=2)
    low_lanes = iota((256, 128), 1) < 64
    for r in range(4):
        half = acc[:, (r // 2) * 128 : (r // 2 + 1) * 128]
        if r % 2:
            half = pltpu.roll(half, 64, 1)
        half = jnp.where(low_lanes, half, 0.0)
        for b in range(2):
            x = 2 * r + b
            rows = half[b * 128 : (b + 1) * 128]
            out[x] = rows
            low_out[x * 8 : x * 8 + 8, :] = rows[:8]
            high_out[x * 8 : x * 8 + 8, :] = rows[120:]


def pack_injected(own, low, high, first_out, last_out):
    rows = [widened(low, own, high, x) for x in range(8)]
    for j in range(3):
        first_out[j] = rows[j] + pltpu.roll(rows[j + 3], 64, 1)
        last_out[j] = rows[j + 2] + pltpu.roll(rows[j + 5], 64, 1)


def apply_row(src, i, diag, wx, wy, wv):
    v = src[i]
    wyi, wvi = wy[i], wv[i]
    out = diag[i] * v - wx[i] * src[i + 1] - wx[i - 1] * src[i - 1]
    out = out - wyi * pltpu.roll(v, YE - 1, 0) - pltpu.roll(wyi * v, 1, 0)
    return out - wvi * pltpu.roll(v, 96, 1) - pltpu.roll(wvi * v, 32, 1)


def power(src, dst, first, last, weights):
    def row(i, carry):
        dst[i] = apply_row(src, i, *weights)
        return carry

    lax.fori_loop(first, last + 1, row, 0, unroll=4)


def moments(fields, out, first):
    own = [f[first : first + 8, 8:136, :].reshape(1024, 128) for f in fields]
    lane, row = iota((32, 128), 1), iota((32, 128), 0)
    packed = jnp.zeros((32, 128), F32)
    for k in range(3):
        pair = jnp.concatenate([own[k], own[k + 1]], axis=1)
        product = dot_split(own[k], pair, ((0,), (0,)))
        column = lane - 32 * k
        totals = []
        for b in range(2):
            total = jnp.zeros((32, 128), F32)
            for l in range(4):
                piece = product[l * 32 : (l + 1) * 32, b * 128 : (b + 1) * 128]
                turn = (32 * (k - l)) % 128
                total = total + (pltpu.roll(piece, turn, 1) if turn else piece)
            totals.append(total)
        even, odd = totals
        inside = (column >= 0) & (column < 32)
        packed = packed + jnp.where(inside, jnp.where(column > row, even, odd), 0.0)
        diagonal = jnp.sum(jnp.where(column == row, even, 0.0), axis=1, keepdims=True)
        packed = packed + jnp.where(lane == 96 + k, diagonal, 0.0)
    out[...] = packed


def coefficients(gram):
    lane, row = iota((32, 128), 1), iota((32, 128), 0)
    packed = gram[...]
    flipped = jnp.concatenate([packed, jnp.zeros((96, 128), F32)], axis=0).T
    bases = []
    for k in range(3):
        direct = pltpu.roll(packed, 128 - 32 * k, 1) if k else packed
        mirror = flipped[k * 32 : (k + 1) * 32, :]
        even = jnp.where(lane > row, direct, mirror)
        even = jnp.where(lane == row, packed[:, 96 + k : 97 + k], even)
        bases.append(jnp.where(lane < 32, even, 0.0))
        odd = jnp.where(lane > row, mirror, direct)
        bases.append(jnp.where(lane < 32, odd, 0.0))

    def moment(k, place):
        return pltpu.roll(bases[k], place, 1) if place else bases[k]

    tiles = []
    for i in range(3):
        block = moment(i, 96)
        for j in range(3):
            block = block + SCALE * moment(i + j + 1, 32 * j) + SHIFT * moment(i + j, 32 * j)
        tiles += [block[r * 8 : r * 8 + 8] for r in range(4)]
    sub = iota((8, 128), 0)
    for t in range(12):
        rows = tiles[t]
        cols = [jnp.broadcast_to(rows[:, t * 8 + j : t * 8 + j + 1], (8, 128)) for j in range(8)]
        for j in range(8):
            inverse = 1.0 / cols[j][j : j + 1, :]
            pivot = rows[j : j + 1, :] * inverse
            rows = jnp.where(sub == j, pivot, rows - cols[j] * pivot)
            for n in range(j + 1, 8):
                top = cols[n][j : j + 1, :] * inverse
                cols[n] = jnp.where(sub == j, top, cols[n] - cols[j] * top)
        for i in range(12):
            block = tiles[i]
            for j in range(8):
                if i != t:
                    block = block - tiles[i][:, t * 8 + j : t * 8 + j + 1] * rows[j : j + 1, :]
            tiles[i] = block
        tiles[t] = rows
    lane = iota((32, 128), 1)
    outs = []
    for i in range(3):
        y = jnp.concatenate(tiles[i * 4 : i * 4 + 4], axis=0)
        y = jnp.where(lane >= 96, y, 0.0)
        y = y + pltpu.roll(y, 32, 1) + pltpu.roll(y, 64, 1) + pltpu.roll(y, 96, 1)
        outs.append(
            jnp.concatenate([jnp.where(lane // 32 == l, y, 0.0) for l in range(4)], axis=0)
        )
    return outs


def combination(gram):
    y0, y1, y2 = coefficients(gram)
    step = jnp.concatenate([y0, y1, y2, jnp.zeros_like(y0)], axis=0)
    less = jnp.concatenate(
        [
            -SHIFT * y0,
            -SCALE * y0 - SHIFT * y1,
            -SCALE * y1 - SHIFT * y2,
            -SCALE * y2,
        ],
        axis=0,
    )
    return jnp.concatenate([step, less], axis=1)


def grid_weights(
    v, c, low, high, x_low, x_high, diag, wx, wy, wv, cap, free, ext,
):
    lane = iota((YE, 128), 1)
    n = iota((128, 512), 1)
    q = iota((128, 512), 0)
    spread = ((q % 16 == (n // 128) * 4 + (n % 128) // 32) & (q < 48)).astype(F32).astype(BF16)

    def expand(i, coef):
        hi, mid, lo = [p.astype(F32) for p in split3(coef)]
        parts = hi + pltpu.roll(mid, 16, 1) + pltpu.roll(lo, 32, 1)
        wide = dot(parts.astype(BF16), spread, ((1,), (0,)))
        cap[i] = wide[:, :128]
        wx[i] = wide[:, 128:256]
        wy[i] = wide[:, 256:384]
        wv[i] = jnp.where(lane < 96, wide[:, 384:], 0.0)
        diag[i] = wide[:, :128] + wide[:, 384:]

    def halo_row(j, ref, base):
        ext[base + j] = ref[j, :YE, :]
        packed = ref[j, YE:, :]
        groups = [packed] + [pltpu.roll(packed, 128 - 16 * g, 1) for g in range(1, 6)]
        coef = jnp.concatenate(groups, axis=0)
        expand(base + j, jnp.where(lane < 16, coef, 0.0))

    def own_row(x, carry):
        at = pl.ds(pl.multiple_of(x * 8, 8), 8)
        at_c = pl.ds(pl.multiple_of(64 + x * 8, 8), 8)
        ext[7 + x] = jnp.concatenate([low[at, :], v[x], high[at, :]], axis=0)
        expand(7 + x, jnp.concatenate([low[at_c, :], c[x], high[at_c, :]], axis=0))
        return carry

    def halo_rows(j, carry):
        halo_row(j, x_low, 0)
        halo_row(j, x_high, 15)
        return carry

    lax.fori_loop(0, 8, own_row, 0, unroll=2)
    lax.fori_loop(0, 7, halo_rows, 0)

    def diagonal(i, carry):
        total = diag[i] + wx[i] + wx[i - 1] + wy[i] + pltpu.roll(wy[i], 1, 0)
        total = total + pltpu.roll(wv[i], 32, 1)
        diag[i] = (total - SHIFT) * (1.0 / SCALE)
        return carry

    lax.fori_loop(1, 21, diagonal, 0, unroll=2)

    def edges(i, carry):
        wx[i] = jnp.where(cap[i + 1] > 0, wx[i] * (1.0 / SCALE), 0.0)
        wy[i] = jnp.where(pltpu.roll(cap[i], YE - 1, 0) > 0, wy[i] * (1.0 / SCALE), 0.0)
        wv[i] = wv[i] * (1.0 / SCALE)
        return carry

    lax.fori_loop(0, 21, edges, 0, unroll=3)
    weights = (diag, wx, wy, wv)


    def start(i, carry):
        e = ext[i]
        free[i] = (cap[i] - SHIFT) * e - SCALE * apply_row(ext, i, *weights)
        return carry

    lax.fori_loop(1, 21, start, 0, unroll=2)


def first_basis(
    diag, wx, wy, wv, free, inj, i_low, i_high, ix_low, ix_high,
    change, v0, v1, v2, v3, gram,
):
    lane = iota((YE, 128), 1)
    weights = (diag, wx, wy, wv)

    def start(i, both):
        now = jnp.where(lane < 32, both, 0.0)
        then = jnp.where(lane < 32, pltpu.roll(both, 96, 1), 0.0)
        change[i] = now - then
        v0[i] = free[i] - now

    def own_start(x, carry):
        at = pl.ds(pl.multiple_of(x * 8, 8), 8)
        start(7 + x, jnp.concatenate([i_low[at, :], inj[x], i_high[at, :]], axis=0))
        return carry

    def halo_start(j, carry):
        for ref, base in ((ix_low, 1), (ix_high, 15)):
            both = ref[j]
            start(base + j, both)
            start(base + 3 + j, pltpu.roll(both, 64, 1))
        return carry

    lax.fori_loop(0, 8, own_start, 0)
    lax.fori_loop(0, 3, halo_start, 0)
    power(v0, v1, 2, 19, weights)
    power(v1, v2, 3, 18, weights)
    power(v2, v3, 4, 17, weights)
    moments((v0, v1, v2, v3), gram, 7)


def second_basis(
    gram, diag, wx, wy, wv, cap, change, v0, v1, v2, v3, v,
    w0, w1, w2, w3, volts, gram_out, b0, b1, b2, b3, step,
):
    weights = (diag, wx, wy, wv)
    mix = combination(gram)

    def row(i, carry):
        fields = jnp.concatenate([v0[i], v1[i], v2[i], v3[i]], axis=1)
        both = dot_split(fields, mix, ((1,), (0,)))
        moved = both[:, :128]
        step[i] = moved
        b0[i] = v0[i] + both[:, 128:] + cap[i] * moved + change[i]
        return carry

    lax.fori_loop(4, 18, row, 0, unroll=2)
    power(b0, b1, 5, 16, weights)
    power(b1, b2, 6, 15, weights)
    power(b2, b3, 7, 14, weights)
    moments((b0, b1, b2, b3), gram_out, 7)
    for x in range(8):
        volts[x] = v[x] + step[7 + x, 8:136, :]
        for src, dst in ((b0, w0), (b1, w1), (b2, w2), (b3, w3)):
            dst[x] = src[7 + x, 8:136, :]


def finish(gram, w0, w1, w2, w3, volts, volts_out, residual_out):
    mix = combination(gram)
    for x in range(8):
        fields = jnp.concatenate([w0[x], w1[x], w2[x], w3[x]], axis=1)
        both = dot_split(fields, mix, ((1,), (0,)))
        for value, out in (
            (volts[x] + both[:, :128], volts_out),
            (w0[x] + both[:, 128:], residual_out),
        ):
            value = value.T
            for l in range(4):
                out[pl.ds(l * 8 + x, 32, stride=32), :] = value[l * 32 : (l + 1) * 32]


def neighbours(to_low, to_high, axis):
    size = lax.axis_size(axis)
    up = [(i, i + 1) for i in range(size - 1)]
    from_low = lax.ppermute(to_high, axis, up)
    return from_low, lax.ppermute(to_low, axis, [(b, a) for a, b in up])


def everywhere(x):
    x = x + lax.ppermute(x, "gy_1", [(0, 1), (1, 0)])
    for axis in ("gy_0", "gx_1", "gx_0"):
        one, two, three = [
            lax.ppermute(x, axis, [(i, i ^ k) for i in range(4)]) for k in (1, 2, 3)
        ]
        x = (x + one) + (two + three)
    return x


def exchange(slots):
    return lax.all_to_all(slots, GX_GY, split_axis=0, concat_axis=0, tiled=True)


def body(volts, cap, cond_x, cond_y, via, waveforms, placement, cells, wave_ids, amps):
    vmem = pltpu.VMEM
    coefs = jnp.concatenate([a.reshape(32, 128) for a in (cap, cond_x, cond_y, via)], axis=0)
    v, c, y_low, y_high = call(
        to_lanes,
        [(8, 128, 128), (8, 128, 128), (128, 128), (128, 128)],
        [volts.reshape(1024, 128), coefs],
    )
    y_low, y_high = neighbours(y_low, y_high, GY)
    codes = (placement.reshape(-1) * 65536 + cells * 64 + wave_ids).reshape(64, 128)
    (slots,) = call(
        place_slots, [(128, 2, 128)], [codes, amps.reshape(64, 128)], [vmem((512, 128), F32)]
    )
    y_low, y_high, slots = lax.optimization_barrier((y_low, y_high, slots))
    x_low, x_high = call(pack_rows, [(7, 168, 128)] * 2, [v, c, y_low, y_high])
    x_low, x_high = neighbours(x_low, x_high, GX)
    slots = exchange(slots)
    inj, i_low, i_high = call(
        add_currents,
        [(8, 128, 128), (64, 128), (64, 128)],
        [slots, waveforms],
        [vmem((256, 256), F32)],
    )
    i_low, i_high = neighbours(i_low, i_high, GY)
    ix_low, ix_high = call(pack_injected, [(3, YE, 128)] * 2, [inj, i_low, i_high])
    ix_low, ix_high = neighbours(ix_low, ix_high, GX)
    wide = (XE, YE, 128)
    diag, wx, wy, wv, cap, free = call(
        grid_weights, [wide] * 6, [v, c, y_low, y_high, x_low, x_high], [vmem(wide, F32)]
    )
    *kept, gram = call(
        first_basis,
        [wide] * 5 + [(32, 128)],
        [diag, wx, wy, wv, free, inj, i_low, i_high, ix_low, ix_high],
    )
    own = (8, 128, 128)
    *basis, gram = call(
        second_basis,
        [own] * 5 + [(32, 128)],
        [everywhere(gram), diag, wx, wy, wv, cap] + kept + [v],
        [vmem(wide, F32)] * 5,
    )
    outs = call(finish, [(1024, 128)] * 2, [everywhere(gram)] + basis)
    return tuple(o.reshape(volts.shape) for o in outs)


def solution(mesh):
    finer = Mesh(mesh.devices.reshape(4, 4, 4, 2), ("gx_0", "gx_1", "gy_0", "gy_1"))
    in_specs = (
        P(None, None, GX, GY),
        P(None, GX, GY),
        P(None, GX, GY),
        P(None, GX, GY),
        P(None, GX, GY),
        P(),
        P(GX_GY, None),
        P(GX_GY),
        P(GX_GY),
        P(GX_GY),
    )
    out_specs = (P(None, None, GX, GY), P(None, None, GX, GY))
    return jax.shard_map(body, mesh=finer, in_specs=in_specs, out_specs=out_specs, check_vma=False)
```

```python
import jax
import jax.numpy as jnp
from jax import lax
from jax.experimental import pallas as pl
from jax.experimental.pallas import tpu as pltpu
from jax.sharding import Mesh
from jax.sharding import PartitionSpec as P

GX = ("gx_0", "gx_1")
GY = ("gy_0", "gy_1")
GX_GY = GX + GY
F32 = jnp.float32
BF16 = jnp.bfloat16
HIGHEST = lax.Precision.HIGHEST
SHIFT = 7.0
SCALE = 7.0
XE = 22
YE = 144


def iota(shape, dim):
    return lax.broadcasted_iota(jnp.int32, shape, dim)


def dot(a, b, dims, precision=None):
    return lax.dot_general(
        a, b, (dims, ((), ())), precision=precision, preferred_element_type=F32
    )


def split2(x):
    hi = x.astype(BF16)
    return hi, (x - hi.astype(F32)).astype(BF16)


def dot_split(a, b, dims):
    a_hi, a_lo = split2(a)
    b_hi, b_lo = split2(b)
    return dot(a_hi, b_hi, dims) + dot(a_hi, b_lo, dims) + dot(a_lo, b_hi, dims)


def split3(x):
    hi = x.astype(BF16)
    rest = x - hi.astype(F32)
    mid = rest.astype(BF16)
    return hi, mid, (rest - mid.astype(F32)).astype(BF16)


def call(kernel, outs, args, scratch=(), limit=14, in_specs=None):
    outs = [o if isinstance(o, jax.ShapeDtypeStruct) else jax.ShapeDtypeStruct(o, F32) for o in outs]
    specs = {} if in_specs is None else {"in_specs": in_specs}
    return pl.pallas_call(
        kernel,
        out_shape=tuple(outs),
        scratch_shapes=list(scratch),
        **specs,
        compiler_params=pltpu.CompilerParams(vmem_limit_bytes=limit << 20),
        name=kernel.__name__,
    )(*args)


def to_lanes(volts, stack, v_out, c_out, low_out, high_out):
    for x in range(8):
        field = load_rows(volts, x).T
        v_out[x] = field
        coef = stack[pl.ds(x, 16, stride=8), :]
        coef = jnp.concatenate([coef, jnp.zeros((112, 128), F32)], axis=0).T
        c_out[x] = coef
        low_out[x * 8 : x * 8 + 8, :] = field[:8]
        low_out[64 + x * 8 : 72 + x * 8, :] = coef[:8]
        high_out[x * 8 : x * 8 + 8, :] = field[120:]
        high_out[64 + x * 8 : 72 + x * 8, :] = coef[120:]


def inside(axis):
    me = lax.axis_index(axis)
    return (me > 0).astype(F32), (me < lax.axis_size(axis) - 1).astype(F32)


def widened(low, own, high, x, base=0):
    at = pl.ds(pl.multiple_of(base + x * 8, 8), 8)
    low_in, high_in = inside(GY)
    return jnp.concatenate([low[at, :] * low_in, own[x], high[at, :] * high_in], axis=0)


def pack_rows(v, c, low, high, first_out, last_out):
    for x in range(8):
        field = widened(low, v, high, x)
        coef = widened(low, c, high, x, 64)
        packed = coef[:24]
        for g in range(1, 6):
            packed = packed + pltpu.roll(coef[g * 24 : (g + 1) * 24], 16 * g, 1)
        row = jnp.concatenate([field, packed], axis=0)
        if x < 7:
            first_out[x] = row
        if x > 0:
            last_out[x - 1] = row


def place_slots(codes, amps, out, acc):
    acc[...] = jnp.zeros_like(acc)
    lane = iota((128, 256), 1)
    before = ((iota((128, 256), 0) < lane) | (lane >= 128)).astype(F32).astype(BF16)
    tile_line = iota((128, 128), 0)

    def chunk(turn, seen):
        at = pl.ds(pl.multiple_of(turn * 8, 8), 8)
        code = codes[at, :]
        tiles = code >> 16
        parts = list(split2(amps[at, :]))
        parts.append(((code >> 8) & 255).astype(F32).astype(BF16))
        parts.append((code & 255).astype(F32).astype(BF16))
        hits = [
            (tile_line == tiles[j : j + 1, :]).astype(F32) for j in range(8)
        ]
        hits_b = [h.astype(BF16) for h in hits]
        ranks = dot(jnp.concatenate(hits_b, axis=0), before, ((1,), (0,)))
        slots = []
        for j in range(8):
            rank = ranks[j * 128 : (j + 1) * 128]
            slot = jnp.sum(hits[j] * (rank[:, :128] + seen), axis=0, keepdims=True)
            slots.append((tile_line == slot.astype(jnp.int32)).astype(F32).astype(BF16))
            seen = seen + rank[:, 128:]
        hit = jnp.concatenate(hits_b, axis=1)
        slot = jnp.concatenate(slots, axis=1)
        left = []
        for part in parts:
            wide = part.astype(F32)
            wide = jnp.concatenate([wide[j : j + 1, :] for j in range(8)], axis=1)
            left.append(hit * wide.astype(BF16))
        acc[...] += dot(jnp.concatenate(left, axis=0), slot, ((1,), (1,)))
        return seen

    lax.fori_loop(0, 8, chunk, jnp.zeros((128, 128), F32), unroll=8)
    out[:, 0, :] = acc[0:128] + acc[128:256]
    out[:, 1, :] = acc[256:384] * 256.0 + acc[384:512]


def add_currents(slots, waves, out, low_out, high_out, acc):
    acc[...] = jnp.zeros_like(acc)
    table = jnp.concatenate([p.astype(F32) for p in split3(waves[...])], axis=1).astype(BF16)
    wave_line = iota((64, 2048), 0).astype(F32).astype(BF16)
    cell_line = iota((256, 2048), 0).astype(F32).astype(BF16)
    one, zero = jnp.ones((), BF16), jnp.zeros((), BF16)

    def chunk(turn, carry):
        rows = [slots[turn * 16 + j] for j in range(16)]
        amp = jnp.concatenate([r[0:1, :] for r in rows], axis=1)
        code = jnp.concatenate([r[1:2, :] for r in rows], axis=1).astype(jnp.int32)
        hit = jnp.where(wave_line == (code & 63).astype(F32).astype(BF16), one, zero)
        picked = dot(table, jnp.concatenate([hit, hit, hit], axis=0), ((1,), (0,)))
        current = (picked * amp).astype(BF16)
        cell = code >> 6
        block = (cell >> 8).astype(F32).astype(BF16)
        right = [jnp.where(block == jnp.array(r, BF16), current, zero) for r in range(4)]
        left = jnp.where(cell_line == (cell & 255).astype(F32).astype(BF16), one, zero)
        acc[...] += dot(left, jnp.concatenate(right, axis=0), ((1,), (1,)))
        return carry

    lax.fori_loop(0, 8, chunk, 0, unroll=2)
    low_lanes = iota((256, 128), 1) < 64
    for r in range(4):
        half = acc[:, (r // 2) * 128 : (r // 2 + 1) * 128]
        if r % 2:
            half = pltpu.roll(half, 64, 1)
        half = jnp.where(low_lanes, half, 0.0)
        for b in range(2):
            x = 2 * r + b
            rows = half[b * 128 : (b + 1) * 128]
            out[x] = rows
            low_out[x * 8 : x * 8 + 8, :] = rows[:8]
            high_out[x * 8 : x * 8 + 8, :] = rows[120:]


def pack_injected(own, low, high, first_out, last_out):
    rows = [widened(low, own, high, x) for x in range(8)]
    for j in range(3):
        first_out[j] = rows[j] + pltpu.roll(rows[j + 3], 64, 1)
        last_out[j] = rows[j + 2] + pltpu.roll(rows[j + 5], 64, 1)


def apply_row(src, i, diag, wx, wy, wv):
    v = src[i]
    wyi, wvi = wy[i], wv[i]
    out = diag[i] * v - wx[i] * src[i + 1] - wx[i - 1] * src[i - 1]
    out = out - wyi * pltpu.roll(v, YE - 1, 0) - pltpu.roll(wyi * v, 1, 0)
    return out - wvi * pltpu.roll(v, 96, 1) - pltpu.roll(wvi * v, 32, 1)


def power(src, dst, first, last, weights):
    def row(i, carry):
        dst[i] = apply_row(src, i, *weights)
        return carry

    lax.fori_loop(first, last + 1, row, 0, unroll=4)


def moments(fields, out, first):
    own = [f[first : first + 8, 8:136, :].reshape(1024, 128) for f in fields]
    lane, row = iota((32, 128), 1), iota((32, 128), 0)
    packed = jnp.zeros((32, 128), F32)
    parts = [split2(f) for f in own]
    for k in range(3):
        (hi, lo), (next_hi, next_lo) = parts[k], parts[k + 1]
        left = jnp.concatenate([hi, lo], axis=1)
        product = dot(left, jnp.concatenate([hi, next_hi], axis=1), ((0,), (0,)))
        cross = dot(hi, jnp.concatenate([lo, next_lo], axis=1), ((0,), (0,)))
        product = product[:128] + product[128:] + cross
        column = lane - 32 * k
        totals = []
        for b in range(2):
            total = jnp.zeros((32, 128), F32)
            for l in range(4):
                piece = product[l * 32 : (l + 1) * 32, b * 128 : (b + 1) * 128]
                turn = (32 * (k - l)) % 128
                total = total + (pltpu.roll(piece, turn, 1) if turn else piece)
            totals.append(total)
        even, odd = totals
        inside = (column >= 0) & (column < 32)
        packed = packed + jnp.where(inside, jnp.where(column > row, even, odd), 0.0)
        diagonal = jnp.sum(jnp.where(column == row, even, 0.0), axis=1, keepdims=True)
        packed = packed + jnp.where(lane == 96 + k, diagonal, 0.0)
    out[...] = packed


def coefficients(gram):
    lane, row = iota((32, 128), 1), iota((32, 128), 0)
    packed = gram[...]
    flipped = jnp.concatenate([packed, jnp.zeros((96, 128), F32)], axis=0).T
    bases = []
    for k in range(3):
        direct = pltpu.roll(packed, 128 - 32 * k, 1) if k else packed
        mirror = flipped[k * 32 : (k + 1) * 32, :]
        even = jnp.where(lane > row, direct, mirror)
        even = jnp.where(lane == row, packed[:, 96 + k : 97 + k], even)
        bases.append(jnp.where(lane < 32, even, 0.0))
        odd = jnp.where(lane > row, mirror, direct)
        bases.append(jnp.where(lane < 32, odd, 0.0))

    def moment(k, place):
        return pltpu.roll(bases[k], place, 1) if place else bases[k]

    tiles = []
    for i in range(3):
        block = moment(i, 96)
        for j in range(3):
            block = block + SCALE * moment(i + j + 1, 32 * j) + SHIFT * moment(i + j, 32 * j)
        tiles += [block[r * 8 : r * 8 + 8] for r in range(4)]
    sub = iota((8, 128), 0)
    for t in range(12):
        rows = tiles[t]
        cols = [jnp.broadcast_to(rows[:, t * 8 + j : t * 8 + j + 1], (8, 128)) for j in range(8)]
        for j in range(8):
            inverse = 1.0 / cols[j][j : j + 1, :]
            pivot = rows[j : j + 1, :] * inverse
            rows = jnp.where(sub == j, pivot, rows - cols[j] * pivot)
            for n in range(j + 1, 8):
                top = cols[n][j : j + 1, :] * inverse
                cols[n] = jnp.where(sub == j, top, cols[n] - cols[j] * top)
        for i in range(12):
            block = tiles[i]
            for j in range(8):
                if i != t:
                    block = block - tiles[i][:, t * 8 + j : t * 8 + j + 1] * rows[j : j + 1, :]
            tiles[i] = block
        tiles[t] = rows
    lane = iota((32, 128), 1)
    outs = []
    for i in range(3):
        y = jnp.concatenate(tiles[i * 4 : i * 4 + 4], axis=0)
        y = jnp.where(lane >= 96, y, 0.0)
        y = y + pltpu.roll(y, 32, 1) + pltpu.roll(y, 64, 1) + pltpu.roll(y, 96, 1)
        outs.append(
            jnp.concatenate([jnp.where(lane // 32 == l, y, 0.0) for l in range(4)], axis=0)
        )
    return outs


def combination(gram):
    y0, y1, y2 = coefficients(gram)
    step = jnp.concatenate([y0, y1, y2, jnp.zeros_like(y0)], axis=0)
    less = jnp.concatenate(
        [
            -SHIFT * y0,
            -SCALE * y0 - SHIFT * y1,
            -SCALE * y1 - SHIFT * y2,
            -SCALE * y2,
        ],
        axis=0,
    )
    return jnp.concatenate([step, less], axis=1)


def grid_weights(
    v, c, low, high, x_low, x_high, diag, wx, wy, wv, cap, free, ext,
):
    lane = iota((YE, 128), 1)
    n = iota((128, 512), 1)
    q = iota((128, 512), 0)
    spread = ((q % 16 == (n // 128) * 4 + (n % 128) // 32) & (q < 48)).astype(F32).astype(BF16)

    def expand(i, coef):
        hi, mid, lo = [p.astype(F32) for p in split3(coef)]
        parts = hi + pltpu.roll(mid, 16, 1) + pltpu.roll(lo, 32, 1)
        wide = dot(parts.astype(BF16), spread, ((1,), (0,)))
        cap[i] = wide[:, :128]
        wx[i] = wide[:, 128:256]
        wy[i] = wide[:, 256:384]
        wv[i] = jnp.where(lane < 96, wide[:, 384:], 0.0)
        diag[i] = wide[:, :128] + wide[:, 384:]

    def halo_row(j, ref, base, present):
        ext[base + j] = ref[j, :YE, :] * present
        packed = ref[j, YE:, :] * present
        groups = [packed] + [pltpu.roll(packed, 128 - 16 * g, 1) for g in range(1, 6)]
        coef = jnp.concatenate(groups, axis=0)
        expand(base + j, jnp.where(lane < 16, coef, 0.0))

    def own_row(x, carry):
        ext[7 + x] = widened(low, v, high, x)
        expand(7 + x, widened(low, c, high, x, 64))
        return carry

    def halo_rows(j, carry):
        low_in, high_in = inside(GX)
        halo_row(j, x_low, 0, low_in)
        halo_row(j, x_high, 15, high_in)
        return carry

    lax.fori_loop(0, 8, own_row, 0, unroll=2)
    lax.fori_loop(0, 7, halo_rows, 0)

    def diagonal(i, carry):
        total = diag[i] + wx[i] + wx[i - 1] + wy[i] + pltpu.roll(wy[i], 1, 0)
        total = total + pltpu.roll(wv[i], 32, 1)
        diag[i] = (total - SHIFT) * (1.0 / SCALE)
        return carry

    lax.fori_loop(1, 21, diagonal, 0, unroll=2)

    def edges(i, carry):
        wx[i] = jnp.where(cap[i + 1] > 0, wx[i] * (1.0 / SCALE), 0.0)
        wy[i] = jnp.where(pltpu.roll(cap[i], YE - 1, 0) > 0, wy[i] * (1.0 / SCALE), 0.0)
        wv[i] = wv[i] * (1.0 / SCALE)
        return carry

    lax.fori_loop(0, 21, edges, 0, unroll=3)
    weights = (diag, wx, wy, wv)


    def start(i, carry):
        e = ext[i]
        free[i] = (cap[i] - SHIFT) * e - SCALE * apply_row(ext, i, *weights)
        return carry

    lax.fori_loop(1, 21, start, 0, unroll=2)


def first_basis(
    diag, wx, wy, wv, free, inj, i_low, i_high, ix_low, ix_high,
    change, v0, v1, v2, v3, gram,
):
    lane = iota((YE, 128), 1)
    weights = (diag, wx, wy, wv)

    def start(i, both):
        now = jnp.where(lane < 32, both, 0.0)
        then = jnp.where(lane < 32, pltpu.roll(both, 96, 1), 0.0)
        change[i] = now - then
        v0[i] = free[i] - now

    def own_start(x, carry):
        start(7 + x, widened(i_low, inj, i_high, x))
        return carry

    def halo_start(j, carry):
        low_in, high_in = inside(GX)
        for ref, base, present in ((ix_low, 1, low_in), (ix_high, 15, high_in)):
            both = ref[j] * present
            start(base + j, both)
            start(base + 3 + j, pltpu.roll(both, 64, 1))
        return carry

    lax.fori_loop(0, 8, own_start, 0)
    lax.fori_loop(0, 3, halo_start, 0)
    power(v0, v1, 2, 19, weights)
    power(v1, v2, 3, 18, weights)
    power(v2, v3, 4, 17, weights)
    moments((v0, v1, v2, v3), gram, 7)


def second_basis(
    gram, diag, wx, wy, wv, cap, change, v0, v1, v2, v3, step, b0, b1, b2, b3, gram_out
):
    weights = (diag, wx, wy, wv)
    mix = combination(gram)

    def row(i, carry):
        fields = jnp.concatenate([v0[i], v1[i], v2[i], v3[i]], axis=1)
        both = dot_split(fields, mix, ((1,), (0,)))
        moved = both[:, :128]
        step[i] = moved
        b0[i] = v0[i] + both[:, 128:] + cap[i] * moved + change[i]
        return carry

    lax.fori_loop(4, 18, row, 0, unroll=2)
    power(b0, b1, 5, 16, weights)
    power(b1, b2, 6, 15, weights)
    power(b2, b3, 7, 14, weights)
    moments((b0, b1, b2, b3), gram_out, 7)


def store_rows(out, x, value):
    for l in range(4):
        out[pl.ds(l * 8 + x, 32, stride=32), :] = value[l * 32 : (l + 1) * 32]


def load_rows(ref, x):
    return jnp.concatenate([ref[pl.ds(l * 8 + x, 32, stride=32), :] for l in range(4)], axis=0)


def from_lanes(step, b0, volts, volts_out, residual_out):
    for x in range(8):
        store_rows(volts_out, x, load_rows(volts, x) + step[7 + x, 8:136, :].T)
        store_rows(residual_out, x, b0[7 + x, 8:136, :].T)


def finish(gram, b0, b1, b2, b3, volts, residual, volts_out, residual_out):
    mix = combination(gram)
    for x in range(0, 8, 2):
        fields = jnp.concatenate(
            [
                jnp.concatenate([b[7 + n, 8:136, :] for b in (b0, b1, b2, b3)], axis=1)
                for n in (x, x + 1)
            ],
            axis=0,
        )
        both = dot_split(mix, fields, ((0,), (1,)))
        for n in range(2):
            own = both[:, n * 128 : (n + 1) * 128]
            store_rows(volts_out, x + n, load_rows(volts, x + n) + own[:128])
            store_rows(residual_out, x + n, load_rows(residual, x + n) + own[128:])


def neighbours(to_low, to_high, axis):
    size = lax.axis_size(axis)
    up = [(i, (i + 1) % size) for i in range(size)]
    from_low = lax.ppermute(to_high, axis, up)
    return from_low, lax.ppermute(to_low, axis, [(b, a) for a, b in up])


def everywhere(x):
    x = x + lax.ppermute(x, "gy_1", [(0, 1), (1, 0)])
    for axis in ("gy_0", "gx_1", "gx_0"):
        one, two, three = [
            lax.ppermute(x, axis, [(i, i ^ k) for i in range(4)]) for k in (1, 2, 3)
        ]
        x = (x + one) + (two + three)
    return x


def exchange(slots):
    return lax.all_to_all(slots, GX_GY, split_axis=0, concat_axis=0, tiled=True)


def body(volts, cap, cond_x, cond_y, via, waveforms, placement, cells, wave_ids, amps):
    vmem = pltpu.VMEM
    coefs = jnp.concatenate([a.reshape(32, 128) for a in (cap, cond_x, cond_y, via)], axis=0)
    v, c, y_low, y_high = call(
        to_lanes,
        [(8, 128, 128), (8, 128, 128), (128, 128), (128, 128)],
        [volts.reshape(1024, 128), coefs],
    )
    y_low, y_high = neighbours(y_low, y_high, GY)
    codes = (placement.reshape(-1) * 65536 + cells * 64 + wave_ids).reshape(64, 128)
    (slots,) = call(
        place_slots, [(128, 2, 128)], [codes, amps.reshape(64, 128)], [vmem((512, 128), F32)]
    )
    y_low, y_high, slots = lax.optimization_barrier((y_low, y_high, slots))
    x_low, x_high = call(pack_rows, [(7, 168, 128)] * 2, [v, c, y_low, y_high])
    x_low, x_high = neighbours(x_low, x_high, GX)
    slots = exchange(slots)
    inj, i_low, i_high = call(
        add_currents,
        [(8, 128, 128), (64, 128), (64, 128)],
        [slots, waveforms],
        [vmem((256, 256), F32)],
    )
    i_low, i_high = neighbours(i_low, i_high, GY)
    ix_low, ix_high = call(pack_injected, [(3, YE, 128)] * 2, [inj, i_low, i_high])
    ix_low, ix_high = neighbours(ix_low, ix_high, GX)
    wide = (XE, YE, 128)
    diag, wx, wy, wv, cap, free = call(
        grid_weights, [wide] * 6, [v, c, y_low, y_high, x_low, x_high], [vmem(wide, F32)]
    )
    *kept, gram = call(
        first_basis,
        [wide] * 5 + [(32, 128)],
        [diag, wx, wy, wv, free, inj, i_low, i_high, ix_low, ix_high],
    )
    step, *basis, gram = call(
        second_basis,
        [wide] * 5 + [(32, 128)],
        [everywhere(gram), diag, wx, wy, wv, cap] + kept,
    )
    so_far = call(
        from_lanes, [(1024, 128)] * 2, [step, basis[0], volts.reshape(1024, 128)]
    )
    outs = call(finish, [(1024, 128)] * 2, [everywhere(gram)] + basis + list(so_far))
    return tuple(o.reshape(volts.shape) for o in outs)


def solution(mesh):
    finer = Mesh(mesh.devices.reshape(4, 4, 4, 2), ("gx_0", "gx_1", "gy_0", "gy_1"))
    in_specs = (
        P(None, None, GX, GY),
        P(None, GX, GY),
        P(None, GX, GY),
        P(None, GX, GY),
        P(None, GX, GY),
        P(),
        P(GX_GY, None),
        P(GX_GY),
        P(GX_GY),
        P(GX_GY),
    )
    out_specs = (P(None, None, GX, GY), P(None, None, GX, GY))
    return jax.shard_map(body, mesh=finer, in_specs=in_specs, out_specs=out_specs, check_vma=False)
```

```python
import jax
import jax.numpy as jnp
from jax import lax
from jax.experimental import pallas as pl
from jax.experimental.pallas import tpu as pltpu
from jax.sharding import Mesh
from jax.sharding import PartitionSpec as P

GX = ("gx_0", "gx_1")
GY = ("gy_0", "gy_1")
GX_GY = GX + GY
F32 = jnp.float32
BF16 = jnp.bfloat16
HIGHEST = lax.Precision.HIGHEST
SHIFT = 7.0
SCALE = 7.0
XE = 22
YE = 144


def iota(shape, dim):
    return lax.broadcasted_iota(jnp.int32, shape, dim)


def dot(a, b, dims, precision=None):
    return lax.dot_general(
        a, b, (dims, ((), ())), precision=precision, preferred_element_type=F32
    )


def split2(x):
    hi = x.astype(BF16)
    return hi, (x - hi.astype(F32)).astype(BF16)


def dot_split(a, b, dims):
    a_hi, a_lo = split2(a)
    b_hi, b_lo = split2(b)
    return dot(a_hi, b_hi, dims) + dot(a_hi, b_lo, dims) + dot(a_lo, b_hi, dims)


def split3(x):
    hi = x.astype(BF16)
    rest = x - hi.astype(F32)
    mid = rest.astype(BF16)
    return hi, mid, (rest - mid.astype(F32)).astype(BF16)


def call(kernel, outs, args, scratch=(), limit=14, in_specs=None):
    outs = [o if isinstance(o, jax.ShapeDtypeStruct) else jax.ShapeDtypeStruct(o, F32) for o in outs]
    specs = {} if in_specs is None else {"in_specs": in_specs}
    return pl.pallas_call(
        kernel,
        out_shape=tuple(outs),
        scratch_shapes=list(scratch),
        **specs,
        compiler_params=pltpu.CompilerParams(vmem_limit_bytes=limit << 20),
        name=kernel.__name__,
    )(*args)


def to_lanes(volts, stack, v_out, c_out, low_out, high_out):
    for x in range(8):
        field = load_rows(volts, x).T
        v_out[x] = field
        coef = stack[pl.ds(x, 16, stride=8), :]
        coef = jnp.concatenate([coef, jnp.zeros((112, 128), F32)], axis=0).T
        c_out[x] = coef
        low_out[x * 8 : x * 8 + 8, :] = field[:8]
        low_out[64 + x * 8 : 72 + x * 8, :] = coef[:8]
        high_out[x * 8 : x * 8 + 8, :] = field[120:]
        high_out[64 + x * 8 : 72 + x * 8, :] = coef[120:]


def inside(axis):
    me = lax.axis_index(axis)
    return (me > 0).astype(F32), (me < lax.axis_size(axis) - 1).astype(F32)


def widened(low, own, high, x, base=0):
    at = pl.ds(pl.multiple_of(base + x * 8, 8), 8)
    low_in, high_in = inside(GY)
    return jnp.concatenate([low[at, :] * low_in, own[x], high[at, :] * high_in], axis=0)


def pack_rows(v, c, low, high, first_out, last_out):
    for x in range(8):
        field = widened(low, v, high, x)
        coef = widened(low, c, high, x, 64)
        packed = coef[:24]
        for g in range(1, 6):
            packed = packed + pltpu.roll(coef[g * 24 : (g + 1) * 24], 16 * g, 1)
        row = jnp.concatenate([field, packed], axis=0)
        if x < 7:
            first_out[x] = row
        if x > 0:
            last_out[x - 1] = row


def place_slots(listed, amps, out, acc):
    acc[...] = jnp.zeros_like(acc)
    lane = iota((128, 256), 1)
    before = ((iota((128, 256), 0) < lane) | (lane >= 128)).astype(F32).astype(BF16)
    tile_line = iota((128, 128), 0)

    def chunk(turn, seen):
        at = pl.ds(pl.multiple_of(turn * 8, 8), 8)
        tiles = listed[at, :]
        cells = listed[pl.ds(pl.multiple_of(64 + turn * 8, 8), 8), :]
        code = cells * 64 + listed[pl.ds(pl.multiple_of(128 + turn * 8, 8), 8), :]
        parts = list(split2(amps[at, :]))
        parts.append((code >> 8).astype(F32).astype(BF16))
        parts.append((code & 255).astype(F32).astype(BF16))
        hits = [
            (tile_line == tiles[j : j + 1, :]).astype(F32) for j in range(8)
        ]
        hits_b = [h.astype(BF16) for h in hits]
        ranks = dot(jnp.concatenate(hits_b, axis=0), before, ((1,), (0,)))
        slots = []
        for j in range(8):
            rank = ranks[j * 128 : (j + 1) * 128]
            slot = jnp.sum(hits[j] * (rank[:, :128] + seen), axis=0, keepdims=True)
            slots.append((tile_line == slot.astype(jnp.int32)).astype(F32).astype(BF16))
            seen = seen + rank[:, 128:]
        hit = jnp.concatenate(hits_b, axis=1)
        slot = jnp.concatenate(slots, axis=1)
        left = []
        for part in parts:
            wide = part.astype(F32)
            wide = jnp.concatenate([wide[j : j + 1, :] for j in range(8)], axis=1)
            left.append(hit * wide.astype(BF16))
        acc[...] += dot(jnp.concatenate(left, axis=0), slot, ((1,), (1,)))
        return seen

    lax.fori_loop(0, 8, chunk, jnp.zeros((128, 128), F32), unroll=8)
    out[:, 0, :] = acc[0:128] + acc[128:256]
    out[:, 1, :] = acc[256:384] * 256.0 + acc[384:512]


def add_currents(slots, waves, out, low_out, high_out, acc):
    acc[...] = jnp.zeros_like(acc)
    table = jnp.concatenate([p.astype(F32) for p in split3(waves[...])], axis=1).astype(BF16)
    wave_line = iota((64, 2048), 0).astype(F32).astype(BF16)
    cell_line = iota((256, 2048), 0).astype(F32).astype(BF16)
    one, zero = jnp.ones((), BF16), jnp.zeros((), BF16)

    def chunk(turn, carry):
        rows = [slots[turn * 16 + j] for j in range(16)]
        amp = jnp.concatenate([r[0:1, :] for r in rows], axis=1)
        code = jnp.concatenate([r[1:2, :] for r in rows], axis=1).astype(jnp.int32)
        hit = jnp.where(wave_line == (code & 63).astype(F32).astype(BF16), one, zero)
        picked = dot(table, jnp.concatenate([hit, hit, hit], axis=0), ((1,), (0,)))
        current = (picked * amp).astype(BF16)
        cell = code >> 6
        block = (cell >> 8).astype(F32).astype(BF16)
        right = [jnp.where(block == jnp.array(r, BF16), current, zero) for r in range(4)]
        left = jnp.where(cell_line == (cell & 255).astype(F32).astype(BF16), one, zero)
        acc[...] += dot(left, jnp.concatenate(right, axis=0), ((1,), (1,)))
        return carry

    lax.fori_loop(0, 8, chunk, 0, unroll=2)
    low_lanes = iota((256, 128), 1) < 64
    for r in range(4):
        half = acc[:, (r // 2) * 128 : (r // 2 + 1) * 128]
        if r % 2:
            half = pltpu.roll(half, 64, 1)
        half = jnp.where(low_lanes, half, 0.0)
        for b in range(2):
            x = 2 * r + b
            rows = half[b * 128 : (b + 1) * 128]
            out[x] = rows
            low_out[x * 8 : x * 8 + 8, :] = rows[:8]
            high_out[x * 8 : x * 8 + 8, :] = rows[120:]


def pack_injected(own, low, high, first_out, last_out):
    rows = [widened(low, own, high, x) for x in range(8)]
    for j in range(3):
        first_out[j] = rows[j] + pltpu.roll(rows[j + 3], 64, 1)
        last_out[j] = rows[j + 2] + pltpu.roll(rows[j + 5], 64, 1)


def apply_row(src, i, diag, wx, wy, wv):
    v = src[i]
    wyi, wvi = wy[i], wv[i]
    out = diag[i] * v - wx[i] * src[i + 1] - wx[i - 1] * src[i - 1]
    out = out - wyi * pltpu.roll(v, YE - 1, 0) - pltpu.roll(wyi * v, 1, 0)
    return out - wvi * pltpu.roll(v, 96, 1) - pltpu.roll(wvi * v, 32, 1)


def power(src, dst, first, last, weights):
    def row(i, carry):
        dst[i] = apply_row(src, i, *weights)
        return carry

    lax.fori_loop(first, last + 1, row, 0, unroll=4)


def moments(fields, out, first):
    own = [f[first : first + 8, 8:136, :].reshape(1024, 128) for f in fields]
    lane, row = iota((32, 128), 1), iota((32, 128), 0)
    packed = jnp.zeros((32, 128), F32)
    parts = [split2(f) for f in own]
    for k in range(3):
        (hi, lo), (next_hi, next_lo) = parts[k], parts[k + 1]
        left = jnp.concatenate([hi, lo], axis=1)
        product = dot(left, jnp.concatenate([hi, next_hi], axis=1), ((0,), (0,)))
        cross = dot(hi, jnp.concatenate([lo, next_lo], axis=1), ((0,), (0,)))
        product = product[:128] + product[128:] + cross
        column = lane - 32 * k
        totals = []
        for b in range(2):
            total = jnp.zeros((32, 128), F32)
            for l in range(4):
                piece = product[l * 32 : (l + 1) * 32, b * 128 : (b + 1) * 128]
                turn = (32 * (k - l)) % 128
                total = total + (pltpu.roll(piece, turn, 1) if turn else piece)
            totals.append(total)
        even, odd = totals
        inside = (column >= 0) & (column < 32)
        packed = packed + jnp.where(inside, jnp.where(column > row, even, odd), 0.0)
        diagonal = jnp.sum(jnp.where(column == row, even, 0.0), axis=1, keepdims=True)
        packed = packed + jnp.where(lane == 96 + k, diagonal, 0.0)
    out[...] = packed


def coefficients(gram):
    lane, row = iota((32, 128), 1), iota((32, 128), 0)
    sums = [gram[n] for n in range(gram.shape[0])]
    while len(sums) > 1:
        sums = [a + b for a, b in zip(sums[::2], sums[1::2])]
    packed = sums[0]
    flipped = jnp.concatenate([packed, jnp.zeros((96, 128), F32)], axis=0).T
    bases = []
    for k in range(3):
        direct = pltpu.roll(packed, 128 - 32 * k, 1) if k else packed
        mirror = flipped[k * 32 : (k + 1) * 32, :]
        even = jnp.where(lane > row, direct, mirror)
        even = jnp.where(lane == row, packed[:, 96 + k : 97 + k], even)
        bases.append(jnp.where(lane < 32, even, 0.0))
        odd = jnp.where(lane > row, mirror, direct)
        bases.append(jnp.where(lane < 32, odd, 0.0))

    def moment(k, place):
        return pltpu.roll(bases[k], place, 1) if place else bases[k]

    tiles = []
    for i in range(3):
        block = moment(i, 96)
        for j in range(3):
            block = block + SCALE * moment(i + j + 1, 32 * j) + SHIFT * moment(i + j, 32 * j)
        tiles += [block[r * 8 : r * 8 + 8] for r in range(4)]
    sub = iota((8, 128), 0)
    for t in range(12):
        rows = tiles[t]
        cols = [jnp.broadcast_to(rows[:, t * 8 + j : t * 8 + j + 1], (8, 128)) for j in range(8)]
        for j in range(8):
            inverse = 1.0 / cols[j][j : j + 1, :]
            pivot = rows[j : j + 1, :] * inverse
            rows = jnp.where(sub == j, pivot, rows - cols[j] * pivot)
            for n in range(j + 1, 8):
                top = cols[n][j : j + 1, :] * inverse
                cols[n] = jnp.where(sub == j, top, cols[n] - cols[j] * top)
        for i in range(12):
            block = tiles[i]
            for j in range(8):
                if i != t:
                    block = block - tiles[i][:, t * 8 + j : t * 8 + j + 1] * rows[j : j + 1, :]
            tiles[i] = block
        tiles[t] = rows
    lane = iota((32, 128), 1)
    outs = []
    for i in range(3):
        y = jnp.concatenate(tiles[i * 4 : i * 4 + 4], axis=0)
        y = jnp.where(lane >= 96, y, 0.0)
        y = y + pltpu.roll(y, 32, 1) + pltpu.roll(y, 64, 1) + pltpu.roll(y, 96, 1)
        outs.append(
            jnp.concatenate([jnp.where(lane // 32 == l, y, 0.0) for l in range(4)], axis=0)
        )
    return outs


def combination(gram):
    y0, y1, y2 = coefficients(gram)
    step = jnp.concatenate([y0, y1, y2, jnp.zeros_like(y0)], axis=0)
    less = jnp.concatenate(
        [
            -SHIFT * y0,
            -SCALE * y0 - SHIFT * y1,
            -SCALE * y1 - SHIFT * y2,
            -SCALE * y2,
        ],
        axis=0,
    )
    return jnp.concatenate([step, less], axis=1)


def grid_weights(
    v, c, low, high, x_low, x_high, diag, wx, wy, wv, cap, free, ext,
):
    lane = iota((YE, 128), 1)
    n = iota((128, 512), 1)
    q = iota((128, 512), 0)
    spread = ((q % 16 == (n // 128) * 4 + (n % 128) // 32) & (q < 48)).astype(F32).astype(BF16)

    def expand(i, coef):
        hi, mid, lo = [p.astype(F32) for p in split3(coef)]
        parts = hi + pltpu.roll(mid, 16, 1) + pltpu.roll(lo, 32, 1)
        wide = dot(parts.astype(BF16), spread, ((1,), (0,)))
        cap[i] = wide[:, :128]
        wx[i] = wide[:, 128:256]
        wy[i] = wide[:, 256:384]
        wv[i] = jnp.where(lane < 96, wide[:, 384:], 0.0)
        diag[i] = wide[:, :128] + wide[:, 384:]

    def halo_row(j, ref, base, present):
        ext[base + j] = ref[j, :YE, :] * present
        packed = ref[j, YE:, :] * present
        groups = [packed] + [pltpu.roll(packed, 128 - 16 * g, 1) for g in range(1, 6)]
        coef = jnp.concatenate(groups, axis=0)
        expand(base + j, jnp.where(lane < 16, coef, 0.0))

    def own_row(x, carry):
        ext[7 + x] = widened(low, v, high, x)
        expand(7 + x, widened(low, c, high, x, 64))
        return carry

    def halo_rows(j, carry):
        low_in, high_in = inside(GX)
        halo_row(j, x_low, 0, low_in)
        halo_row(j, x_high, 15, high_in)
        return carry

    lax.fori_loop(0, 8, own_row, 0, unroll=2)
    lax.fori_loop(0, 7, halo_rows, 0)

    def diagonal(i, carry):
        total = diag[i] + wx[i] + wx[i - 1] + wy[i] + pltpu.roll(wy[i], 1, 0)
        total = total + pltpu.roll(wv[i], 32, 1)
        diag[i] = (total - SHIFT) * (1.0 / SCALE)
        return carry

    lax.fori_loop(1, 21, diagonal, 0, unroll=2)

    def edges(i, carry):
        wx[i] = jnp.where(cap[i + 1] > 0, wx[i] * (1.0 / SCALE), 0.0)
        wy[i] = jnp.where(pltpu.roll(cap[i], YE - 1, 0) > 0, wy[i] * (1.0 / SCALE), 0.0)
        wv[i] = wv[i] * (1.0 / SCALE)
        return carry

    lax.fori_loop(0, 21, edges, 0, unroll=3)
    weights = (diag, wx, wy, wv)


    def start(i, carry):
        e = ext[i]
        free[i] = (cap[i] - SHIFT) * e - SCALE * apply_row(ext, i, *weights)
        return carry

    lax.fori_loop(1, 21, start, 0, unroll=2)


def first_basis(
    diag, wx, wy, wv, free, inj, i_low, i_high, ix_low, ix_high,
    change, v0, v1, v2, v3, gram,
):
    lane = iota((YE, 128), 1)
    weights = (diag, wx, wy, wv)

    def start(i, both):
        now = jnp.where(lane < 32, both, 0.0)
        then = jnp.where(lane < 32, pltpu.roll(both, 96, 1), 0.0)
        change[i] = now - then
        v0[i] = free[i] - now

    def own_start(x, carry):
        start(7 + x, widened(i_low, inj, i_high, x))
        return carry

    def halo_start(j, carry):
        low_in, high_in = inside(GX)
        for ref, base, present in ((ix_low, 1, low_in), (ix_high, 15, high_in)):
            both = ref[j] * present
            start(base + j, both)
            start(base + 3 + j, pltpu.roll(both, 64, 1))
        return carry

    lax.fori_loop(0, 8, own_start, 0)
    lax.fori_loop(0, 3, halo_start, 0)
    power(v0, v1, 2, 19, weights)
    power(v1, v2, 3, 18, weights)
    power(v2, v3, 4, 17, weights)
    moments((v0, v1, v2, v3), gram, 7)


def second_basis(
    gram, diag, wx, wy, wv, cap, change, v0, v1, v2, v3, step, b0, b1, b2, b3, gram_out
):
    weights = (diag, wx, wy, wv)
    mix = combination(gram)

    def row(i, carry):
        fields = jnp.concatenate([v0[i], v1[i], v2[i], v3[i]], axis=1)
        both = dot_split(fields, mix, ((1,), (0,)))
        moved = both[:, :128]
        step[i] = moved
        b0[i] = v0[i] + both[:, 128:] + cap[i] * moved + change[i]
        return carry

    lax.fori_loop(4, 18, row, 0, unroll=2)
    power(b0, b1, 5, 16, weights)
    power(b1, b2, 6, 15, weights)
    power(b2, b3, 7, 14, weights)
    moments((b0, b1, b2, b3), gram_out, 7)


def store_rows(out, x, value):
    for l in range(4):
        out[pl.ds(l * 8 + x, 32, stride=32), :] = value[l * 32 : (l + 1) * 32]


def load_rows(ref, x):
    return jnp.concatenate([ref[pl.ds(l * 8 + x, 32, stride=32), :] for l in range(4)], axis=0)


def from_lanes(step, b0, volts, volts_out, residual_out):
    for x in range(8):
        store_rows(volts_out, x, load_rows(volts, x) + step[7 + x, 8:136, :].T)
        store_rows(residual_out, x, b0[7 + x, 8:136, :].T)


def finish(gram, b0, b1, b2, b3, volts, residual, volts_out, residual_out):
    mix = combination(gram)
    for x in range(0, 8, 2):
        fields = jnp.concatenate(
            [
                jnp.concatenate([b[7 + n, 8:136, :] for b in (b0, b1, b2, b3)], axis=1)
                for n in (x, x + 1)
            ],
            axis=0,
        )
        both = dot_split(mix, fields, ((0,), (1,)))
        for n in range(2):
            own = both[:, n * 128 : (n + 1) * 128]
            store_rows(volts_out, x + n, load_rows(volts, x + n) + own[:128])
            store_rows(residual_out, x + n, load_rows(residual, x + n) + own[128:])


def neighbours(to_low, to_high, axis):
    size = lax.axis_size(axis)
    up = [(i, (i + 1) % size) for i in range(size)]
    from_low = lax.ppermute(to_high, axis, up)
    return from_low, lax.ppermute(to_low, axis, [(b, a) for a, b in up])


def everywhere(x, beside=()):
    x = x + lax.ppermute(x, "gy_1", [(0, 1), (1, 0)])
    one, two, three = [
        lax.ppermute(x, "gy_0", [(i, i ^ k) for i in range(4)]) for k in (1, 2, 3)
    ]
    x = (x + one) + (two + three)
    x, beside = lax.optimization_barrier((x, beside))
    x = jnp.broadcast_to(x[None], (lax.axis_size(GX),) + x.shape)
    return lax.all_to_all(x, GX, split_axis=0, concat_axis=0, tiled=True), beside


def exchange(slots):
    return lax.all_to_all(slots, GX_GY, split_axis=0, concat_axis=0, tiled=True)


def body(volts, cap, cond_x, cond_y, via, waveforms, placement, cells, wave_ids, amps):
    vmem = pltpu.VMEM
    coefs = jnp.concatenate([a.reshape(32, 128) for a in (cap, cond_x, cond_y, via)], axis=0)
    v, c, y_low, y_high = call(
        to_lanes,
        [(8, 128, 128), (8, 128, 128), (128, 128), (128, 128)],
        [volts.reshape(1024, 128), coefs],
    )
    y_low, y_high = neighbours(y_low, y_high, GY)
    listed = [a.reshape(64, 128) for a in (placement, cells, wave_ids)]
    (slots,) = call(
        place_slots,
        [(128, 2, 128)],
        [jnp.concatenate(listed, axis=0), amps.reshape(64, 128)],
        [vmem((512, 128), F32)],
    )
    y_low, y_high, slots = lax.optimization_barrier((y_low, y_high, slots))
    x_low, x_high = call(pack_rows, [(7, 168, 128)] * 2, [v, c, y_low, y_high])
    x_low, x_high = neighbours(x_low, x_high, GX)
    slots = exchange(slots)
    inj, i_low, i_high = call(
        add_currents,
        [(8, 128, 128), (64, 128), (64, 128)],
        [slots, waveforms],
        [vmem((256, 256), F32)],
    )
    i_low, i_high = neighbours(i_low, i_high, GY)
    ix_low, ix_high = call(pack_injected, [(3, YE, 128)] * 2, [inj, i_low, i_high])
    ix_low, ix_high = neighbours(ix_low, ix_high, GX)
    wide = (XE, YE, 128)
    diag, wx, wy, wv, cap, free = call(
        grid_weights, [wide] * 6, [v, c, y_low, y_high, x_low, x_high], [vmem(wide, F32)]
    )
    *kept, gram = call(
        first_basis,
        [wide] * 5 + [(32, 128)],
        [diag, wx, wy, wv, free, inj, i_low, i_high, ix_low, ix_high],
    )
    gram, _ = everywhere(gram)
    step, *basis, gram = call(
        second_basis,
        [wide] * 5 + [(32, 128)],
        [gram, diag, wx, wy, wv, cap] + kept,
    )
    so_far = call(
        from_lanes, [(1024, 128)] * 2, [step, basis[0], volts.reshape(1024, 128)]
    )
    gram, so_far = everywhere(gram, so_far)
    outs = call(finish, [(1024, 128)] * 2, [gram] + basis + list(so_far))
    return tuple(o.reshape(volts.shape) for o in outs)


def solution(mesh):
    finer = Mesh(mesh.devices.reshape(4, 4, 4, 2), ("gx_0", "gx_1", "gy_0", "gy_1"))
    in_specs = (
        P(None, None, GX, GY),
        P(None, GX, GY),
        P(None, GX, GY),
        P(None, GX, GY),
        P(None, GX, GY),
        P(),
        P(GX_GY, None),
        P(GX_GY),
        P(GX_GY),
        P(GX_GY),
    )
    out_specs = (P(None, None, GX, GY), P(None, None, GX, GY))
    return jax.shard_map(body, mesh=finer, in_specs=in_specs, out_specs=out_specs, check_vma=False)
```

```python
import jax
import jax.numpy as jnp
from jax import lax
from jax.experimental import pallas as pl
from jax.experimental.pallas import tpu as pltpu
from jax.sharding import Mesh
from jax.sharding import PartitionSpec as P

GX = ("gx_0", "gx_1")
GY = ("gy_0", "gy_1")
GX_GY = GX + GY
F32 = jnp.float32
BF16 = jnp.bfloat16
SHIFT = 7.0
SCALE = 7.0
XE = 22
YE = 144


def iota(shape, dim):
    return lax.broadcasted_iota(jnp.int32, shape, dim)


def dot(a, b, dims):
    return lax.dot_general(a, b, (dims, ((), ())), preferred_element_type=F32)


def split2(x):
    hi = x.astype(BF16)
    return hi, (x - hi.astype(F32)).astype(BF16)


def split3(x):
    hi = x.astype(BF16)
    rest = x - hi.astype(F32)
    mid = rest.astype(BF16)
    return hi, mid, (rest - mid.astype(F32)).astype(BF16)


def call(kernel, outs, args, scratch=(), limit=14, in_specs=None):
    outs = [o if isinstance(o, jax.ShapeDtypeStruct) else jax.ShapeDtypeStruct(o, F32) for o in outs]
    specs = {} if in_specs is None else {"in_specs": in_specs}
    return pl.pallas_call(
        kernel,
        out_shape=tuple(outs),
        scratch_shapes=list(scratch),
        **specs,
        compiler_params=pltpu.CompilerParams(vmem_limit_bytes=limit << 20),
        name=kernel.__name__,
    )(*args)


def to_lanes(volts, stack, v_out, c_out, low_out, high_out):
    for x in range(8):
        field = load_rows(volts, x).T
        v_out[x] = field
        coef = stack[pl.ds(x, 16, stride=8), :]
        coef = jnp.concatenate([coef, jnp.zeros((112, 128), F32)], axis=0).T
        c_out[x] = coef
        low_out[x * 8 : x * 8 + 8, :] = field[:8]
        low_out[64 + x * 8 : 72 + x * 8, :] = coef[:8]
        high_out[x * 8 : x * 8 + 8, :] = field[120:]
        high_out[64 + x * 8 : 72 + x * 8, :] = coef[120:]


def inside(axis):
    me = lax.axis_index(axis)
    return (me > 0).astype(F32), (me < lax.axis_size(axis) - 1).astype(F32)


def widened(low, own, high, x, base=0):
    at = pl.ds(pl.multiple_of(base + x * 8, 8), 8)
    low_in, high_in = inside(GY)
    return jnp.concatenate([low[at, :] * low_in, own[x], high[at, :] * high_in], axis=0)


def pack_rows(v, c, low, high, first_out, last_out):
    for x in range(8):
        field = widened(low, v, high, x)
        coef = widened(low, c, high, x, 64)
        packed = coef[:24]
        for g in range(1, 6):
            packed = packed + pltpu.roll(coef[g * 24 : (g + 1) * 24], 16 * g, 1)
        row = jnp.concatenate([field, packed], axis=0)
        if x < 7:
            first_out[x] = row
        if x > 0:
            last_out[x - 1] = row


def place_slots(listed, amps, out, acc):
    acc[...] = jnp.zeros_like(acc)
    lane = iota((128, 256), 1)
    before = ((iota((128, 256), 0) < lane) | (lane >= 128)).astype(F32).astype(BF16)
    tile_line = iota((128, 128), 0)

    def chunk(turn, seen):
        at = pl.ds(pl.multiple_of(turn * 8, 8), 8)
        tiles = listed[at, :]
        cells = listed[pl.ds(pl.multiple_of(64 + turn * 8, 8), 8), :]
        code = cells * 64 + listed[pl.ds(pl.multiple_of(128 + turn * 8, 8), 8), :]
        parts = list(split2(amps[at, :]))
        parts.append((code >> 8).astype(F32).astype(BF16))
        parts.append((code & 255).astype(F32).astype(BF16))
        hits = [
            (tile_line == tiles[j : j + 1, :]).astype(F32) for j in range(8)
        ]
        hits_b = [h.astype(BF16) for h in hits]
        ranks = dot(jnp.concatenate(hits_b, axis=0), before, ((1,), (0,)))
        slots = []
        for j in range(8):
            rank = ranks[j * 128 : (j + 1) * 128]
            slot = jnp.sum(hits[j] * (rank[:, :128] + seen), axis=0, keepdims=True)
            slots.append((tile_line == slot.astype(jnp.int32)).astype(F32).astype(BF16))
            seen = seen + rank[:, 128:]
        hit = jnp.concatenate(hits_b, axis=1)
        slot = jnp.concatenate(slots, axis=1)
        left = []
        for part in parts:
            wide = part.astype(F32)
            wide = jnp.concatenate([wide[j : j + 1, :] for j in range(8)], axis=1)
            left.append(hit * wide.astype(BF16))
        acc[...] += dot(jnp.concatenate(left, axis=0), slot, ((1,), (1,)))
        return seen

    lax.fori_loop(0, 8, chunk, jnp.zeros((128, 128), F32), unroll=8)
    out[:, 0, :] = acc[0:128] + acc[128:256]
    out[:, 1, :] = acc[256:384] * 256.0 + acc[384:512]


def add_currents(slots, waves, out, low_out, high_out, acc):
    acc[...] = jnp.zeros_like(acc)
    table = jnp.concatenate([p.astype(F32) for p in split3(waves[...])], axis=1).astype(BF16)
    wave_line = iota((64, 4096), 0).astype(F32).astype(BF16)
    cell_line = iota((256, 4096), 0).astype(F32).astype(BF16)
    one, zero = jnp.ones((), BF16), jnp.zeros((), BF16)

    def chunk(turn, carry):
        rows = [slots[turn * 32 + j] for j in range(32)]
        amp = jnp.concatenate([r[0:1, :] for r in rows], axis=1)
        code = jnp.concatenate([r[1:2, :] for r in rows], axis=1).astype(jnp.int32)
        hit = jnp.where(wave_line == (code & 63).astype(F32).astype(BF16), one, zero)
        picked = dot(table, jnp.concatenate([hit, hit, hit], axis=0), ((1,), (0,)))
        current = (picked * amp).astype(BF16)
        cell = code >> 6
        block = (cell >> 8).astype(F32).astype(BF16)
        right = [jnp.where(block == jnp.array(r, BF16), current, zero) for r in range(4)]
        left = jnp.where(cell_line == (cell & 255).astype(F32).astype(BF16), one, zero)
        acc[...] += dot(left, jnp.concatenate(right, axis=0), ((1,), (1,)))
        return carry

    lax.fori_loop(0, 4, chunk, 0, unroll=4)
    low_lanes = iota((256, 128), 1) < 64
    for r in range(4):
        half = acc[:, (r // 2) * 128 : (r // 2 + 1) * 128]
        if r % 2:
            half = pltpu.roll(half, 64, 1)
        half = jnp.where(low_lanes, half, 0.0)
        for b in range(2):
            x = 2 * r + b
            rows = half[b * 128 : (b + 1) * 128]
            out[x] = rows
            low_out[x * 8 : x * 8 + 8, :] = rows[:8]
            high_out[x * 8 : x * 8 + 8, :] = rows[120:]


def pack_injected(own, low, high, first_out, last_out):
    rows = [widened(low, own, high, x) for x in range(8)]
    for j in range(3):
        first_out[j] = rows[j] + pltpu.roll(rows[j + 3], 64, 1)
        last_out[j] = rows[j + 2] + pltpu.roll(rows[j + 5], 64, 1)


def apply_row(src, i, diag, wx, wy, wv):
    v = src[i]
    wyi, wvi = wy[i], wv[i]
    out = diag[i] * v - wx[i] * src[i + 1] - wx[i - 1] * src[i - 1]
    out = out - wyi * pltpu.roll(v, YE - 1, 0) - pltpu.roll(wyi * v, 1, 0)
    return out - wvi * pltpu.roll(v, 96, 1) - pltpu.roll(wvi * v, 32, 1)


def power(src, dst, first, last, weights):
    def row(i, carry):
        dst[i] = apply_row(src, i, *weights)
        return carry

    lax.fori_loop(first, last + 1, row, 0, unroll=4)


def moments(fields, out, first):
    own = [f[first : first + 8, 8:136, :].reshape(1024, 128) for f in fields]
    lane, row = iota((32, 128), 1), iota((32, 128), 0)
    packed = jnp.zeros((32, 128), F32)
    parts = [split2(f) for f in own]
    for k in range(3):
        (hi, lo), (next_hi, next_lo) = parts[k], parts[k + 1]
        left = jnp.concatenate([hi, lo], axis=1)
        product = dot(left, jnp.concatenate([hi, next_hi], axis=1), ((0,), (0,)))
        cross = dot(hi, jnp.concatenate([lo, next_lo], axis=1), ((0,), (0,)))
        product = product[:128] + product[128:] + cross
        column = lane - 32 * k
        totals = []
        for b in range(2):
            total = jnp.zeros((32, 128), F32)
            for l in range(4):
                piece = product[l * 32 : (l + 1) * 32, b * 128 : (b + 1) * 128]
                turn = (32 * (k - l)) % 128
                total = total + (pltpu.roll(piece, turn, 1) if turn else piece)
            totals.append(total)
        even, odd = totals
        inside = (column >= 0) & (column < 32)
        packed = packed + jnp.where(inside, jnp.where(column > row, even, odd), 0.0)
        diagonal = jnp.sum(jnp.where(column == row, even, 0.0), axis=1, keepdims=True)
        packed = packed + jnp.where(lane == 96 + k, diagonal, 0.0)
    out[...] = packed


def coefficients(gram):
    lane, row = iota((32, 128), 1), iota((32, 128), 0)
    sums = [gram[n] for n in range(gram.shape[0])]
    while len(sums) > 1:
        sums = [a + b for a, b in zip(sums[::2], sums[1::2])]
    packed = sums[0]
    flipped = jnp.concatenate([packed, jnp.zeros((96, 128), F32)], axis=0).T
    bases = []
    for k in range(3):
        direct = pltpu.roll(packed, 128 - 32 * k, 1) if k else packed
        mirror = flipped[k * 32 : (k + 1) * 32, :]
        even = jnp.where(lane > row, direct, mirror)
        even = jnp.where(lane == row, packed[:, 96 + k : 97 + k], even)
        bases.append(jnp.where(lane < 32, even, 0.0))
        odd = jnp.where(lane > row, mirror, direct)
        bases.append(jnp.where(lane < 32, odd, 0.0))

    def moment(k, place):
        return pltpu.roll(bases[k], place, 1) if place else bases[k]

    tiles = []
    for i in range(3):
        block = moment(i, 96)
        for j in range(3):
            block = block + SCALE * moment(i + j + 1, 32 * j) + SHIFT * moment(i + j, 32 * j)
        tiles += [block[r * 8 : r * 8 + 8] for r in range(4)]
    sub = iota((8, 128), 0)
    for t in range(12):
        rows = tiles[t]
        cols = [jnp.broadcast_to(rows[:, t * 8 + j : t * 8 + j + 1], (8, 128)) for j in range(8)]
        for j in range(8):
            inverse = 1.0 / cols[j][j : j + 1, :]
            pivot = rows[j : j + 1, :] * inverse
            rows = jnp.where(sub == j, pivot, rows - cols[j] * pivot)
            for n in range(j + 1, 8):
                top = cols[n][j : j + 1, :] * inverse
                cols[n] = jnp.where(sub == j, top, cols[n] - cols[j] * top)
        for i in range(12):
            block = tiles[i]
            for j in range(8):
                if i != t:
                    block = block - tiles[i][:, t * 8 + j : t * 8 + j + 1] * rows[j : j + 1, :]
            tiles[i] = block
        tiles[t] = rows
    lane = iota((32, 128), 1)
    outs = []
    for i in range(3):
        y = jnp.concatenate(tiles[i * 4 : i * 4 + 4], axis=0)
        y = jnp.where(lane >= 96, y, 0.0)
        y = y + pltpu.roll(y, 32, 1) + pltpu.roll(y, 64, 1) + pltpu.roll(y, 96, 1)
        outs.append(
            jnp.concatenate([jnp.where(lane // 32 == l, y, 0.0) for l in range(4)], axis=0)
        )
    return outs


def combination(gram):
    y0, y1, y2 = coefficients(gram)
    step = jnp.concatenate([y0, y1, y2, jnp.zeros_like(y0)], axis=0)
    less = jnp.concatenate(
        [
            -SHIFT * y0,
            -SCALE * y0 - SHIFT * y1,
            -SCALE * y1 - SHIFT * y2,
            -SCALE * y2,
        ],
        axis=0,
    )
    return jnp.concatenate([step, less], axis=1)


def grid_weights(
    v, c, low, high, x_low, x_high, diag, wx, wy, wv, cap, free, ext,
):
    lane = iota((YE, 128), 1)
    n = iota((128, 512), 1)
    q = iota((128, 512), 0)
    spread = ((q % 16 == (n // 128) * 4 + (n % 128) // 32) & (q < 48)).astype(F32).astype(BF16)

    def expand(i, coef):
        hi, mid, lo = [p.astype(F32) for p in split3(coef)]
        parts = hi + pltpu.roll(mid, 16, 1) + pltpu.roll(lo, 32, 1)
        wide = dot(parts.astype(BF16), spread, ((1,), (0,)))
        cap[i] = wide[:, :128]
        wx[i] = wide[:, 128:256]
        wy[i] = wide[:, 256:384]
        wv[i] = wide[:, 384:]

    def halo_row(j, ref, base, present):
        ext[base + j] = ref[j, :YE, :] * present
        packed = ref[j, YE:, :] * present
        groups = [packed] + [pltpu.roll(packed, 128 - 16 * g, 1) for g in range(1, 6)]
        coef = jnp.concatenate(groups, axis=0)
        expand(base + j, jnp.where(lane < 16, coef, 0.0))

    def own_row(x, carry):
        ext[7 + x] = widened(low, v, high, x)
        expand(7 + x, widened(low, c, high, x, 64))
        return carry

    def halo_rows(j, carry):
        low_in, high_in = inside(GX)
        halo_row(j, x_low, 0, low_in)
        halo_row(j, x_high, 15, high_in)
        return carry

    lax.fori_loop(0, 8, own_row, 0, unroll=2)
    lax.fori_loop(0, 7, halo_rows, 0)

    scale = 1.0 / SCALE

    def edge_x(i):
        wx[i] = jnp.where(cap[i + 1] > 0, wx[i] * scale, 0.0)

    def weigh(i, carry):
        own, raw_x, raw_y, raw_v = cap[i], wx[i], wy[i], wv[i]
        edge_x(i)
        wyi = jnp.where(pltpu.roll(own, YE - 1, 0) > 0, raw_y * scale, 0.0)
        wvi = jnp.where(lane < 96, raw_v * scale, 0.0)
        wy[i], wv[i] = wyi, wvi
        total = (own + raw_x + raw_y + raw_v - SHIFT) * scale + wx[i - 1]
        diag[i] = total + pltpu.roll(wyi, 1, 0) + pltpu.roll(wvi, 32, 1)
        free[i] = (own - SHIFT) * ext[i] - SCALE * apply_row(ext, i, diag, wx, wy, wv)
        return carry

    edge_x(0)
    lax.fori_loop(1, 21, weigh, 0, unroll=2)


def first_basis(
    diag, wx, wy, wv, free, inj, i_low, i_high, ix_low, ix_high,
    change, v0, v1, v2, v3, gram,
):
    lane = iota((YE, 128), 1)
    weights = (diag, wx, wy, wv)

    def start(i, both):
        now = jnp.where(lane < 32, both, 0.0)
        then = jnp.where(lane < 32, pltpu.roll(both, 96, 1), 0.0)
        change[i] = now - then
        v0[i] = free[i] - now

    def own_start(x, carry):
        start(7 + x, widened(i_low, inj, i_high, x))
        return carry

    def halo_start(j, carry):
        low_in, high_in = inside(GX)
        for ref, base, present in ((ix_low, 1, low_in), (ix_high, 15, high_in)):
            both = ref[j] * present
            start(base + j, both)
            start(base + 3 + j, pltpu.roll(both, 64, 1))
        return carry

    lax.fori_loop(0, 8, own_start, 0)
    lax.fori_loop(0, 3, halo_start, 0)
    power(v0, v1, 2, 19, weights)
    power(v1, v2, 3, 18, weights)
    power(v2, v3, 4, 17, weights)
    moments((v0, v1, v2, v3), gram, 7)


def split_rows(v0, v1, v2, v3, hi_out, lo_out):
    def row(i, carry):
        for n, field in enumerate((v0, v1, v2, v3)):
            at = slice(n * 128, (n + 1) * 128)
            hi_out[i, :, at], lo_out[i, :, at] = split2(field[4 + i])
        return carry

    lax.fori_loop(0, 14, row, 0, unroll=2)


def second_basis(
    gram, diag, wx, wy, wv, cap, change, v0, hi, lo, step, b0, b1, b2, b3, gram_out
):
    weights = (diag, wx, wy, wv)
    mix_hi, mix_lo = split2(combination(gram))
    across = ((1,), (0,))

    def row(i, carry):
        both = dot(hi[i - 4], mix_hi, across) + dot(hi[i - 4], mix_lo, across)
        both = both + dot(lo[i - 4], mix_hi, across)
        moved = both[:, :128]
        step[i] = moved
        b0[i] = v0[i] + both[:, 128:] + cap[i] * moved + change[i]
        return carry

    lax.fori_loop(4, 18, row, 0, unroll=2)
    power(b0, b1, 5, 16, weights)
    power(b1, b2, 6, 15, weights)
    power(b2, b3, 7, 14, weights)
    moments((b0, b1, b2, b3), gram_out, 7)


def store_rows(out, x, value):
    for l in range(4):
        out[pl.ds(l * 8 + x, 32, stride=32), :] = value[l * 32 : (l + 1) * 32]


def load_rows(ref, x):
    return jnp.concatenate([ref[pl.ds(l * 8 + x, 32, stride=32), :] for l in range(4)], axis=0)


def from_lanes(step, b0, b1, b2, b3, volts, volts_out, residual_out, hi_out, lo_out):
    for x in range(8):
        volts_out[x] = load_rows(volts, x) + step[7 + x, 8:136, :].T
        for n, field in enumerate((b0, b1, b2, b3)):
            rows = field[7 + x, 8:136, :].T
            if n == 0:
                residual_out[x] = rows
            at = slice(n * 128, (n + 1) * 128)
            hi_out[x, at, :], lo_out[x, at, :] = split2(rows)


def finish(gram, hi, lo, volts, residual, volts_out, residual_out):
    mix_hi, mix_lo = split2(combination(gram).T)
    for x in range(0, 8, 2):
        field_hi = jnp.concatenate([hi[x], hi[x + 1]], axis=1)
        field_lo = jnp.concatenate([lo[x], lo[x + 1]], axis=1)
        across = ((1,), (0,))
        both = dot(mix_hi, field_hi, across) + dot(mix_hi, field_lo, across)
        both = both + dot(mix_lo, field_hi, across)
        for n in range(2):
            own = both[:, n * 128 : (n + 1) * 128]
            store_rows(volts_out, x + n, volts[x + n] + own[:128])
            store_rows(residual_out, x + n, residual[x + n] + own[128:])


def neighbours(to_low, to_high, axis):
    size = lax.axis_size(axis)
    up = [(i, (i + 1) % size) for i in range(size)]
    from_low = lax.ppermute(to_high, axis, up)
    return from_low, lax.ppermute(to_low, axis, [(b, a) for a, b in up])


def everywhere(x, beside=()):
    x = x + lax.ppermute(x, "gy_1", [(0, 1), (1, 0)])
    one, two, three = [
        lax.ppermute(x, "gy_0", [(i, i ^ k) for i in range(4)]) for k in (1, 2, 3)
    ]
    x = (x + one) + (two + three)
    x, beside = lax.optimization_barrier((x, beside))
    x = jnp.broadcast_to(x[None], (lax.axis_size(GX),) + x.shape)
    return lax.all_to_all(x, GX, split_axis=0, concat_axis=0, tiled=True), beside


def exchange(slots):
    return lax.all_to_all(slots, GX_GY, split_axis=0, concat_axis=0, tiled=True)


def body(volts, cap, cond_x, cond_y, via, waveforms, placement, cells, wave_ids, amps):
    vmem = pltpu.VMEM
    coefs = jnp.concatenate([a.reshape(32, 128) for a in (cap, cond_x, cond_y, via)], axis=0)
    v, c, y_low, y_high = call(
        to_lanes,
        [(8, 128, 128), (8, 128, 128), (128, 128), (128, 128)],
        [volts.reshape(1024, 128), coefs],
    )
    y_low, y_high = neighbours(y_low, y_high, GY)
    listed = [a.reshape(64, 128) for a in (placement, cells, wave_ids)]
    (slots,) = call(
        place_slots,
        [(128, 2, 128)],
        [jnp.concatenate(listed, axis=0), amps.reshape(64, 128)],
        [vmem((512, 128), F32)],
    )
    y_low, y_high, slots = lax.optimization_barrier((y_low, y_high, slots))
    x_low, x_high = call(pack_rows, [(7, 168, 128)] * 2, [v, c, y_low, y_high])
    x_low, x_high = neighbours(x_low, x_high, GX)
    slots = exchange(slots)
    inj, i_low, i_high = call(
        add_currents,
        [(8, 128, 128), (64, 128), (64, 128)],
        [slots, waveforms],
        [vmem((256, 256), F32)],
    )
    i_low, i_high = neighbours(i_low, i_high, GY)
    ix_low, ix_high = call(pack_injected, [(3, YE, 128)] * 2, [inj, i_low, i_high])
    ix_low, ix_high = neighbours(ix_low, ix_high, GX)
    wide = (XE, YE, 128)
    diag, wx, wy, wv, cap, free = call(
        grid_weights, [wide] * 6, [v, c, y_low, y_high, x_low, x_high], [vmem(wide, F32)]
    )
    *kept, gram = call(
        first_basis,
        [wide] * 5 + [(32, 128)],
        [diag, wx, wy, wv, free, inj, i_low, i_high, ix_low, ix_high],
    )
    change, *fields = kept
    halves = [jax.ShapeDtypeStruct((14, YE, 512), BF16)] * 2
    gram, (hi, lo) = everywhere(gram, call(split_rows, halves, fields))
    step, *basis, gram = call(
        second_basis,
        [wide] * 5 + [(32, 128)],
        [gram, diag, wx, wy, wv, cap, change, fields[0], hi, lo],
    )
    halves = [jax.ShapeDtypeStruct((8, 512, 128), BF16)] * 2
    so_far = call(
        from_lanes,
        [(8, 128, 128)] * 2 + halves,
        [step] + basis + [volts.reshape(1024, 128)],
    )
    gram, so_far = everywhere(gram, so_far)
    volts_so_far, residual, hi, lo = so_far
    outs = call(finish, [(1024, 128)] * 2, [gram, hi, lo, volts_so_far, residual])
    return tuple(o.reshape(volts.shape) for o in outs)


def solution(mesh):
    finer = Mesh(mesh.devices.reshape(4, 4, 4, 2), ("gx_0", "gx_1", "gy_0", "gy_1"))
    in_specs = (
        P(None, None, GX, GY),
        P(None, GX, GY),
        P(None, GX, GY),
        P(None, GX, GY),
        P(None, GX, GY),
        P(),
        P(GX_GY, None),
        P(GX_GY),
        P(GX_GY),
        P(GX_GY),
    )
    out_specs = (P(None, None, GX, GY), P(None, None, GX, GY))
    return jax.shard_map(body, mesh=finer, in_specs=in_specs, out_specs=out_specs, check_vma=False)
```

```python
import jax
import jax.numpy as jnp
from jax import lax
from jax.experimental import pallas as pl
from jax.experimental.pallas import tpu as pltpu
from jax.sharding import Mesh
from jax.sharding import PartitionSpec as P

GX = ("gx_0", "gx_1")
GY = ("gy_0", "gy_1")
GX_GY = GX + GY
F32 = jnp.float32
BF16 = jnp.bfloat16
SHIFT = 7.0
SCALE = 7.0
XE = 22
YE = 144


def iota(shape, dim):
    return lax.broadcasted_iota(jnp.int32, shape, dim)


def dot(a, b, dims):
    return lax.dot_general(a, b, (dims, ((), ())), preferred_element_type=F32)


def split2(x):
    hi = x.astype(BF16)
    return hi, (x - hi.astype(F32)).astype(BF16)


def split3(x):
    hi = x.astype(BF16)
    rest = x - hi.astype(F32)
    mid = rest.astype(BF16)
    return hi, mid, (rest - mid.astype(F32)).astype(BF16)


def call(kernel, outs, args, scratch=(), limit=14, in_specs=None):
    outs = [o if isinstance(o, jax.ShapeDtypeStruct) else jax.ShapeDtypeStruct(o, F32) for o in outs]
    specs = {} if in_specs is None else {"in_specs": in_specs}
    return pl.pallas_call(
        kernel,
        out_shape=tuple(outs),
        scratch_shapes=list(scratch),
        **specs,
        compiler_params=pltpu.CompilerParams(vmem_limit_bytes=limit << 20),
        name=kernel.__name__,
    )(*args)


def to_lanes(volts, stack, v_out, c_out, low_out, high_out):
    for x in range(8):
        field = load_rows(volts, x).T
        v_out[x] = field
        coef = stack[pl.ds(x, 16, stride=8), :]
        coef = jnp.concatenate([coef, jnp.zeros((112, 128), F32)], axis=0).T
        c_out[x] = coef
        low_out[x * 8 : x * 8 + 8, :] = field[:8]
        low_out[64 + x * 8 : 72 + x * 8, :] = coef[:8]
        high_out[x * 8 : x * 8 + 8, :] = field[120:]
        high_out[64 + x * 8 : 72 + x * 8, :] = coef[120:]


def inside(axis):
    me = lax.axis_index(axis)
    return (me > 0).astype(F32), (me < lax.axis_size(axis) - 1).astype(F32)


def widened(low, own, high, x, base=0):
    at = pl.ds(pl.multiple_of(base + x * 8, 8), 8)
    low_in, high_in = inside(GY)
    return jnp.concatenate([low[at, :] * low_in, own[x], high[at, :] * high_in], axis=0)


def pack_rows(v, c, low, high, first_out, last_out):
    for x in range(8):
        field = widened(low, v, high, x)
        coef = widened(low, c, high, x, 64)
        packed = coef[:24]
        for g in range(1, 6):
            packed = packed + pltpu.roll(coef[g * 24 : (g + 1) * 24], 16 * g, 1)
        row = jnp.concatenate([field, packed], axis=0)
        if x < 7:
            first_out[x] = row
        if x > 0:
            last_out[x - 1] = row


def place_slots(listed, amps, out, acc):
    acc[...] = jnp.zeros_like(acc)
    lane = iota((128, 256), 1)
    before = ((iota((128, 256), 0) < lane) | (lane >= 128)).astype(F32).astype(BF16)
    tile_line = iota((128, 128), 0)

    def chunk(turn, seen):
        at = pl.ds(pl.multiple_of(turn * 8, 8), 8)
        tiles = listed[at, :]
        cells = listed[pl.ds(pl.multiple_of(64 + turn * 8, 8), 8), :]
        code = cells * 64 + listed[pl.ds(pl.multiple_of(128 + turn * 8, 8), 8), :]
        parts = list(split2(amps[at, :]))
        parts.append((code >> 8).astype(F32).astype(BF16))
        parts.append((code & 255).astype(F32).astype(BF16))
        hits = [
            (tile_line == tiles[j : j + 1, :]).astype(F32) for j in range(8)
        ]
        hits_b = [h.astype(BF16) for h in hits]
        ranks = dot(jnp.concatenate(hits_b, axis=0), before, ((1,), (0,)))
        slots = []
        for j in range(8):
            rank = ranks[j * 128 : (j + 1) * 128]
            slot = jnp.sum(hits[j] * (rank[:, :128] + seen), axis=0, keepdims=True)
            slots.append((tile_line == slot.astype(jnp.int32)).astype(F32).astype(BF16))
            seen = seen + rank[:, 128:]
        hit = jnp.concatenate(hits_b, axis=1)
        slot = jnp.concatenate(slots, axis=1)
        left = []
        for part in parts:
            wide = part.astype(F32)
            wide = jnp.concatenate([wide[j : j + 1, :] for j in range(8)], axis=1)
            left.append(hit * wide.astype(BF16))
        acc[...] += dot(jnp.concatenate(left, axis=0), slot, ((1,), (1,)))
        return seen

    lax.fori_loop(0, 8, chunk, jnp.zeros((128, 128), F32), unroll=8)
    out[:, 0, :] = acc[0:128] + acc[128:256]
    out[:, 1, :] = acc[256:384] * 256.0 + acc[384:512]


def add_currents(slots, waves, out, low_out, high_out, acc):
    acc[...] = jnp.zeros_like(acc)
    table = jnp.concatenate([p.astype(F32) for p in split3(waves[...])], axis=1).astype(BF16)
    wave_line = iota((64, 4096), 0).astype(F32).astype(BF16)
    cell_line = iota((256, 4096), 0).astype(F32).astype(BF16)
    one, zero = jnp.ones((), BF16), jnp.zeros((), BF16)

    def chunk(turn, carry):
        rows = [slots[turn * 32 + j] for j in range(32)]
        amp = jnp.concatenate([r[0:1, :] for r in rows], axis=1)
        code = jnp.concatenate([r[1:2, :] for r in rows], axis=1).astype(jnp.int32)
        hit = jnp.where(wave_line == (code & 63).astype(F32).astype(BF16), one, zero)
        picked = dot(table, jnp.concatenate([hit, hit, hit], axis=0), ((1,), (0,)))
        current = (picked * amp).astype(BF16)
        cell = code >> 6
        block = (cell >> 8).astype(F32).astype(BF16)
        right = [jnp.where(block == jnp.array(r, BF16), current, zero) for r in range(4)]
        left = jnp.where(cell_line == (cell & 255).astype(F32).astype(BF16), one, zero)
        acc[...] += dot(left, jnp.concatenate(right, axis=0), ((1,), (1,)))
        return carry

    lax.fori_loop(0, 4, chunk, 0, unroll=4)
    low_lanes = iota((256, 128), 1) < 64
    for r in range(4):
        half = acc[:, (r // 2) * 128 : (r // 2 + 1) * 128]
        if r % 2:
            half = pltpu.roll(half, 64, 1)
        half = jnp.where(low_lanes, half, 0.0)
        for b in range(2):
            x = 2 * r + b
            rows = half[b * 128 : (b + 1) * 128]
            out[x] = rows
            low_out[x * 8 : x * 8 + 8, :] = rows[:8]
            high_out[x * 8 : x * 8 + 8, :] = rows[120:]


def pack_injected(own, low, high, first_out, last_out):
    rows = [widened(low, own, high, x) for x in range(8)]
    for j in range(3):
        first_out[j] = rows[j] + pltpu.roll(rows[j + 3], 64, 1)
        last_out[j] = rows[j + 2] + pltpu.roll(rows[j + 5], 64, 1)


def apply_row(src, i, diag, wx, wy, wv):
    v = src[i]
    wyi, wvi = wy[i], wv[i]
    out = diag[i] * v - wx[i] * src[i + 1] - wx[i - 1] * src[i - 1]
    out = out - wyi * pltpu.roll(v, YE - 1, 0) - pltpu.roll(wyi * v, 1, 0)
    return out - wvi * pltpu.roll(v, 96, 1) - pltpu.roll(wvi * v, 32, 1)


def power(src, dst, first, last, weights):
    def row(i, carry):
        dst[i] = apply_row(src, i, *weights)
        return carry

    lax.fori_loop(first, last + 1, row, 0, unroll=True)


def moments(fields, out, first):
    own = [f[first : first + 8, 8:136, :].reshape(1024, 128) for f in fields]
    lane, row = iota((32, 128), 1), iota((32, 128), 0)
    packed = jnp.zeros((32, 128), F32)
    parts = [split2(f) for f in own]
    for k in range(3):
        (hi, lo), (next_hi, next_lo) = parts[k], parts[k + 1]
        left = jnp.concatenate([hi, lo], axis=1)
        product = dot(left, jnp.concatenate([hi, next_hi], axis=1), ((0,), (0,)))
        cross = dot(hi, jnp.concatenate([lo, next_lo], axis=1), ((0,), (0,)))
        product = product[:128] + product[128:] + cross
        column = lane - 32 * k
        totals = []
        for b in range(2):
            total = jnp.zeros((32, 128), F32)
            for l in range(4):
                piece = product[l * 32 : (l + 1) * 32, b * 128 : (b + 1) * 128]
                turn = (32 * (k - l)) % 128
                total = total + (pltpu.roll(piece, turn, 1) if turn else piece)
            totals.append(total)
        even, odd = totals
        inside = (column >= 0) & (column < 32)
        packed = packed + jnp.where(inside, jnp.where(column > row, even, odd), 0.0)
        diagonal = jnp.sum(jnp.where(column == row, even, 0.0), axis=1, keepdims=True)
        packed = packed + jnp.where(lane == 96 + k, diagonal, 0.0)
    out[...] = packed


def coefficients(gram):
    lane, row = iota((32, 128), 1), iota((32, 128), 0)
    sums = [gram[n] for n in range(gram.shape[0])]
    while len(sums) > 1:
        sums = [a + b for a, b in zip(sums[::2], sums[1::2])]
    packed = sums[0]
    flipped = jnp.concatenate([packed, jnp.zeros((96, 128), F32)], axis=0).T
    bases = []
    for k in range(3):
        direct = pltpu.roll(packed, 128 - 32 * k, 1) if k else packed
        mirror = flipped[k * 32 : (k + 1) * 32, :]
        even = jnp.where(lane > row, direct, mirror)
        even = jnp.where(lane == row, packed[:, 96 + k : 97 + k], even)
        bases.append(jnp.where(lane < 32, even, 0.0))
        odd = jnp.where(lane > row, mirror, direct)
        bases.append(jnp.where(lane < 32, odd, 0.0))

    def moment(k, place):
        return pltpu.roll(bases[k], place, 1) if place else bases[k]

    tiles = []
    for i in range(3):
        block = moment(i, 96)
        for j in range(3):
            block = block + SCALE * moment(i + j + 1, 32 * j) + SHIFT * moment(i + j, 32 * j)
        tiles += [block[r * 8 : r * 8 + 8] for r in range(4)]
    sub = iota((8, 128), 0)
    for t in range(12):
        rows = tiles[t]
        cols = [jnp.broadcast_to(rows[:, t * 8 + j : t * 8 + j + 1], (8, 128)) for j in range(8)]
        for j in range(8):
            inverse = 1.0 / cols[j][j : j + 1, :]
            pivot = rows[j : j + 1, :] * inverse
            rows = jnp.where(sub == j, pivot, rows - cols[j] * pivot)
            for n in range(j + 1, 8):
                top = cols[n][j : j + 1, :] * inverse
                cols[n] = jnp.where(sub == j, top, cols[n] - cols[j] * top)
        for i in range(12):
            block = tiles[i]
            for j in range(8):
                if i != t:
                    block = block - tiles[i][:, t * 8 + j : t * 8 + j + 1] * rows[j : j + 1, :]
            tiles[i] = block
        tiles[t] = rows
    lane = iota((32, 128), 1)
    outs = []
    for i in range(3):
        y = jnp.concatenate(tiles[i * 4 : i * 4 + 4], axis=0)
        y = jnp.where(lane >= 96, y, 0.0)
        y = y + pltpu.roll(y, 32, 1) + pltpu.roll(y, 64, 1) + pltpu.roll(y, 96, 1)
        outs.append(
            jnp.concatenate([jnp.where(lane // 32 == l, y, 0.0) for l in range(4)], axis=0)
        )
    return outs


def combination(gram):
    y0, y1, y2 = coefficients(gram)
    step = jnp.concatenate([y0, y1, y2, jnp.zeros_like(y0)], axis=0)
    less = jnp.concatenate(
        [
            -SHIFT * y0,
            -SCALE * y0 - SHIFT * y1,
            -SCALE * y1 - SHIFT * y2,
            -SCALE * y2,
        ],
        axis=0,
    )
    return jnp.concatenate([step, less], axis=1)


def spreading():
    n, q = iota((128, 512), 1), iota((128, 512), 0)
    hit = (q % 16 == (n // 128) * 4 + (n % 128) // 32) & (q < 48)
    return hit.astype(F32).astype(BF16)


def expand(coef, spread, cap, wx, wy, wv, i):
    hi, mid, lo = [p.astype(F32) for p in split3(coef)]
    parts = hi + pltpu.roll(mid, 16, 1) + pltpu.roll(lo, 32, 1)
    wide = dot(parts.astype(BF16), spread, ((1,), (0,)))
    for n, out in enumerate((cap, wx, wy, wv)):
        out[i] = wide[:, n * 128 : (n + 1) * 128]


def weigh(i, ext, raw_x, diag, wx, wy, wv, cap, free):
    scale = 1.0 / SCALE
    own, raw_y, raw_v = cap[i], wy[i], wv[i]
    wyi = jnp.where(pltpu.roll(own, YE - 1, 0) > 0, raw_y * scale, 0.0)
    wvi = jnp.where(iota((YE, 128), 1) < 96, raw_v * scale, 0.0)
    wy[i], wv[i] = wyi, wvi
    total = (own + raw_x + raw_y + raw_v - SHIFT) * scale + wx[i - 1]
    diag[i] = total + pltpu.roll(wyi, 1, 0) + pltpu.roll(wvi, 32, 1)
    free[i] = (own - SHIFT) * ext[i] - SCALE * apply_row(ext, i, diag, wx, wy, wv)


def own_weights(v, c, low, high, diag, wx, wy, wv, cap, free, ext, scaled):
    spread = spreading()
    for x in range(8):
        ext[x] = widened(low, v, high, x)
        expand(widened(low, c, high, x, 64), spread, cap, wx, wy, wv, x)
        scaled[x] = wx[x] * (1.0 / SCALE)
    for x in (0, 7):
        diag[x] = jnp.zeros((YE, 128), F32)
        free[x] = jnp.zeros((YE, 128), F32)
    for x in range(1, 7):
        weigh(x, ext, wx[x], diag, scaled, wy, wv, cap, free)
        wx[x] = scaled[x]


def grid_weights(
    v, low, high, x_low, x_high, diag_in, wx_in, wy_in, wv_in, cap_in, free_in,
    diag, wx, wy, wv, cap, free, ext,
):
    lane = iota((YE, 128), 1)
    spread = spreading()
    for x in (0, 1, 6, 7):
        ext[7 + x] = widened(low, v, high, x)

    def own_row(x, carry):
        for src, dst in (
            (diag_in, diag), (wx_in, wx), (wy_in, wy), (wv_in, wv), (cap_in, cap), (free_in, free)
        ):
            dst[7 + x] = src[x]
        return carry

    def halo_row(j, ref, base, present):
        ext[base + j] = ref[j, :YE, :] * present
        packed = ref[j, YE:, :] * present
        groups = [packed] + [pltpu.roll(packed, 128 - 16 * g, 1) for g in range(1, 6)]
        coef = jnp.where(lane < 16, jnp.concatenate(groups, axis=0), 0.0)
        expand(coef, spread, cap, wx, wy, wv, base + j)

    def halo_rows(j, carry):
        low_in, high_in = inside(GX)
        halo_row(j, x_low, 0, low_in)
        halo_row(j, x_high, 15, high_in)
        return carry

    lax.fori_loop(0, 8, own_row, 0, unroll=True)
    lax.fori_loop(0, 7, halo_rows, 0, unroll=True)

    def edge_x(i):
        wx[i] = jnp.where(cap[i + 1] > 0, wx[i] * (1.0 / SCALE), 0.0)

    def row(i, carry):
        raw = wx[i]
        edge_x(i)
        weigh(i, ext, raw, diag, wx, wy, wv, cap, free)
        return carry

    edge_x(0)
    lax.fori_loop(1, 8, row, 0, unroll=True)
    lax.fori_loop(14, 21, row, 0, unroll=True)


def first_basis(
    diag, wx, wy, wv, free, inj, i_low, i_high, ix_low, ix_high,
    change, v0, v1, v2, v3, gram,
):
    lane = iota((YE, 128), 1)
    weights = (diag, wx, wy, wv)

    def start(i, both):
        now = jnp.where(lane < 32, both, 0.0)
        then = jnp.where(lane < 32, pltpu.roll(both, 96, 1), 0.0)
        change[i] = now - then
        v0[i] = free[i] - now

    def own_start(x, carry):
        start(7 + x, widened(i_low, inj, i_high, x))
        return carry

    def halo_start(j, carry):
        low_in, high_in = inside(GX)
        for ref, base, present in ((ix_low, 1, low_in), (ix_high, 15, high_in)):
            both = ref[j] * present
            start(base + j, both)
            start(base + 3 + j, pltpu.roll(both, 64, 1))
        return carry

    lax.fori_loop(0, 8, own_start, 0, unroll=True)
    lax.fori_loop(0, 3, halo_start, 0, unroll=True)
    power(v0, v1, 2, 19, weights)
    power(v1, v2, 3, 18, weights)
    power(v2, v3, 4, 17, weights)
    moments((v0, v1, v2, v3), gram, 7)


def split_rows(v0, v1, v2, v3, hi_out, lo_out):
    def row(i, carry):
        for n, field in enumerate((v0, v1, v2, v3)):
            at = slice(n * 128, (n + 1) * 128)
            hi_out[i, :, at], lo_out[i, :, at] = split2(field[4 + i])
        return carry

    lax.fori_loop(0, 14, row, 0, unroll=2)


def second_basis(
    gram, diag, wx, wy, wv, cap, change, v0, hi, lo, step, b0, b1, b2, b3, gram_out
):
    weights = (diag, wx, wy, wv)
    mix_hi, mix_lo = split2(combination(gram))
    across = ((1,), (0,))

    def row(i, carry):
        both = dot(hi[i - 4], mix_hi, across) + dot(hi[i - 4], mix_lo, across)
        both = both + dot(lo[i - 4], mix_hi, across)
        moved = both[:, :128]
        step[i] = moved
        b0[i] = v0[i] + both[:, 128:] + cap[i] * moved + change[i]
        return carry

    lax.fori_loop(4, 18, row, 0, unroll=True)
    power(b0, b1, 5, 16, weights)
    power(b1, b2, 6, 15, weights)
    power(b2, b3, 7, 14, weights)
    moments((b0, b1, b2, b3), gram_out, 7)


def store_rows(out, x, value):
    for l in range(4):
        out[pl.ds(l * 8 + x, 32, stride=32), :] = value[l * 32 : (l + 1) * 32]


def load_rows(ref, x):
    return jnp.concatenate([ref[pl.ds(l * 8 + x, 32, stride=32), :] for l in range(4)], axis=0)


def from_lanes(step, b0, b1, b2, b3, volts, volts_out, residual_out, hi_out, lo_out):
    for x in range(8):
        volts_out[x] = load_rows(volts, x) + step[7 + x, 8:136, :].T
        for n, field in enumerate((b0, b1, b2, b3)):
            rows = field[7 + x, 8:136, :].T
            if n == 0:
                residual_out[x] = rows
            at = slice(n * 128, (n + 1) * 128)
            hi_out[x, at, :], lo_out[x, at, :] = split2(rows)


def finish(gram, hi, lo, volts, residual, volts_out, residual_out):
    mix_hi, mix_lo = split2(combination(gram).T)
    for x in range(0, 8, 2):
        field_hi = jnp.concatenate([hi[x], hi[x + 1]], axis=1)
        field_lo = jnp.concatenate([lo[x], lo[x + 1]], axis=1)
        across = ((1,), (0,))
        both = dot(mix_hi, field_hi, across) + dot(mix_hi, field_lo, across)
        both = both + dot(mix_lo, field_hi, across)
        for n in range(2):
            own = both[:, n * 128 : (n + 1) * 128]
            store_rows(volts_out, x + n, volts[x + n] + own[:128])
            store_rows(residual_out, x + n, residual[x + n] + own[128:])


def neighbours(to_low, to_high, axis):
    size = lax.axis_size(axis)
    up = [(i, (i + 1) % size) for i in range(size)]
    from_low = lax.ppermute(to_high, axis, up)
    return from_low, lax.ppermute(to_low, axis, [(b, a) for a, b in up])


def everywhere(x, beside=()):
    x = x + lax.ppermute(x, "gy_1", [(0, 1), (1, 0)])
    one, two, three = [
        lax.ppermute(x, "gy_0", [(i, i ^ k) for i in range(4)]) for k in (1, 2, 3)
    ]
    x = (x + one) + (two + three)
    x, beside = lax.optimization_barrier((x, beside))
    x = jnp.broadcast_to(x[None], (lax.axis_size(GX),) + x.shape)
    return lax.all_to_all(x, GX, split_axis=0, concat_axis=0, tiled=True), beside


def exchange(slots):
    return lax.all_to_all(slots, GX_GY, split_axis=0, concat_axis=0, tiled=True)


def body(volts, cap, cond_x, cond_y, via, waveforms, placement, cells, wave_ids, amps):
    vmem = pltpu.VMEM
    coefs = jnp.concatenate([a.reshape(32, 128) for a in (cap, cond_x, cond_y, via)], axis=0)
    v, c, y_low, y_high = call(
        to_lanes,
        [(8, 128, 128), (8, 128, 128), (128, 128), (128, 128)],
        [volts.reshape(1024, 128), coefs],
    )
    y_low, y_high = neighbours(y_low, y_high, GY)
    listed = [a.reshape(64, 128) for a in (placement, cells, wave_ids)]
    (slots,) = call(
        place_slots,
        [(128, 2, 128)],
        [jnp.concatenate(listed, axis=0), amps.reshape(64, 128)],
        [vmem((512, 128), F32)],
    )
    y_low, y_high, slots = lax.optimization_barrier((y_low, y_high, slots))
    x_low, x_high = call(pack_rows, [(7, 168, 128)] * 2, [v, c, y_low, y_high])
    x_low, x_high = neighbours(x_low, x_high, GX)
    slots = exchange(slots)
    inj, i_low, i_high = call(
        add_currents,
        [(8, 128, 128), (64, 128), (64, 128)],
        [slots, waveforms],
        [vmem((256, 256), F32)],
    )
    i_low, i_high = neighbours(i_low, i_high, GY)
    tile = (8, YE, 128)
    v, c, y_low, y_high, inj = lax.optimization_barrier((v, c, y_low, y_high, inj))
    partial = call(
        own_weights, [tile] * 6, [v, c, y_low, y_high], [vmem(tile, F32), vmem(tile, F32)]
    )
    i_low, i_high, partial = lax.optimization_barrier((i_low, i_high, partial))
    ix_low, ix_high = call(pack_injected, [(3, YE, 128)] * 2, [inj, i_low, i_high])
    ix_low, ix_high = neighbours(ix_low, ix_high, GX)
    wide = (XE, YE, 128)
    diag, wx, wy, wv, cap, free = call(
        grid_weights,
        [wide] * 6,
        [v, y_low, y_high, x_low, x_high, *partial],
        [vmem(wide, F32)],
    )
    *kept, gram = call(
        first_basis,
        [wide] * 5 + [(32, 128)],
        [diag, wx, wy, wv, free, inj, i_low, i_high, ix_low, ix_high],
    )
    change, *fields = kept
    halves = [jax.ShapeDtypeStruct((14, YE, 512), BF16)] * 2
    gram, (hi, lo) = everywhere(gram, call(split_rows, halves, fields))
    step, *basis, gram = call(
        second_basis,
        [wide] * 5 + [(32, 128)],
        [gram, diag, wx, wy, wv, cap, change, fields[0], hi, lo],
    )
    halves = [jax.ShapeDtypeStruct((8, 512, 128), BF16)] * 2
    so_far = call(
        from_lanes,
        [(8, 128, 128)] * 2 + halves,
        [step] + basis + [volts.reshape(1024, 128)],
    )
    gram, so_far = everywhere(gram, so_far)
    volts_so_far, residual, hi, lo = so_far
    outs = call(finish, [(1024, 128)] * 2, [gram, hi, lo, volts_so_far, residual])
    return tuple(o.reshape(volts.shape) for o in outs)


def solution(mesh):
    finer = Mesh(mesh.devices.reshape(4, 4, 4, 2), ("gx_0", "gx_1", "gy_0", "gy_1"))
    in_specs = (
        P(None, None, GX, GY),
        P(None, GX, GY),
        P(None, GX, GY),
        P(None, GX, GY),
        P(None, GX, GY),
        P(),
        P(GX_GY, None),
        P(GX_GY),
        P(GX_GY),
        P(GX_GY),
    )
    out_specs = (P(None, None, GX, GY), P(None, None, GX, GY))
    return jax.shard_map(body, mesh=finer, in_specs=in_specs, out_specs=out_specs, check_vma=False)
```

```python
import jax
import jax.numpy as jnp
from jax import lax
from jax.experimental import pallas as pl
from jax.experimental.pallas import tpu as pltpu
from jax.sharding import Mesh
from jax.sharding import PartitionSpec as P

GX = ("gx_0", "gx_1")
GY = ("gy_0", "gy_1")
GX_GY = GX + GY
F32 = jnp.float32
BF16 = jnp.bfloat16
SHIFT = 7.0
SCALE = 7.0
XE = 22
YE = 144


def iota(shape, dim):
    return lax.broadcasted_iota(jnp.int32, shape, dim)


def dot(a, b, dims):
    return lax.dot_general(a, b, (dims, ((), ())), preferred_element_type=F32)


def split2(x):
    hi = x.astype(BF16)
    return hi, (x - hi.astype(F32)).astype(BF16)


def split3(x):
    hi = x.astype(BF16)
    rest = x - hi.astype(F32)
    mid = rest.astype(BF16)
    return hi, mid, (rest - mid.astype(F32)).astype(BF16)


def call(kernel, outs, args, scratch=(), limit=14, in_specs=None):
    outs = [o if isinstance(o, jax.ShapeDtypeStruct) else jax.ShapeDtypeStruct(o, F32) for o in outs]
    specs = {} if in_specs is None else {"in_specs": in_specs}
    return pl.pallas_call(
        kernel,
        out_shape=tuple(outs),
        scratch_shapes=list(scratch),
        **specs,
        compiler_params=pltpu.CompilerParams(vmem_limit_bytes=limit << 20),
        name=kernel.__name__,
    )(*args)


def to_lanes(volts, stack, v_out, c_out, low_out, high_out):
    for x in range(8):
        field = load_rows(volts, x).T
        v_out[x] = field
        coef = stack[pl.ds(x, 16, stride=8), :]
        coef = jnp.concatenate([coef, jnp.zeros((112, 128), F32)], axis=0).T
        c_out[x] = coef
        low_out[x * 8 : x * 8 + 8, :] = field[:8]
        low_out[64 + x * 8 : 72 + x * 8, :] = coef[:8]
        high_out[x * 8 : x * 8 + 8, :] = field[120:]
        high_out[64 + x * 8 : 72 + x * 8, :] = coef[120:]


def inside(axis):
    me = lax.axis_index(axis)
    return (me > 0).astype(F32), (me < lax.axis_size(axis) - 1).astype(F32)


def widened(low, own, high, x, base=0):
    at = pl.ds(pl.multiple_of(base + x * 8, 8), 8)
    low_in, high_in = inside(GY)
    return jnp.concatenate([low[at, :] * low_in, own[x], high[at, :] * high_in], axis=0)


def pack_rows(v, c, low, high, first_out, last_out):
    for x in range(8):
        field = widened(low, v, high, x)
        coef = widened(low, c, high, x, 64)
        packed = coef[:24]
        for g in range(1, 6):
            packed = packed + pltpu.roll(coef[g * 24 : (g + 1) * 24], 16 * g, 1)
        row = jnp.concatenate([field, packed], axis=0)
        if x < 7:
            first_out[x] = row
        if x > 0:
            last_out[x - 1] = row


def place_slots(listed, amps, out):
    lane = iota((128, 256), 1)
    before = ((iota((128, 256), 0) < lane) | (lane >= 128)).astype(F32).astype(BF16)
    tile_line = iota((128, 128), 0)

    lefts, rights = [], []
    seen = jnp.zeros((128, 128), F32)
    for turn in range(8):
        at = slice(turn * 8, turn * 8 + 8)
        tiles = listed[at, :]
        cells = listed[64 + turn * 8 : 72 + turn * 8, :]
        code = cells * 64 + listed[128 + turn * 8 : 136 + turn * 8, :]
        parts = list(split2(amps[at, :]))
        parts.append((code >> 8).astype(F32).astype(BF16))
        parts.append((code & 255).astype(F32).astype(BF16))
        hits = [
            (tile_line == tiles[j : j + 1, :]).astype(F32) for j in range(8)
        ]
        hits_b = [h.astype(BF16) for h in hits]
        ranks = dot(jnp.concatenate(hits_b, axis=0), before, ((1,), (0,)))
        slots = []
        for j in range(8):
            rank = ranks[j * 128 : (j + 1) * 128]
            slot = jnp.sum(hits[j] * (rank[:, :128] + seen), axis=0, keepdims=True)
            slots.append((tile_line == slot.astype(jnp.int32)).astype(F32).astype(BF16))
            seen = seen + rank[:, 128:]
        hit = jnp.concatenate(hits_b, axis=1)
        slot = jnp.concatenate(slots, axis=1)
        left = []
        for part in parts:
            wide = part.astype(F32)
            wide = jnp.concatenate([wide[j : j + 1, :] for j in range(8)], axis=1)
            left.append(hit * wide.astype(BF16))
        lefts.append(jnp.concatenate(left, axis=0))
        rights.append(slot)

    acc = dot(jnp.concatenate(lefts, axis=1), jnp.concatenate(rights, axis=1), ((1,), (1,)))
    out[:, 0, :] = acc[0:128] + acc[128:256]
    out[:, 1, :] = acc[256:384] * 256.0 + acc[384:512]


def add_currents(slots, waves, out, low_out, high_out, acc):
    acc[...] = jnp.zeros_like(acc)
    table = jnp.concatenate([p.astype(F32) for p in split3(waves[...])], axis=1).astype(BF16)
    wave_line = iota((64, 16384), 0).astype(F32).astype(BF16)
    cell_line = iota((256, 16384), 0).astype(F32).astype(BF16)
    one, zero = jnp.ones((), BF16), jnp.zeros((), BF16)

    def chunk(turn, carry):
        rows = [slots[turn * 128 + j] for j in range(128)]
        amp = jnp.concatenate([r[0:1, :] for r in rows], axis=1)
        code = jnp.concatenate([r[1:2, :] for r in rows], axis=1).astype(jnp.int32)
        hit = jnp.where(wave_line == (code & 63).astype(F32).astype(BF16), one, zero)
        picked = dot(table, jnp.concatenate([hit, hit, hit], axis=0), ((1,), (0,)))
        current = (picked * amp).astype(BF16)
        cell = code >> 6
        block = (cell >> 8).astype(F32).astype(BF16)
        right = [jnp.where(block == jnp.array(r, BF16), current, zero) for r in range(4)]
        left = jnp.where(cell_line == (cell & 255).astype(F32).astype(BF16), one, zero)
        acc[...] += dot(left, jnp.concatenate(right, axis=0), ((1,), (1,)))
        return carry

    lax.fori_loop(0, 1, chunk, 0, unroll=1)
    low_lanes = iota((256, 128), 1) < 64
    for r in range(4):
        half = acc[:, (r // 2) * 128 : (r // 2 + 1) * 128]
        if r % 2:
            half = pltpu.roll(half, 64, 1)
        half = jnp.where(low_lanes, half, 0.0)
        for b in range(2):
            x = 2 * r + b
            rows = half[b * 128 : (b + 1) * 128]
            out[x] = rows
            low_out[x * 8 : x * 8 + 8, :] = rows[:8]
            high_out[x * 8 : x * 8 + 8, :] = rows[120:]


def pack_injected(own, low, high, first_out, last_out):
    rows = [widened(low, own, high, x) for x in range(8)]
    for j in range(3):
        first_out[j] = rows[j] + pltpu.roll(rows[j + 3], 64, 1)
        last_out[j] = rows[j + 2] + pltpu.roll(rows[j + 5], 64, 1)


def apply_row(src, i, diag, wx, wy, wv):
    v = src[i]
    wyi, wvi = wy[i], wv[i]
    out = diag[i] * v - wx[i] * src[i + 1] - wx[i - 1] * src[i - 1]
    out = out - wyi * pltpu.roll(v, YE - 1, 0) - pltpu.roll(wyi * v, 1, 0)
    return out - wvi * pltpu.roll(v, 96, 1) - pltpu.roll(wvi * v, 32, 1)


def power(src, dst, first, last, weights):
    def row(i, carry):
        dst[i] = apply_row(src, i, *weights)
        return carry

    lax.fori_loop(first, last + 1, row, 0, unroll=True)


def moments(fields, out, first):
    own = [f[first : first + 8, 8:136, :].reshape(1024, 128) for f in fields]
    lane, row = iota((32, 128), 1), iota((32, 128), 0)
    packed = jnp.zeros((32, 128), F32)
    parts = [split2(f) for f in own]
    for k in range(3):
        (hi, lo), (next_hi, next_lo) = parts[k], parts[k + 1]
        left = jnp.concatenate([hi, lo], axis=1)
        product = dot(left, jnp.concatenate([hi, next_hi], axis=1), ((0,), (0,)))
        cross = dot(hi, jnp.concatenate([lo, next_lo], axis=1), ((0,), (0,)))
        product = product[:128] + product[128:] + cross
        column = lane - 32 * k
        totals = []
        for b in range(2):
            total = jnp.zeros((32, 128), F32)
            for l in range(4):
                piece = product[l * 32 : (l + 1) * 32, b * 128 : (b + 1) * 128]
                turn = (32 * (k - l)) % 128
                total = total + (pltpu.roll(piece, turn, 1) if turn else piece)
            totals.append(total)
        even, odd = totals
        inside = (column >= 0) & (column < 32)
        packed = packed + jnp.where(inside, jnp.where(column > row, even, odd), 0.0)
        diagonal = jnp.sum(jnp.where(column == row, even, 0.0), axis=1, keepdims=True)
        packed = packed + jnp.where(lane == 96 + k, diagonal, 0.0)
    out[...] = packed


def coefficients(gram):
    lane, row = iota((32, 128), 1), iota((32, 128), 0)
    sums = [gram[n] for n in range(gram.shape[0])]
    while len(sums) > 1:
        sums = [a + b for a, b in zip(sums[::2], sums[1::2])]
    packed = sums[0]
    flipped = jnp.concatenate([packed, jnp.zeros((96, 128), F32)], axis=0).T
    bases = []
    for k in range(3):
        direct = pltpu.roll(packed, 128 - 32 * k, 1) if k else packed
        mirror = flipped[k * 32 : (k + 1) * 32, :]
        even = jnp.where(lane > row, direct, mirror)
        even = jnp.where(lane == row, packed[:, 96 + k : 97 + k], even)
        bases.append(jnp.where(lane < 32, even, 0.0))
        odd = jnp.where(lane > row, mirror, direct)
        bases.append(jnp.where(lane < 32, odd, 0.0))

    def moment(k, place):
        return pltpu.roll(bases[k], place, 1) if place else bases[k]

    tiles = []
    for i in range(3):
        block = moment(i, 96)
        for j in range(3):
            block = block + SCALE * moment(i + j + 1, 32 * j) + SHIFT * moment(i + j, 32 * j)
        tiles += [block[r * 8 : r * 8 + 8] for r in range(4)]
    sub = iota((8, 128), 0)
    for t in range(12):
        rows = tiles[t]
        cols = [jnp.broadcast_to(rows[:, t * 8 + j : t * 8 + j + 1], (8, 128)) for j in range(8)]
        for j in range(8):
            inverse = 1.0 / cols[j][j : j + 1, :]
            pivot = rows[j : j + 1, :] * inverse
            rows = jnp.where(sub == j, pivot, rows - cols[j] * pivot)
            for n in range(j + 1, 8):
                top = cols[n][j : j + 1, :] * inverse
                cols[n] = jnp.where(sub == j, top, cols[n] - cols[j] * top)
        for i in range(12):
            block = tiles[i]
            for j in range(8):
                if i != t:
                    block = block - tiles[i][:, t * 8 + j : t * 8 + j + 1] * rows[j : j + 1, :]
            tiles[i] = block
        tiles[t] = rows
    lane = iota((32, 128), 1)
    outs = []
    for i in range(3):
        y = jnp.concatenate(tiles[i * 4 : i * 4 + 4], axis=0)
        y = jnp.where(lane >= 96, y, 0.0)
        y = y + pltpu.roll(y, 32, 1) + pltpu.roll(y, 64, 1) + pltpu.roll(y, 96, 1)
        outs.append(
            jnp.concatenate([jnp.where(lane // 32 == l, y, 0.0) for l in range(4)], axis=0)
        )
    return outs


def combination(gram):
    y0, y1, y2 = coefficients(gram)
    step = jnp.concatenate([y0, y1, y2, jnp.zeros_like(y0)], axis=0)
    less = jnp.concatenate(
        [
            -SHIFT * y0,
            -SCALE * y0 - SHIFT * y1,
            -SCALE * y1 - SHIFT * y2,
            -SCALE * y2,
        ],
        axis=0,
    )
    return jnp.concatenate([step, less], axis=1)


def spreading():
    n, q = iota((128, 512), 1), iota((128, 512), 0)
    hit = (q % 16 == (n // 128) * 4 + (n % 128) // 32) & (q < 48)
    return hit.astype(F32).astype(BF16)


def expand(coef, spread, cap, wx, wy, wv, i):
    hi, mid, lo = [p.astype(F32) for p in split3(coef)]
    parts = hi + pltpu.roll(mid, 16, 1) + pltpu.roll(lo, 32, 1)
    wide = dot(parts.astype(BF16), spread, ((1,), (0,)))
    for n, out in enumerate((cap, wx, wy, wv)):
        out[i] = wide[:, n * 128 : (n + 1) * 128]


def weigh(i, ext, raw_x, diag, wx, wy, wv, cap, free):
    scale = 1.0 / SCALE
    own, raw_y, raw_v = cap[i], wy[i], wv[i]
    wyi = jnp.where(pltpu.roll(own, YE - 1, 0) > 0, raw_y * scale, 0.0)
    wvi = jnp.where(iota((YE, 128), 1) < 96, raw_v * scale, 0.0)
    wy[i], wv[i] = wyi, wvi
    total = (own + raw_x + raw_y + raw_v - SHIFT) * scale + wx[i - 1]
    diag[i] = total + pltpu.roll(wyi, 1, 0) + pltpu.roll(wvi, 32, 1)
    free[i] = (own - SHIFT) * ext[i] - SCALE * apply_row(ext, i, diag, wx, wy, wv)


def own_weights(v, c, low, high, diag, wx, wy, wv, cap, free, ext, scaled):
    spread = spreading()
    for x in range(8):
        ext[x] = widened(low, v, high, x)
        expand(widened(low, c, high, x, 64), spread, cap, wx, wy, wv, x)
        scaled[x] = wx[x] * (1.0 / SCALE)
    for x in (0, 7):
        diag[x] = jnp.zeros((YE, 128), F32)
        free[x] = jnp.zeros((YE, 128), F32)
    for x in range(1, 7):
        weigh(x, ext, wx[x], diag, scaled, wy, wv, cap, free)
        wx[x] = scaled[x]


def grid_weights(
    v, low, high, x_low, x_high, diag_in, wx_in, wy_in, wv_in, cap_in, free_in,
    diag, wx, wy, wv, cap, free, ext,
):
    lane = iota((YE, 128), 1)
    spread = spreading()
    for x in (0, 1, 6, 7):
        ext[7 + x] = widened(low, v, high, x)

    def own_row(x, carry):
        for src, dst in (
            (diag_in, diag), (wx_in, wx), (wy_in, wy), (wv_in, wv), (cap_in, cap), (free_in, free)
        ):
            dst[7 + x] = src[x]
        return carry

    def halo_row(j, ref, base, present):
        ext[base + j] = ref[j, :YE, :] * present
        packed = ref[j, YE:, :] * present
        groups = [packed] + [pltpu.roll(packed, 128 - 16 * g, 1) for g in range(1, 6)]
        coef = jnp.where(lane < 16, jnp.concatenate(groups, axis=0), 0.0)
        expand(coef, spread, cap, wx, wy, wv, base + j)

    def halo_rows(j, carry):
        low_in, high_in = inside(GX)
        halo_row(j, x_low, 0, low_in)
        halo_row(j, x_high, 15, high_in)
        return carry

    lax.fori_loop(0, 8, own_row, 0, unroll=True)
    lax.fori_loop(0, 7, halo_rows, 0, unroll=True)

    def edge_x(i):
        wx[i] = jnp.where(cap[i + 1] > 0, wx[i] * (1.0 / SCALE), 0.0)

    def row(i, carry):
        raw = wx[i]
        edge_x(i)
        weigh(i, ext, raw, diag, wx, wy, wv, cap, free)
        return carry

    edge_x(0)
    lax.fori_loop(1, 8, row, 0, unroll=True)
    lax.fori_loop(14, 21, row, 0, unroll=True)


def first_basis(
    diag, wx, wy, wv, free, inj, i_low, i_high, ix_low, ix_high,
    change, v0, v1, v2, v3, gram,
):
    lane = iota((YE, 128), 1)
    weights = (diag, wx, wy, wv)

    def start(i, both):
        now = jnp.where(lane < 32, both, 0.0)
        then = jnp.where(lane < 32, pltpu.roll(both, 96, 1), 0.0)
        change[i] = now - then
        v0[i] = free[i] - now

    def own_start(x, carry):
        start(7 + x, widened(i_low, inj, i_high, x))
        return carry

    def halo_start(j, carry):
        low_in, high_in = inside(GX)
        for ref, base, present in ((ix_low, 1, low_in), (ix_high, 15, high_in)):
            both = ref[j] * present
            start(base + j, both)
            start(base + 3 + j, pltpu.roll(both, 64, 1))
        return carry

    lax.fori_loop(0, 8, own_start, 0, unroll=True)
    lax.fori_loop(0, 3, halo_start, 0, unroll=True)
    power(v0, v1, 2, 19, weights)
    power(v1, v2, 3, 18, weights)
    power(v2, v3, 4, 17, weights)
    moments((v0, v1, v2, v3), gram, 7)


def split_rows(v0, v1, v2, v3, hi_out, lo_out):
    def row(i, carry):
        for n, field in enumerate((v0, v1, v2, v3)):
            at = slice(n * 128, (n + 1) * 128)
            hi_out[i, :, at], lo_out[i, :, at] = split2(field[4 + i])
        return carry

    lax.fori_loop(0, 14, row, 0, unroll=2)


def second_basis(
    gram, diag, wx, wy, wv, cap, change, v0, hi, lo, step, b0, b1, b2, b3, gram_out
):
    weights = (diag, wx, wy, wv)
    mix_hi, mix_lo = split2(combination(gram))
    across = ((1,), (0,))

    def row(i, carry):
        both = dot(hi[i - 4], mix_hi, across) + dot(hi[i - 4], mix_lo, across)
        both = both + dot(lo[i - 4], mix_hi, across)
        moved = both[:, :128]
        step[i] = moved
        b0[i] = v0[i] + both[:, 128:] + cap[i] * moved + change[i]
        return carry

    lax.fori_loop(4, 18, row, 0, unroll=True)
    power(b0, b1, 5, 16, weights)
    power(b1, b2, 6, 15, weights)
    power(b2, b3, 7, 14, weights)
    moments((b0, b1, b2, b3), gram_out, 7)


def store_rows(out, x, value):
    for l in range(4):
        out[pl.ds(l * 8 + x, 32, stride=32), :] = value[l * 32 : (l + 1) * 32]


def load_rows(ref, x):
    return jnp.concatenate([ref[pl.ds(l * 8 + x, 32, stride=32), :] for l in range(4)], axis=0)


def from_lanes(step, b0, b1, b2, b3, volts, volts_out, residual_out, hi_out, lo_out):
    for x in range(8):
        volts_out[x] = load_rows(volts, x) + step[7 + x, 8:136, :].T
        for n, field in enumerate((b0, b1, b2, b3)):
            rows = field[7 + x, 8:136, :].T
            if n == 0:
                residual_out[x] = rows
            at = slice(n * 128, (n + 1) * 128)
            hi_out[x, at, :], lo_out[x, at, :] = split2(rows)


def finish(gram, hi, lo, volts, residual, volts_out, residual_out):
    mix_hi, mix_lo = split2(combination(gram).T)
    for x in range(0, 8, 2):
        field_hi = jnp.concatenate([hi[x], hi[x + 1]], axis=1)
        field_lo = jnp.concatenate([lo[x], lo[x + 1]], axis=1)
        across = ((1,), (0,))
        both = dot(mix_hi, field_hi, across) + dot(mix_hi, field_lo, across)
        both = both + dot(mix_lo, field_hi, across)
        for n in range(2):
            own = both[:, n * 128 : (n + 1) * 128]
            store_rows(volts_out, x + n, volts[x + n] + own[:128])
            store_rows(residual_out, x + n, residual[x + n] + own[128:])


def neighbours(to_low, to_high, axis):
    size = lax.axis_size(axis)
    up = [(i, (i + 1) % size) for i in range(size)]
    from_low = lax.ppermute(to_high, axis, up)
    return from_low, lax.ppermute(to_low, axis, [(b, a) for a, b in up])


def everywhere(x, beside=()):
    x = x + lax.ppermute(x, "gy_1", [(0, 1), (1, 0)])
    one, two, three = [
        lax.ppermute(x, "gy_0", [(i, i ^ k) for i in range(4)]) for k in (1, 2, 3)
    ]
    x = (x + one) + (two + three)
    x, beside = lax.optimization_barrier((x, beside))
    x = jnp.broadcast_to(x[None], (lax.axis_size(GX),) + x.shape)
    return lax.all_to_all(x, GX, split_axis=0, concat_axis=0, tiled=True), beside


def exchange(slots):
    return lax.all_to_all(slots, GX_GY, split_axis=0, concat_axis=0, tiled=True)


def body(volts, cap, cond_x, cond_y, via, waveforms, placement, cells, wave_ids, amps):
    vmem = pltpu.VMEM
    coefs = jnp.concatenate([a.reshape(32, 128) for a in (cap, cond_x, cond_y, via)], axis=0)
    v, c, y_low, y_high = call(
        to_lanes,
        [(8, 128, 128), (8, 128, 128), (128, 128), (128, 128)],
        [volts.reshape(1024, 128), coefs],
    )
    y_low, y_high = neighbours(y_low, y_high, GY)
    listed = [a.reshape(64, 128) for a in (placement, cells, wave_ids)]
    (slots,) = call(
        place_slots,
        [(128, 2, 128)],
        [jnp.concatenate(listed, axis=0), amps.reshape(64, 128)],
    )
    y_low, y_high, slots = lax.optimization_barrier((y_low, y_high, slots))
    x_low, x_high = call(pack_rows, [(7, 168, 128)] * 2, [v, c, y_low, y_high])
    x_low, x_high = neighbours(x_low, x_high, GX)
    slots = exchange(slots)
    inj, i_low, i_high = call(
        add_currents,
        [(8, 128, 128), (64, 128), (64, 128)],
        [slots, waveforms],
        [vmem((256, 256), F32)],
    )
    i_low, i_high = neighbours(i_low, i_high, GY)
    tile = (8, YE, 128)
    v, c, y_low, y_high, inj = lax.optimization_barrier((v, c, y_low, y_high, inj))
    partial = call(
        own_weights, [tile] * 6, [v, c, y_low, y_high], [vmem(tile, F32), vmem(tile, F32)]
    )
    i_low, i_high, partial = lax.optimization_barrier((i_low, i_high, partial))
    ix_low, ix_high = call(pack_injected, [(3, YE, 128)] * 2, [inj, i_low, i_high])
    ix_low, ix_high = neighbours(ix_low, ix_high, GX)
    wide = (XE, YE, 128)
    diag, wx, wy, wv, cap, free = call(
        grid_weights,
        [wide] * 6,
        [v, y_low, y_high, x_low, x_high, *partial],
        [vmem(wide, F32)],
    )
    *kept, gram = call(
        first_basis,
        [wide] * 5 + [(32, 128)],
        [diag, wx, wy, wv, free, inj, i_low, i_high, ix_low, ix_high],
    )
    change, *fields = kept
    halves = [jax.ShapeDtypeStruct((14, YE, 512), BF16)] * 2
    gram, (hi, lo) = everywhere(gram, call(split_rows, halves, fields))
    step, *basis, gram = call(
        second_basis,
        [wide] * 5 + [(32, 128)],
        [gram, diag, wx, wy, wv, cap, change, fields[0], hi, lo],
    )
    halves = [jax.ShapeDtypeStruct((8, 512, 128), BF16)] * 2
    so_far = call(
        from_lanes,
        [(8, 128, 128)] * 2 + halves,
        [step] + basis + [volts.reshape(1024, 128)],
    )
    gram, so_far = everywhere(gram, so_far)
    volts_so_far, residual, hi, lo = so_far
    outs = call(finish, [(1024, 128)] * 2, [gram, hi, lo, volts_so_far, residual])
    return tuple(o.reshape(volts.shape) for o in outs)


def solution(mesh):
    finer = Mesh(mesh.devices.reshape(4, 4, 4, 2), ("gx_0", "gx_1", "gy_0", "gy_1"))
    in_specs = (
        P(None, None, GX, GY),
        P(None, GX, GY),
        P(None, GX, GY),
        P(None, GX, GY),
        P(None, GX, GY),
        P(),
        P(GX_GY, None),
        P(GX_GY),
        P(GX_GY),
        P(GX_GY),
    )
    out_specs = (P(None, None, GX, GY), P(None, None, GX, GY))
    return jax.shard_map(body, mesh=finer, in_specs=in_specs, out_specs=out_specs, check_vma=False)
```

```python
import jax
import jax.numpy as jnp
from jax import lax
from jax.experimental import pallas as pl
from jax.experimental.pallas import tpu as pltpu
from jax.sharding import Mesh
from jax.sharding import PartitionSpec as P

GX = ("gx_0", "gx_1")
GY = ("gy_0", "gy_1")
GX_GY = GX + GY
F32 = jnp.float32
BF16 = jnp.bfloat16
SHIFT = 7.0
SCALE = 7.0
XE = 22
YE = 144


def iota(shape, dim):
    return lax.broadcasted_iota(jnp.int32, shape, dim)


def dot(a, b, dims):
    return lax.dot_general(a, b, (dims, ((), ())), preferred_element_type=F32)


def split2(x):
    hi = x.astype(BF16)
    return hi, (x - hi.astype(F32)).astype(BF16)


def split3(x):
    hi = x.astype(BF16)
    rest = x - hi.astype(F32)
    mid = rest.astype(BF16)
    return hi, mid, (rest - mid.astype(F32)).astype(BF16)


def call(kernel, outs, args, scratch=(), limit=14, in_specs=None):
    outs = [o if isinstance(o, jax.ShapeDtypeStruct) else jax.ShapeDtypeStruct(o, F32) for o in outs]
    specs = {} if in_specs is None else {"in_specs": in_specs}
    return pl.pallas_call(
        kernel,
        out_shape=tuple(outs),
        scratch_shapes=list(scratch),
        **specs,
        compiler_params=pltpu.CompilerParams(vmem_limit_bytes=limit << 20),
        name=kernel.__name__,
    )(*args)


def to_lanes(volts, stack, v_out, c_out, low_out, high_out):
    for x in range(8):
        field = load_rows(volts, x).T
        v_out[x] = field
        coef = stack[pl.ds(x, 16, stride=8), :]
        coef = jnp.concatenate([coef, jnp.zeros((112, 128), F32)], axis=0).T
        c_out[x] = coef
        low_out[x * 8 : x * 8 + 8, :] = field[:8]
        low_out[64 + x * 8 : 72 + x * 8, :] = coef[:8]
        high_out[x * 8 : x * 8 + 8, :] = field[120:]
        high_out[64 + x * 8 : 72 + x * 8, :] = coef[120:]


def inside(axis):
    me = lax.axis_index(axis)
    return (me > 0).astype(F32), (me < lax.axis_size(axis) - 1).astype(F32)


def widened(low, own, high, x, base=0):
    at = pl.ds(pl.multiple_of(base + x * 8, 8), 8)
    low_in, high_in = inside(GY)
    return jnp.concatenate([low[at, :] * low_in, own[x], high[at, :] * high_in], axis=0)


def pack_rows(v, c, low, high, first_out, last_out):
    for x in range(8):
        field = widened(low, v, high, x)
        coef = widened(low, c, high, x, 64)
        packed = coef[:24]
        for g in range(1, 6):
            packed = packed + pltpu.roll(coef[g * 24 : (g + 1) * 24], 16 * g, 1)
        row = jnp.concatenate([field, packed], axis=0)
        if x < 7:
            first_out[x] = row
        if x > 0:
            last_out[x - 1] = row


def place_slots(listed, amps, out):
    lane = iota((128, 256), 1)
    before = ((iota((128, 256), 0) < lane) | (lane >= 128)).astype(F32).astype(BF16)
    tile_line = iota((128, 128), 0)

    lefts, rights = [], []
    seen = jnp.zeros((128, 128), F32)
    for turn in range(8):
        at = slice(turn * 8, turn * 8 + 8)
        tiles = listed[at, :]
        cells = listed[64 + turn * 8 : 72 + turn * 8, :]
        code = cells * 64 + listed[128 + turn * 8 : 136 + turn * 8, :]
        parts = list(split2(amps[at, :]))
        parts.append((code >> 8).astype(F32).astype(BF16))
        parts.append((code & 255).astype(F32).astype(BF16))
        hits = [
            (tile_line == tiles[j : j + 1, :]).astype(F32) for j in range(8)
        ]
        hits_b = [h.astype(BF16) for h in hits]
        ranks = dot(jnp.concatenate(hits_b, axis=0), before, ((1,), (0,)))
        slots = []
        for j in range(8):
            rank = ranks[j * 128 : (j + 1) * 128]
            slot = jnp.sum(hits[j] * (rank[:, :128] + seen), axis=0, keepdims=True)
            slots.append((tile_line == slot.astype(jnp.int32)).astype(F32).astype(BF16))
            seen = seen + rank[:, 128:]
        hit = jnp.concatenate(hits_b, axis=1)
        slot = jnp.concatenate(slots, axis=1)
        left = []
        for part in parts:
            wide = part.astype(F32)
            wide = jnp.concatenate([wide[j : j + 1, :] for j in range(8)], axis=1)
            left.append(hit * wide.astype(BF16))
        lefts.append(jnp.concatenate(left, axis=0))
        rights.append(slot)

    acc = dot(jnp.concatenate(lefts, axis=1), jnp.concatenate(rights, axis=1), ((1,), (1,)))
    out[:, 0, :] = acc[0:128] + acc[128:256]
    out[:, 1, :] = acc[256:384] * 256.0 + acc[384:512]


def add_currents(slots, waves, out, low_out, high_out, acc):
    acc[...] = jnp.zeros_like(acc)
    table = jnp.concatenate([p.astype(F32) for p in split3(waves[...])], axis=1).astype(BF16)
    wave_line = iota((64, 16384), 0).astype(F32).astype(BF16)
    cell_line = iota((256, 16384), 0).astype(F32).astype(BF16)
    one, zero = jnp.ones((), BF16), jnp.zeros((), BF16)

    def chunk(turn, carry):
        rows = [slots[turn * 128 + j] for j in range(128)]
        amp = jnp.concatenate([r[0:1, :] for r in rows], axis=1)
        code = jnp.concatenate([r[1:2, :] for r in rows], axis=1).astype(jnp.int32)
        hit = jnp.where(wave_line == (code & 63).astype(F32).astype(BF16), one, zero)
        picked = dot(table, jnp.concatenate([hit, hit, hit], axis=0), ((1,), (0,)))
        current = (picked * amp).astype(BF16)
        cell = code >> 6
        block = (cell >> 8).astype(F32).astype(BF16)
        right = [jnp.where(block == jnp.array(r, BF16), current, zero) for r in range(4)]
        left = jnp.where(cell_line == (cell & 255).astype(F32).astype(BF16), one, zero)
        acc[...] += dot(left, jnp.concatenate(right, axis=0), ((1,), (1,)))
        return carry

    lax.fori_loop(0, 1, chunk, 0, unroll=1)
    low_lanes = iota((256, 128), 1) < 64
    for r in range(4):
        half = acc[:, (r // 2) * 128 : (r // 2 + 1) * 128]
        if r % 2:
            half = pltpu.roll(half, 64, 1)
        half = jnp.where(low_lanes, half, 0.0)
        for b in range(2):
            x = 2 * r + b
            rows = half[b * 128 : (b + 1) * 128]
            out[x] = rows
            low_out[x * 8 : x * 8 + 8, :] = rows[:8]
            high_out[x * 8 : x * 8 + 8, :] = rows[120:]


def pack_injected(own, low, high, first_out, last_out):
    rows = [widened(low, own, high, x) for x in range(8)]
    for j in range(3):
        first_out[j] = rows[j] + pltpu.roll(rows[j + 3], 64, 1)
        last_out[j] = rows[j + 2] + pltpu.roll(rows[j + 5], 64, 1)


def apply_row(src, i, diag, wx, wy, wv):
    v = src[i]
    wyi, wvi = wy[i], wv[i]
    out = diag[i] * v - wx[i] * src[i + 1] - wx[i - 1] * src[i - 1]
    out = out - wyi * pltpu.roll(v, YE - 1, 0) - pltpu.roll(wyi * v, 1, 0)
    return out - wvi * pltpu.roll(v, 96, 1) - pltpu.roll(wvi * v, 32, 1)


def power(src, dst, first, last, weights):
    def row(i, carry):
        dst[i] = apply_row(src, i, *weights)
        return carry

    lax.fori_loop(first, last + 1, row, 0, unroll=True)


def moments(fields, out, first):
    own = [f[first : first + 8, 8:136, :].reshape(1024, 128) for f in fields]
    lane, row = iota((32, 128), 1), iota((32, 128), 0)
    packed = jnp.zeros((32, 128), F32)
    parts = [split2(f) for f in own]
    for k in range(3):
        (hi, lo), (next_hi, next_lo) = parts[k], parts[k + 1]
        left = jnp.concatenate([hi, lo], axis=1)
        product = dot(left, jnp.concatenate([hi, next_hi], axis=1), ((0,), (0,)))
        cross = dot(hi, jnp.concatenate([lo, next_lo], axis=1), ((0,), (0,)))
        product = product[:128] + product[128:] + cross
        column = lane - 32 * k
        totals = []
        for b in range(2):
            total = jnp.zeros((32, 128), F32)
            for l in range(4):
                piece = product[l * 32 : (l + 1) * 32, b * 128 : (b + 1) * 128]
                turn = (32 * (k - l)) % 128
                total = total + (pltpu.roll(piece, turn, 1) if turn else piece)
            totals.append(total)
        even, odd = totals
        inside = (column >= 0) & (column < 32)
        packed = packed + jnp.where(inside, jnp.where(column > row, even, odd), 0.0)
        diagonal = jnp.sum(jnp.where(column == row, even, 0.0), axis=1, keepdims=True)
        packed = packed + jnp.where(lane == 96 + k, diagonal, 0.0)
    out[...] = packed


def coefficients(gram):
    lane, row = iota((32, 128), 1), iota((32, 128), 0)
    sums = [gram[n] for n in range(gram.shape[0])]
    while len(sums) > 1:
        sums = [a + b for a, b in zip(sums[::2], sums[1::2])]
    packed = sums[0]
    flipped = jnp.concatenate([packed, jnp.zeros((96, 128), F32)], axis=0).T
    bases = []
    for k in range(3):
        direct = pltpu.roll(packed, 128 - 32 * k, 1) if k else packed
        mirror = flipped[k * 32 : (k + 1) * 32, :]
        even = jnp.where(lane > row, direct, mirror)
        even = jnp.where(lane == row, packed[:, 96 + k : 97 + k], even)
        bases.append(jnp.where(lane < 32, even, 0.0))
        odd = jnp.where(lane > row, mirror, direct)
        bases.append(jnp.where(lane < 32, odd, 0.0))

    def moment(k, place):
        return pltpu.roll(bases[k], place, 1) if place else bases[k]

    tiles = []
    for i in range(3):
        block = moment(i, 96)
        for j in range(3):
            block = block + SCALE * moment(i + j + 1, 32 * j) + SHIFT * moment(i + j, 32 * j)
        tiles += [block[r * 8 : r * 8 + 8] for r in range(4)]
    sub = iota((8, 128), 0)
    for t in range(12):
        rows = tiles[t]
        cols = [jnp.broadcast_to(rows[:, t * 8 + j : t * 8 + j + 1], (8, 128)) for j in range(8)]
        for j in range(8):
            inverse = 1.0 / cols[j][j : j + 1, :]
            pivot = rows[j : j + 1, :] * inverse
            rows = jnp.where(sub == j, pivot, rows - cols[j] * pivot)
            for n in range(j + 1, 8):
                top = cols[n][j : j + 1, :] * inverse
                cols[n] = jnp.where(sub == j, top, cols[n] - cols[j] * top)
        for i in range(12):
            block = tiles[i]
            for j in range(8):
                if i != t:
                    block = block - tiles[i][:, t * 8 + j : t * 8 + j + 1] * rows[j : j + 1, :]
            tiles[i] = block
        tiles[t] = rows
    lane = iota((32, 128), 1)
    outs = []
    for i in range(3):
        y = jnp.concatenate(tiles[i * 4 : i * 4 + 4], axis=0)
        y = jnp.where(lane >= 96, y, 0.0)
        y = y + pltpu.roll(y, 32, 1) + pltpu.roll(y, 64, 1) + pltpu.roll(y, 96, 1)
        outs.append(
            jnp.concatenate([jnp.where(lane // 32 == l, y, 0.0) for l in range(4)], axis=0)
        )
    return outs


def combination(gram):
    y0, y1, y2 = coefficients(gram)
    step = jnp.concatenate([y0, y1, y2, jnp.zeros_like(y0)], axis=0)
    less = jnp.concatenate(
        [
            -SHIFT * y0,
            -SCALE * y0 - SHIFT * y1,
            -SCALE * y1 - SHIFT * y2,
            -SCALE * y2,
        ],
        axis=0,
    )
    return jnp.concatenate([step, less], axis=1)


def spreading():
    n, q = iota((128, 512), 1), iota((128, 512), 0)
    hit = (q % 16 == (n // 128) * 4 + (n % 128) // 32) & (q < 48)
    return hit.astype(F32).astype(BF16)


def expand(coef, spread, cap, wx, wy, wv, i):
    hi, mid, lo = [p.astype(F32) for p in split3(coef)]
    parts = hi + pltpu.roll(mid, 16, 1) + pltpu.roll(lo, 32, 1)
    wide = dot(parts.astype(BF16), spread, ((1,), (0,)))
    for n, out in enumerate((cap, wx, wy, wv)):
        out[i] = wide[:, n * 128 : (n + 1) * 128]


def weigh(i, ext, raw_x, diag, wx, wy, wv, cap, free):
    scale = 1.0 / SCALE
    own, raw_y, raw_v = cap[i], wy[i], wv[i]
    wyi = jnp.where(pltpu.roll(own, YE - 1, 0) > 0, raw_y * scale, 0.0)
    wvi = jnp.where(iota((YE, 128), 1) < 96, raw_v * scale, 0.0)
    wy[i], wv[i] = wyi, wvi
    total = (own + raw_x + raw_y + raw_v - SHIFT) * scale + wx[i - 1]
    diag[i] = total + pltpu.roll(wyi, 1, 0) + pltpu.roll(wvi, 32, 1)
    free[i] = (own - SHIFT) * ext[i] - SCALE * apply_row(ext, i, diag, wx, wy, wv)


def own_weights(v, c, low, high, diag, wx, wy, wv, cap, free, ext, scaled):
    spread = spreading()
    for x in range(8):
        ext[x] = widened(low, v, high, x)
        expand(widened(low, c, high, x, 64), spread, cap, wx, wy, wv, x)
        scaled[x] = wx[x] * (1.0 / SCALE)
    for x in (0, 7):
        diag[x] = jnp.zeros((YE, 128), F32)
        free[x] = jnp.zeros((YE, 128), F32)
    for x in range(1, 7):
        weigh(x, ext, wx[x], diag, scaled, wy, wv, cap, free)
        wx[x] = scaled[x]


def grid_weights(
    v, low, high, x_low, x_high, diag_in, wx_in, wy_in, wv_in, cap_in, free_in,
    diag, wx, wy, wv, cap, free, ext,
):
    lane = iota((YE, 128), 1)
    spread = spreading()
    for x in (0, 1, 6, 7):
        ext[7 + x] = widened(low, v, high, x)

    def own_row(x, carry):
        for src, dst in (
            (diag_in, diag), (wx_in, wx), (wy_in, wy), (wv_in, wv), (cap_in, cap), (free_in, free)
        ):
            dst[7 + x] = src[x]
        return carry

    def halo_row(j, ref, base, present):
        ext[base + j] = ref[j, :YE, :] * present
        packed = ref[j, YE:, :] * present
        groups = [packed] + [pltpu.roll(packed, 128 - 16 * g, 1) for g in range(1, 6)]
        coef = jnp.where(lane < 16, jnp.concatenate(groups, axis=0), 0.0)
        expand(coef, spread, cap, wx, wy, wv, base + j)

    def halo_rows(j, carry):
        low_in, high_in = inside(GX)
        halo_row(j, x_low, 0, low_in)
        halo_row(j, x_high, 15, high_in)
        return carry

    lax.fori_loop(0, 8, own_row, 0, unroll=True)
    lax.fori_loop(0, 7, halo_rows, 0, unroll=True)

    def edge_x(i):
        wx[i] = jnp.where(cap[i + 1] > 0, wx[i] * (1.0 / SCALE), 0.0)

    def row(i, carry):
        raw = wx[i]
        edge_x(i)
        weigh(i, ext, raw, diag, wx, wy, wv, cap, free)
        return carry

    edge_x(0)
    lax.fori_loop(1, 8, row, 0, unroll=True)
    lax.fori_loop(14, 21, row, 0, unroll=True)


def first_basis(
    diag, wx, wy, wv, free, inj, i_low, i_high, ix_low, ix_high,
    change, v0, v1, v2, v3, gram,
):
    lane = iota((YE, 128), 1)
    weights = (diag, wx, wy, wv)

    def start(i, both):
        now = jnp.where(lane < 32, both, 0.0)
        then = jnp.where(lane < 32, pltpu.roll(both, 96, 1), 0.0)
        change[i] = now - then
        v0[i] = free[i] - now

    def own_start(x, carry):
        start(7 + x, widened(i_low, inj, i_high, x))
        return carry

    def halo_start(j, carry):
        low_in, high_in = inside(GX)
        for ref, base, present in ((ix_low, 1, low_in), (ix_high, 15, high_in)):
            both = ref[j] * present
            start(base + j, both)
            start(base + 3 + j, pltpu.roll(both, 64, 1))
        return carry

    lax.fori_loop(0, 8, own_start, 0, unroll=True)
    lax.fori_loop(0, 3, halo_start, 0, unroll=True)
    power(v0, v1, 2, 19, weights)
    power(v1, v2, 3, 18, weights)
    power(v2, v3, 4, 17, weights)
    moments((v0, v1, v2, v3), gram, 7)


def split_rows(v0, v1, v2, v3, hi_out, lo_out):
    def row(i, carry):
        for n, field in enumerate((v0, v1, v2, v3)):
            at = slice(n * 128, (n + 1) * 128)
            hi_out[i, :, at], lo_out[i, :, at] = split2(field[4 + i])
        return carry

    lax.fori_loop(0, 14, row, 0, unroll=True)


def second_basis(
    gram, diag, wx, wy, wv, cap, change, v0, hi, lo, step, b0, b1, b2, b3, gram_out
):
    weights = (diag, wx, wy, wv)
    mix_hi, mix_lo = split2(combination(gram))
    across = ((1,), (0,))

    def row(i, carry):
        both = dot(hi[i - 4], mix_hi, across) + dot(hi[i - 4], mix_lo, across)
        both = both + dot(lo[i - 4], mix_hi, across)
        moved = both[:, :128]
        step[i] = moved
        b0[i] = v0[i] + both[:, 128:] + cap[i] * moved + change[i]
        return carry

    lax.fori_loop(4, 18, row, 0, unroll=True)
    power(b0, b1, 5, 16, weights)
    power(b1, b2, 6, 15, weights)
    power(b2, b3, 7, 14, weights)
    moments((b0, b1, b2, b3), gram_out, 7)


def store_rows(out, x, value):
    for l in range(4):
        out[pl.ds(l * 8 + x, 32, stride=32), :] = value[l * 32 : (l + 1) * 32]


def load_rows(ref, x):
    return jnp.concatenate([ref[pl.ds(l * 8 + x, 32, stride=32), :] for l in range(4)], axis=0)


def from_lanes(step, b0, b1, b2, b3, volts, volts_out, residual_out, hi_out, lo_out):
    for x in range(8):
        volts_out[x] = load_rows(volts, x) + step[7 + x, 8:136, :].T
        for n, field in enumerate((b0, b1, b2, b3)):
            rows = field[7 + x, 8:136, :].T
            if n == 0:
                residual_out[x] = rows
            at = slice(n * 128, (n + 1) * 128)
            hi_out[x, at, :], lo_out[x, at, :] = split2(rows)


def finish(gram, hi, lo, volts, residual, volts_out, residual_out):
    mix_hi, mix_lo = split2(combination(gram).T)
    for x in range(0, 8, 2):
        field_hi = jnp.concatenate([hi[x], hi[x + 1]], axis=1)
        field_lo = jnp.concatenate([lo[x], lo[x + 1]], axis=1)
        across = ((1,), (0,))
        both = dot(mix_hi, field_hi, across) + dot(mix_hi, field_lo, across)
        both = both + dot(mix_lo, field_hi, across)
        for n in range(2):
            own = both[:, n * 128 : (n + 1) * 128]
            store_rows(volts_out, x + n, volts[x + n] + own[:128])
            store_rows(residual_out, x + n, residual[x + n] + own[128:])


def neighbours(to_low, to_high, axis):
    size = lax.axis_size(axis)
    up = [(i, (i + 1) % size) for i in range(size)]
    from_low = lax.ppermute(to_high, axis, up)
    return from_low, lax.ppermute(to_low, axis, [(b, a) for a, b in up])


def sum_copies(a, b, c, d, out):
    total = (a[...] + b[...]) + (c[...] + d[...])
    for n in range(out.shape[0]):
        out[n] = total


def everywhere(x, beside=()):
    x = x + lax.ppermute(x, "gy_1", [(0, 1), (1, 0)])
    one, two, three = [
        lax.ppermute(x, "gy_0", [(i, i ^ k) for i in range(4)]) for k in (1, 2, 3)
    ]
    x, one, two, three, beside = lax.optimization_barrier((x, one, two, three, beside))
    (x,) = call(sum_copies, [(lax.axis_size(GX),) + x.shape], [x, one, two, three])
    return lax.all_to_all(x, GX, split_axis=0, concat_axis=0, tiled=True), beside


def exchange(slots):
    return lax.all_to_all(slots, GX_GY, split_axis=0, concat_axis=0, tiled=True)


def body(volts, cap, cond_x, cond_y, via, waveforms, placement, cells, wave_ids, amps):
    vmem = pltpu.VMEM
    coefs = jnp.concatenate([a.reshape(32, 128) for a in (cap, cond_x, cond_y, via)], axis=0)
    v, c, y_low, y_high = call(
        to_lanes,
        [(8, 128, 128), (8, 128, 128), (128, 128), (128, 128)],
        [volts.reshape(1024, 128), coefs],
    )
    y_low, y_high = neighbours(y_low, y_high, GY)
    listed = [a.reshape(64, 128) for a in (placement, cells, wave_ids)]
    (slots,) = call(
        place_slots,
        [(128, 2, 128)],
        [jnp.concatenate(listed, axis=0), amps.reshape(64, 128)],
    )
    y_low, y_high, slots = lax.optimization_barrier((y_low, y_high, slots))
    x_low, x_high = call(pack_rows, [(7, 168, 128)] * 2, [v, c, y_low, y_high])
    x_low, x_high = neighbours(x_low, x_high, GX)
    slots = exchange(slots)
    inj, i_low, i_high = call(
        add_currents,
        [(8, 128, 128), (64, 128), (64, 128)],
        [slots, waveforms],
        [vmem((256, 256), F32)],
    )
    i_low, i_high = neighbours(i_low, i_high, GY)
    tile = (8, YE, 128)
    v, c, y_low, y_high, inj = lax.optimization_barrier((v, c, y_low, y_high, inj))
    partial = call(
        own_weights, [tile] * 6, [v, c, y_low, y_high], [vmem(tile, F32), vmem(tile, F32)]
    )
    i_low, i_high, partial = lax.optimization_barrier((i_low, i_high, partial))
    ix_low, ix_high = call(pack_injected, [(3, YE, 128)] * 2, [inj, i_low, i_high])
    ix_low, ix_high = neighbours(ix_low, ix_high, GX)
    wide = (XE, YE, 128)
    diag, wx, wy, wv, cap, free = call(
        grid_weights,
        [wide] * 6,
        [v, y_low, y_high, x_low, x_high, *partial],
        [vmem(wide, F32)],
    )
    *kept, gram = call(
        first_basis,
        [wide] * 5 + [(32, 128)],
        [diag, wx, wy, wv, free, inj, i_low, i_high, ix_low, ix_high],
    )
    change, *fields = kept
    halves = [jax.ShapeDtypeStruct((14, YE, 512), BF16)] * 2
    gram, (hi, lo) = everywhere(gram, call(split_rows, halves, fields))
    step, *basis, gram = call(
        second_basis,
        [wide] * 5 + [(32, 128)],
        [gram, diag, wx, wy, wv, cap, change, fields[0], hi, lo],
    )
    halves = [jax.ShapeDtypeStruct((8, 512, 128), BF16)] * 2
    so_far = call(
        from_lanes,
        [(8, 128, 128)] * 2 + halves,
        [step] + basis + [volts.reshape(1024, 128)],
    )
    gram, so_far = everywhere(gram, so_far)
    volts_so_far, residual, hi, lo = so_far
    outs = call(finish, [(1024, 128)] * 2, [gram, hi, lo, volts_so_far, residual])
    return tuple(o.reshape(volts.shape) for o in outs)


def solution(mesh):
    finer = Mesh(mesh.devices.reshape(4, 4, 4, 2), ("gx_0", "gx_1", "gy_0", "gy_1"))
    in_specs = (
        P(None, None, GX, GY),
        P(None, GX, GY),
        P(None, GX, GY),
        P(None, GX, GY),
        P(None, GX, GY),
        P(),
        P(GX_GY, None),
        P(GX_GY),
        P(GX_GY),
        P(GX_GY),
    )
    out_specs = (P(None, None, GX, GY), P(None, None, GX, GY))
    return jax.shard_map(body, mesh=finer, in_specs=in_specs, out_specs=out_specs, check_vma=False)
```
